32 devices in a mesh: rep: 4 (over x, core), fsdp: 8 (over z, y).
Axes of the slice: x: 2, y: 2, z: 4, core: 2. Of those that a mesh axis runs over, the one named last changes fastest.
Arguments:
- layer_input: bfloat16 [24576, 1024], P(('rep', 'fsdp')), may hold values from -6 to 6
- item_ids: int32 [24576], P(('rep', 'fsdp')), may hold values from 0 to 48, as said below
- norm_gain: bfloat16 [1024], P('fsdp'), may hold values from 0.25 to 1.75
- norm_bias: bfloat16 [1024], P('fsdp'), may hold values from -1.5 to 1.5
- joint_weight: bfloat16 [1024, 3072], P('fsdp'), may hold values from -0.1875 to 0.1875
- joint_bias: bfloat16 [2048], P('fsdp'), may hold values from -1.5 to 1.5
- out_weight: bfloat16 [1024, 1024], P('fsdp'), may hold values from -0.5 to 0.5
- out_bias: bfloat16 [1024], P('fsdp'), may hold values from -1.5 to 1.5
- second_gain: bfloat16 [1024], P('fsdp'), may hold values from 0.25 to 1.75
- second_bias: bfloat16 [1024], P('fsdp'), may hold values from -1.5 to 1.5
- up_weight: bfloat16 [1024, 2048], P('fsdp'), may hold values from -0.1875 to 0.1875
- up_bias: bfloat16 [2048], P('fsdp'), may hold values from -1.5 to 1.5
- down_weight: bfloat16 [2048, 1024], P('fsdp'), may hold values from -0.125 to 0.125
- down_bias: bfloat16 [1024], P('fsdp'), may hold values from -1.5 to 1.5
- output_grad: bfloat16 [24576, 1024], P(('rep', 'fsdp')), may hold values from -6 to 6
Outputs:
- layer_output: bfloat16 [24576, 1024], P(('rep', 'fsdp'))
- input_grad: bfloat16 [24576, 1024], P(('rep', 'fsdp'))
- norm_gain_grad: float32 [1024], P('fsdp')
- norm_bias_grad: float32 [1024], P('fsdp')
- joint_weight_grad: float32 [1024, 3072], P('fsdp')
- joint_bias_grad: float32 [2048], P('fsdp')
- out_weight_grad: float32 [1024, 1024], P('fsdp')
- out_bias_grad: float32 [1024], P('fsdp')
- second_gain_grad: float32 [1024], P('fsdp')
- second_bias_grad: float32 [1024], P('fsdp')
- up_weight_grad: float32 [1024, 2048], P('fsdp')
- up_bias_grad: float32 [2048], P('fsdp')
- down_weight_grad: float32 [2048, 1024], P('fsdp')
- down_bias_grad: float32 [1024], P('fsdp')
The draws below stay inside these ranges and needn't reach their ends.
Inputs may be any that keep to these rules, and one draw needn't show every extreme that they name: `item_ids`: every aligned block of 768 rows holds whole items, numbered 0, 1, 2, ... in order of position inside the block; items have 15 or 60 tokens, save at most one item of fewer than 15 tokens in a block, and each block holds at least one item of 60 tokens.
All inputs are finite; a program needn't handle non-finite values.
Results may differ from the reference program's by a relative error of at most 0.018.
Values may be sent and summed in bfloat16 or wider, within the bound.
No kernel may reach another device: no remote copies, remote signals or barrier semaphores. Data moves between devices by JAX's collectives and lax.ppermute only.
A program may use at most 192 MiB of HBM per device.

```python
import jax
import jax.numpy as jnp
from jax import lax

D = 1024
H = 8
HD = 128
FF = 2048
QBLK = 768
TOKENS = 24576


def draw_item_ids(key, part):
    block_count = TOKENS // QBLK
    slot_count = QBLK // 15 + 2
    most_long = max(1, QBLK // 256)
    key_long = jax.random.fold_in(key, 11)
    key_order = jax.random.fold_in(key, 23)
    key_pick = jax.random.fold_in(key, 37)
    long_count = jax.random.randint(key_long, (block_count, 1), 1, most_long + 1)
    chosen_block = jax.random.randint(key_pick, (), 0, block_count)
    block_index = jnp.arange(block_count, dtype=jnp.int32)[:, None]
    long_count = jnp.where(block_index == chosen_block, 1, long_count)
    leftover = QBLK - 60 * long_count
    short_count = leftover // 15
    remainder = leftover - 15 * short_count
    slot_index = jnp.arange(slot_count, dtype=jnp.int32)[None, :]
    item_sizes = jnp.where(slot_index < long_count, 60, jnp.where(slot_index < long_count + short_count, 15, jnp.where(slot_index == long_count + short_count, remainder, 0)))
    random_keys = jax.random.randint(key_order, (block_count, slot_count), 0, 1 << 20) * slot_count + slot_index
    random_keys = jnp.where(item_sizes > 0, random_keys, (1 << 30) + slot_index)
    ranking = jnp.argsort(random_keys, axis=1)
    ordered = jnp.take_along_axis(item_sizes, ranking, axis=1)
    item_ends = jnp.cumsum(ordered, axis=1)
    position = jnp.arange(QBLK, dtype=jnp.int32)
    item_index = jnp.sum((item_ends[:, None, :] <= position[None, :, None]).astype(jnp.int32), axis=2)
    return item_index.reshape(TOKENS).astype(jnp.int32)


def strengthened(drawn, stream_key, source, target, blocks, factor):
    owner, partner = [(jnp.arange(drawn.shape[axis_at]) // (drawn.shape[axis_at] // blocks)).reshape([-1 if axis == axis_at else 1 for axis in range(drawn.ndim)]) for axis_at in (source, target)]
    chosen = jax.random.permutation(stream_key, blocks)[partner]
    strong = (owner == chosen) | (owner == (partner + blocks // 2) % blocks)
    return jnp.where(strong, factor * drawn, drawn)


def block_scale(key, shape, cuts, smallest, largest):
    loudness = 1.0
    for axis_at, parts in cuts:
        steps = jax.random.uniform(jax.random.fold_in(jax.random.fold_in(key, 6), axis_at), (parts,), jnp.float32, smallest / len(cuts), largest / len(cuts))
        loudness = loudness * jnp.repeat(jnp.exp(steps), shape[axis_at] // parts).reshape((-1,) + (1,) * (len(shape) - 1 - axis_at))
    return loudness


def normal_values(rng, dims, scale, most, cuts=(), held_as=jnp.bfloat16):
    array = jax.random.normal(rng, dims, jnp.float32) * scale
    if len(cuts) > 0:
        array = block_scale(rng, dims, cuts, -0.22, 0.18) * array
    return jnp.clip(array, min=-most, max=most).astype(held_as)


def heavy_noise(own_key, extent, scale, most, cuts, heavy, kind=jnp.bfloat16):
    values = scale * jax.random.normal(own_key, extent, jnp.float32)
    if cuts:
        values = values * block_scale(own_key, extent, cuts, -0.22, 0.18)
    return jnp.clip(strengthened(values, jax.random.fold_in(own_key, 3), *heavy), -most, most).astype(kind)


def setup_inputs(seed: int = 0) -> dict:
    seeds = jax.random.split(jax.random.key(seed), 16)
    layer_input = normal_values(seeds[0], (TOKENS, D), 1.0, 6.0, ((0, 32),))
    item_ids = draw_item_ids(jax.random.fold_in(seeds[15], 71), 0)
    norm_gain = jnp.clip(1.0 + 0.15 * jax.random.normal(seeds[2], (D,), jnp.float32), 0.25, 1.75).astype(jnp.bfloat16)
    norm_bias = normal_values(seeds[3], (D,), 0.3, 1.5, ((0, 8),))
    joint_weight = normal_values(seeds[4], (D, 3 * D), D ** -0.5, 0.1875, ((0, 8),))
    joint_bias = normal_values(seeds[5], (2 * D,), 0.3, 1.5, ((0, 8),))
    out_weight = normal_values(seeds[6], (D, D), (D // 8) ** -0.5, 0.5, ((0, 8),))
    out_bias = normal_values(seeds[7], (D,), 0.3, 1.5, ((0, 8),))
    second_gain = jnp.clip(1.0 + 0.15 * jax.random.normal(seeds[8], (D,), jnp.float32), 0.25, 1.75).astype(jnp.bfloat16)
    second_bias = normal_values(seeds[9], (D,), 0.3, 1.5, ((0, 8),))
    up_weight = normal_values(seeds[10], (D, FF), D ** -0.5, 0.1875, ((0, 8),))
    up_bias = normal_values(seeds[11], (FF,), 0.3, 1.5, ((0, 8),))
    down_weight = normal_values(seeds[12], (FF, D), FF ** -0.5, 0.125, ((0, 8),))
    down_bias = normal_values(seeds[13], (D,), 0.3, 1.5, ((0, 8),))
    output_grad = heavy_noise(seeds[14], (TOKENS, D), 1.0, 6.0, ((0, 32),), (0, 1, 32, 2.75))
    return dict(layer_input=layer_input, item_ids=item_ids, norm_gain=norm_gain, norm_bias=norm_bias, joint_weight=joint_weight, joint_bias=joint_bias, out_weight=out_weight, out_bias=out_bias, second_gain=second_gain, second_bias=second_bias, up_weight=up_weight, up_bias=up_bias, down_weight=down_weight, down_bias=down_bias, output_grad=output_grad)


@jax.custom_vjp
def low(v):
    return lax.optimization_barrier(v.astype(jnp.bfloat16)).astype(jnp.float32)

@jax.custom_vjp
def low_back(v):
    return v

def low_keep(v):
    return (low(v), None)

def low_pass(kept, grad):
    return (grad,)

def back_keep(v):
    return (v, None)

def back_low(kept, grad):
    return (low(grad),)
low.defvjp(low_keep, low_pass)
low_back.defvjp(back_keep, back_low)
eps = 1e-05
highest = lax.Precision.HIGHEST

def norm_affine(values, gain, bias):
    center = values - lax.optimization_barrier(jnp.mean(values, axis=-1, keepdims=True))
    spread = lax.optimization_barrier(jnp.mean(center * center, axis=-1, keepdims=True))
    return center * lax.rsqrt(spread + eps) * gain + bias

def attend_block(pieces):
    queries, key_rows, value_rows, labels = pieces
    length = queries.shape[0]
    queries = queries.reshape(length, H, HD)
    key_rows = key_rows.reshape(length, H, HD)
    value_rows = value_rows.reshape(length, H, HD)
    scores = jnp.einsum('qhd,khd->hqk', queries, key_rows, precision=highest) * HD ** (-0.5)
    scores = low_back(scores)
    position = jnp.arange(length)
    allowed = (labels[:, None] == labels[None, :]) & (position[:, None] >= position[None, :])
    scores = jnp.where(allowed[None], scores, -1e+30)
    weights = jax.nn.softmax(scores, axis=-1)
    mixed = jnp.einsum('hqk,khd->qhd', low(weights), value_rows, precision=highest)
    return mixed.reshape(length, H * HD)

def decoder_layer(inputs, labels, params):
    gain_one, bias_one, joint_matrix, joint_shift, out_matrix, out_shift, gain_two, bias_two, up_matrix, up_shift, down_matrix, down_shift = params
    row_count = inputs.shape[0]
    first = low(norm_affine(inputs, gain_one, bias_one))
    projected = jnp.dot(first, joint_matrix, precision=highest)
    offset = jnp.concatenate([joint_shift[:D], jnp.zeros((D,), inputs.dtype), joint_shift[D:]])
    projected = low(low_back(projected + offset))
    blocks = row_count // QBLK
    queries = projected[:, :D].reshape(blocks, QBLK, D)
    key_rows = projected[:, D:2 * D].reshape(blocks, QBLK, D)
    value_rows = projected[:, 2 * D:].reshape(blocks, QBLK, D)
    attended = lax.map(jax.checkpoint(attend_block), (queries, key_rows, value_rows, labels.reshape(blocks, QBLK)))
    attended = low(low_back(attended.reshape(row_count, D)))
    branch = low_back(jnp.dot(attended, out_matrix, precision=highest) + out_shift)
    middle = inputs + branch
    second = low(norm_affine(middle, gain_two, bias_two))
    hidden = low_back(jnp.dot(second, up_matrix, precision=highest) + up_shift)
    active = low(jax.nn.gelu(hidden))
    feed_out = low_back(jnp.dot(active, down_matrix, precision=highest) + down_shift)
    return middle + feed_out

def reference(layer_input, item_ids, norm_gain, norm_bias, joint_weight, joint_bias, out_weight, out_bias, second_gain, second_bias, up_weight, up_bias, down_weight, down_bias, output_grad):
    params = tuple((tensor.astype(jnp.float32) for tensor in (norm_gain, norm_bias, joint_weight, joint_bias, out_weight, out_bias, second_gain, second_bias, up_weight, up_bias, down_weight, down_bias)))
    block_count = TOKENS // QBLK
    per_group = 4 if block_count % 4 == 0 else 1
    groups = block_count // per_group
    group_rows = per_group * QBLK
    inputs = layer_input.reshape(groups, group_rows, D)
    labels = item_ids.reshape(groups, group_rows)
    cotangent = output_grad.reshape(groups, group_rows, D)

    def advance(totals, element):
        rows_in, rows_ids, rows_grad = element

        def runner(values, weights):
            return decoder_layer(values, rows_ids, weights)
        result, puller = jax.vjp(runner, rows_in.astype(jnp.float32), params)
        grad_rows, grad_params = puller(rows_grad.astype(jnp.float32))
        totals = tuple((running + addend for running, addend in zip(totals, grad_params)))
        return (totals, (result.astype(jnp.bfloat16), grad_rows.astype(jnp.bfloat16)))
    initial = tuple((jnp.zeros(weight.shape, jnp.float32) for weight in params))
    totals, (outputs, grads) = lax.scan(advance, initial, (inputs, labels, cotangent))
    return (outputs.reshape(TOKENS, D), grads.reshape(TOKENS, D), totals[0], totals[1], totals[2], totals[3], totals[4], totals[5], totals[6], totals[7], totals[8], totals[9], totals[10], totals[11])
```

```python
import functools
import math

import jax
import jax.numpy as jnp
from jax import lax
from jax.experimental import pallas as pl
from jax.experimental.pallas import tpu as pltpu
from jax.sharding import PartitionSpec as P

H = 8
HD = 128
EPS = 1e-05
MASKED = -1e30
BF = jnp.bfloat16
F32 = jnp.float32
VM = pltpu.VMEM
TQ = 128
BAND = 128


def nbytes(a):
    return math.prod(a.shape) * jnp.dtype(a.dtype).itemsize


def kernel_call(body, outs, args, anys=(), smem=(), scratch=(), extra=6, flops=0, name=None):
    room = sum(nbytes(a) for i, a in enumerate(args) if i not in anys and i not in smem)
    room += sum(nbytes(o) for o in outs) + sum(nbytes(s) for s in scratch if hasattr(s, "shape") and s.dtype in (BF, F32))
    moved = sum(nbytes(a) for a in args) + sum(nbytes(o) for o in outs)
    specs = [
        pl.BlockSpec(memory_space=pl.ANY) if i in anys
        else pl.BlockSpec(memory_space=pltpu.SMEM) if i in smem
        else pl.BlockSpec(memory_space=VM)
        for i in range(len(args))
    ]
    return pl.pallas_call(
        body,
        out_shape=[jax.ShapeDtypeStruct(o.shape, o.dtype) for o in outs],
        in_specs=specs,
        out_specs=[pl.BlockSpec(memory_space=VM) for _ in outs],
        scratch_shapes=list(scratch),
        compiler_params=pltpu.CompilerParams(
            vmem_limit_bytes=min(60 * 2**20, int(room + extra * 2**20))
        ),
        cost_estimate=pl.CostEstimate(flops=flops, bytes_accessed=moved, transcendentals=0),
        name=name,
    )(*args)


def out(shape, dtype):
    return jax.ShapeDtypeStruct(shape, dtype)


def dot(a, b):
    return jnp.dot(a, b, preferred_element_type=F32)


def dot_tn(a, b):
    return lax.dot_general(a, b, (((0,), (0,)), ((), ())), preferred_element_type=F32)


def dot_nt(a, b):
    return lax.dot_general(a, b, (((1,), (1,)), ((), ())), preferred_element_type=F32)


def loop(count, step):
    lax.fori_loop(0, count, lambda i, z: (step(i), z)[1], 0)


def normalized(values):
    center = values - jnp.mean(values, axis=-1, keepdims=True)
    spread = jnp.mean(center * center, axis=-1, keepdims=True)
    factor = lax.rsqrt(spread + EPS)
    return center * factor, factor


GAIN1, BIAS1, JB_Q, JB_V, OUT_B, GAIN2, BIAS2, UP_B, DOWN_B = 0, 1, 2, 3, 4, 5, 6, 7, 9


class Ring:
    def __init__(self, mesh):
        self.axes = ("rep", "fsdp")
        self.n = mesh.shape["fsdp"]
        self.reps = mesh.shape["rep"]
        n = self.n
        self.order = list(range(0, n, 2)) + list(range(n - 1, 0, -2))
        self.place = [self.order.index(f) for f in range(n)]
        self.half = n // 2

    def perm(self, target, keep=lambda r, f: True):
        n = self.n
        pairs = []
        for r in range(self.reps):
            for f in range(n):
                if keep(r, f):
                    r2, f2 = target(r, f)
                    pairs.append((r * n + f, r2 * n + f2))
        return pairs

    def send(self, v, target, keep=lambda r, f: True):
        return lax.ppermute(v, self.axes, self.perm(target, keep))

    def along(self, v):
        def target(r, f):
            step = 1 if r % 2 == 0 else -1
            return r, self.order[(self.place[f] + step) % self.n]

        return self.send(v, target)

    def core(self, v, keep=lambda r, f: True):
        return self.send(v, lambda r, f: (r ^ 1, f), keep)

    def across(self, v, keep=lambda r, f: True):
        return self.send(v, lambda r, f: (r ^ 2, f), keep)

    def tables(self):
        n = self.n
        rows, slots = [], []
        for c in range(2):
            for f in range(n):
                d = 1 if c == 0 else -1
                rows.append([self.order[(self.place[f] - d * h) % n] for h in range(n)])
                slots.append([((self.place[j] - self.place[f]) * d) % n for j in range(n)])
        return rows, slots


def gather(ring, ext, mid, xbit, cbit):
    a, b = ext.shape[0], mid.shape[0]
    m = ring.half
    cur = jnp.concatenate([ext, mid])
    rings, outs = [], []
    for h in range(1, m + 1):
        if h == m:
            cur = lax.dynamic_slice_in_dim(cur, cbit * a, b, 0)
        cur = ring.along(cur)
        rings.append(cur)
        if h < m:
            outs.append(ring.across(cur[:a]))
        else:
            outs.append(ring.across(cur[:a], lambda r, f: r % 2 == 0))
    prings = [ring.core(v) for v in rings]
    pouts = [ring.core(v) for v in outs]
    first = cbit == 0
    last_ext = jnp.where(first, rings[-1][:a], prings[-1][:a])
    last_mid = jnp.where(first, prings[-1], rings[-1])
    last_opp = jnp.where(first, outs[-1], pouts[-1])
    return rings[:-1] + prings[:-1], outs[:-1] + pouts[:-1], (last_ext, last_mid, last_opp)


def placements(ring, a, b):
    n, m = ring.n, ring.half
    plan = [(0, ("own", 0), ("own", 1), ("own", 2))]
    for h in range(1, m):
        plan.append((h, h - 1, None, None))
        plan.append((n - h, m - 1 + h - 1, None, None))
    plan.append((m, ("last", 0), ("last", 1), ("last", 2)))
    return plan


def copies(ring, own, rings, outs, last, a, b, dest, sems, start):
    n, m = ring.n, ring.half
    sources = [(0, own[0], 0, own[1], 0, own[2])]
    for h in range(1, m):
        sources.append((h, rings[h - 1], 0, rings[h - 1], a, outs[h - 1]))
        sources.append((n - h, rings[m - 1 + h - 1], 0, rings[m - 1 + h - 1], a, outs[m - 1 + h - 1]))
    sources.append((m, last[0], 0, last[1], 0, last[2]))
    made = {"mid": [], "ext": [], "opp": []}
    k = 0
    for part in ("mid", "ext", "opp"):
        for step, e, e0, md, m0, op in sources:
            src, base = {"mid": (md, m0), "ext": (e, e0), "opp": (op, 0)}[part]
            for row, rows, target in dest(part, step):
                c = pltpu.make_async_copy(src.at[pl.ds(base + row, rows), :], target, sems.at[k])
                k += 1
                if start:
                    c.start()
                made[part].append(c)
    return made


def piece_count(ring, parts):
    return ring.n * parts


def ln_rows(x_ref, gain, bias, o_ref, rows=64):
    def step(i):
        at = pl.ds(pl.multiple_of(i * rows, rows), rows)
        n, _ = normalized(x_ref[at, :].astype(F32))
        o_ref[at, :] = (n * gain + bias).astype(BF)

    loop(x_ref.shape[0] // rows, step)


def qkv_kernel(ring, a, b, t, nr, meta, x_ref, small, *refs):
    own, refs = refs[:3], refs[3:]
    rings, refs = refs[:nr], refs[nr:]
    outs, refs = refs[:nr], refs[nr:]
    last, refs = refs[:3], refs[3:]
    first, proj, wj, wo, sems = refs
    n = ring.n
    width = x_ref.shape[1]
    rps = width // n
    xb = meta[0, n]

    def dest(part, step):
        row = pl.multiple_of(meta[0, step] * rps, rps)
        if part == "mid":
            yield 0, rps, wj.at[pl.ds(row, rps), pl.ds(width, width)]
            yield rps, rps - 2 * t, wo.at[pl.ds(row + t, rps - 2 * t), :]
        else:
            side = xb if part == "ext" else 1 - xb
            col = pl.multiple_of(side * 2 * width, width)
            yield 0, rps, wj.at[pl.ds(row, rps), pl.ds(col, width)]
            if t:
                yield rps, t, wo.at[pl.ds(pl.multiple_of(row + side * (rps - t), 16), t), :]

    made = copies(ring, own, rings, outs, last, a, b, dest, sems, True)
    ln_rows(x_ref, small[pl.ds(GAIN1, 1), :], small[pl.ds(BIAS1, 1), :], first)
    tn = 512

    def tile(j):
        at = pl.ds(pl.multiple_of(j * tn, tn), tn)
        return at, dot(first[...], wj[:, at])

    for c in made["mid"]:
        c.wait()

    def keys(i):
        at, v = tile(width // tn + i)
        proj[:, at] = v.astype(BF)

    loop(width // tn, keys)
    for part in ("ext", "opp"):
        for c in made[part]:
            c.wait()

    def qv(i):
        col = pl.multiple_of((i % (width // tn)) * tn, tn)
        side = i // (width // tn)
        at, v = tile(i + side * (width // tn))
        shift = small[pl.ds(JB_Q + side, 1), pl.ds(col, tn)]
        proj[:, at] = (v + shift).astype(BF)

    loop(2 * width // tn, qv)


def masks(col_ids, row_ids, i, lo):
    q0 = pl.multiple_of(i * TQ, TQ)
    at_q = pl.ds(q0, TQ)
    at_k = pl.ds(pl.multiple_of(q0 - lo, BAND), TQ + lo)
    span = TQ + lo
    same = col_ids[at_q, :] == row_ids[:, at_k]
    qpos = lax.broadcasted_iota(jnp.int32, (TQ, span), 0) + lo
    kpos = lax.broadcasted_iota(jnp.int32, (TQ, span), 1)
    return at_q, at_k, jnp.where(same & (kpos <= qpos), 0.0, MASKED).astype(F32)


LOG2E = 1.4426950408889634


def soft(q, k, bias):
    s = dot_nt(q, k) * (HD ** (-0.5) * LOG2E) + bias
    p = jnp.exp2(s - jnp.max(s, axis=1, keepdims=True))
    return p * (1.0 / jnp.sum(p, axis=1, keepdims=True))


def attend_kernel(proj, col_ids, row_ids, o_ref):
    rows, width = o_ref.shape

    def block(i, lo):
        at_q, at_k, bias = masks(col_ids, row_ids, i, lo)
        for h in range(H):
            q = proj[at_q, h * HD : (h + 1) * HD]
            k = proj[at_k, width + h * HD : width + (h + 1) * HD]
            v = proj[at_k, 2 * width + h * HD : 2 * width + (h + 1) * HD]
            w = soft(q, k, bias).astype(BF)
            o_ref[at_q, h * HD : (h + 1) * HD] = dot(w, v).astype(BF)

    block(0, 0)
    loop(rows // TQ - 1, lambda i: block(i + 1, BAND))


def out_kernel(att, wo, x_ref, small, middle, second):
    rows = 256
    g, bias = small[pl.ds(GAIN2, 1), :], small[pl.ds(BIAS2, 1), :]
    ob = small[pl.ds(OUT_B, 1), :]

    def step(i):
        at = pl.ds(pl.multiple_of(i * rows, rows), rows)
        mid = x_ref[at, :].astype(F32) + dot(att[at, :], wo[...]) + ob
        middle[at, :] = mid
        n, _ = normalized(mid)
        second[at, :] = (n * g + bias).astype(BF)

    loop(att.shape[0] // rows, step)


C0 = math.sqrt(2.0 / math.pi)


def gelu_both(h):
    h2 = h * h
    u = jnp.tanh(C0 * h * (1.0 + 0.044715 * h2))
    half = 0.5 * (1.0 + u)
    slope = half + (0.5 * C0) * h * (1.0 - u * u) * (1.0 + (3 * 0.044715) * h2)
    return h * half, slope


def up_kernel(ring, a, b, t, nr, meta, second, small, *refs):
    own, refs = refs[:3], refs[3:]
    rings, refs = refs[:nr], refs[nr:]
    outs, refs = refs[:nr], refs[nr:]
    last, refs = refs[:3], refs[3:]
    active, slope, wu, wd, sems = refs
    n = ring.n
    width = second.shape[1]
    rps = width // n
    xb = meta[0, n]

    def dest(part, step):
        row = pl.multiple_of(meta[0, step] * rps, rps)
        drow = pl.multiple_of(meta[0, step] * (2 * rps), 2 * rps)
        if part == "mid":
            yield 0, 2 * rps - 2 * t, wd.at[pl.ds(drow + t, 2 * rps - 2 * t), :]
        else:
            side = xb if part == "ext" else 1 - xb
            yield 0, rps, wu.at[pl.ds(row, rps), pl.ds(pl.multiple_of(side * width, width), width)]
            if t:
                yield rps, t, wd.at[pl.ds(pl.multiple_of(drow + side * (2 * rps - t), 16), t), :]

    made = copies(ring, own, rings, outs, last, a, b, dest, sems, True)
    for part in ("ext", "opp"):
        for c in made[part]:
            c.wait()
    tn = 256
    per = width // tn

    def step(i):
        at = pl.ds(pl.multiple_of(i * tn, tn), tn)
        shift = small[pl.ds(UP_B + i // per, 1), pl.ds(pl.multiple_of((i % per) * tn, tn), tn)]
        act, s = gelu_both(dot(second[...], wu[:, at]) + shift)
        active[:, at] = act.astype(BF)
        slope[:, at] = s.astype(BF)

    loop(2 * per, step)
    for c in made["mid"]:
        c.wait()


def dact_kernel(og, wd, slope, o_ref):
    tn = 256

    def step(i):
        at = pl.ds(pl.multiple_of(i * tn, tn), tn)
        v = dot_nt(og[...], wd[at, :])
        o_ref[:, at] = (v * slope[:, at].astype(F32)).astype(BF)

    loop(o_ref.shape[1] // tn, step)


def down_kernel(active, wd, middle, small, o_ref):
    tn = 512

    def step(i):
        at = pl.ds(pl.multiple_of(i * tn, tn), tn)
        v = dot(active[...], wd[:, at]) + small[pl.ds(DOWN_B, 1), at]
        o_ref[:, at] = (middle[:, at] + v).astype(BF)

    loop(o_ref.shape[1] // tn, step)


def weight_grad_kernel(n, tn, tl, offs, left, right, buf, sums):
    cols = right.shape[1]
    half = left.shape[1] // n // 2
    ones = jnp.ones((8, right.shape[0]), BF)
    per = tl // (2 * half)

    def step(i):
        at = pl.ds(pl.multiple_of(i * tn, tn), tn)
        r = right[:, at]
        sums[:, at] = dot(ones, r)
        for l in range(left.shape[1] // tl):
            v = dot_tn(left[:, l * tl : (l + 1) * tl], r).astype(BF)
            for s in range(2 * per):
                k = l * 2 * per + s
                row = pl.multiple_of(offs[0, k], half)
                buf[pl.ds(row, half), at] = v[s * half : (s + 1) * half, :]

    loop(cols // tn, step)


def norm_back(values, d, gain):
    n, r = normalized(values)
    g = d * gain
    t = r * (g - jnp.mean(g, axis=-1, keepdims=True) - n * jnp.mean(g * n, axis=-1, keepdims=True))
    return t, d * n


def group_sum(v):
    return jnp.sum(v.reshape(v.shape[0] // 8, 8, v.shape[1]), axis=0)


def dsecond_kernel(dh, wu, wo, middle, og, small, dmid, dbranch, datt, sg, sb):
    rows = 256
    g = small[pl.ds(GAIN2, 1), :]
    sg[...] = jnp.zeros_like(sg)
    sb[...] = jnp.zeros_like(sb)

    def step(i):
        at = pl.ds(pl.multiple_of(i * rows, rows), rows)
        dmid[at, :] = dot_nt(dh[at, :], wu[...])

    loop(dh.shape[0] // rows, step)
    rows2 = 64

    def norm(i):
        at = pl.ds(pl.multiple_of(i * rows2, rows2), rows2)
        d = dmid[at, :]
        t, dn = norm_back(middle[at, :], d, g)
        sg[...] += group_sum(dn)
        sb[...] += group_sum(d)
        v = og[at, :].astype(F32) + t
        dmid[at, :] = v
        dbranch[at, :] = v.astype(BF)

    loop(dh.shape[0] // rows2, norm)

    def back(i):
        at = pl.ds(pl.multiple_of(i * rows, rows), rows)
        datt[at, :] = dot_nt(dbranch[at, :], wo[...]).astype(BF)

    loop(dh.shape[0] // rows, back)


def attend_back_kernel(proj, datt, col_ids, row_ids, o_ref, acc_k, acc_v):
    rows, width = datt.shape
    scale = HD ** (-0.5)
    acc_k[...] = jnp.zeros_like(acc_k)
    acc_v[...] = jnp.zeros_like(acc_v)

    def block(i, lo):
        at_q, at_k, bias = masks(col_ids, row_ids, i, lo)
        for h in range(H):
            hs = slice(h * HD, (h + 1) * HD)
            q = proj[at_q, h * HD : (h + 1) * HD]
            k = proj[at_k, width + h * HD : width + (h + 1) * HD]
            v = proj[at_k, 2 * width + h * HD : 2 * width + (h + 1) * HD]
            do = datt[at_q, hs]
            p = soft(q, k, bias)
            dw = dot_nt(do, v)
            acc_v[at_k, hs] += dot_tn(p.astype(BF), do)
            inner = jnp.sum(p * dw, axis=1, keepdims=True)
            ds = (p * (dw - inner)).astype(BF)
            o_ref[at_q, hs] = (dot(ds, k) * scale).astype(BF)
            acc_k[at_k, hs] += dot_tn(ds, q) * scale

    block(0, 0)
    loop(rows // TQ - 1, lambda i: block(i + 1, BAND))
    o_ref[:, width : 2 * width] = acc_k[...].astype(BF)
    o_ref[:, 2 * width :] = acc_v[...].astype(BF)


def dfirst_kernel(dproj, wj, x_ref, dmid, small, o_ref, sg, sb, acc):
    rows = 256
    g = small[pl.ds(GAIN1, 1), :]
    sg[...] = jnp.zeros_like(sg)
    sb[...] = jnp.zeros_like(sb)

    def step(i):
        at = pl.ds(pl.multiple_of(i * rows, rows), rows)
        acc[at, :] = dot_nt(dproj[at, :], wj[...])

    loop(dproj.shape[0] // rows, step)
    rows2 = 64

    def norm(i):
        at = pl.ds(pl.multiple_of(i * rows2, rows2), rows2)
        d = acc[at, :]
        t, dn = norm_back(x_ref[at, :].astype(F32), d, g)
        sg[...] += group_sum(dn)
        sb[...] += group_sum(d)
        o_ref[at, :] = (dmid[at, :] + t).astype(BF)

    loop(dproj.shape[0] // rows2, norm)


def chunked(rows, per, step):
    per = min(per, rows)
    for i in range(0, rows, per):
        step(i, min(per, rows - i))


def joined(buf, k, rows, part):
    return buf, k * rows


def reduce_step(ring, bufs, recvs, k, got, cbit_meta):
    m, n = ring.half, ring.n
    width = 1024
    sizes = []
    for buf in bufs:
        r = buf.shape[0] // n
        sizes.append((r, buf.shape[1] // width))
    full = sum(r * c for r, c in sizes)
    half = k == m
    total = full // 2 if half else full
    args = [cbit_meta, *bufs, *recvs] + ([got] if got is not None else [])
    nb = len(bufs)

    def body(meta, *refs):
        bs, rs = refs[:nb], refs[nb : 2 * nb]
        g = refs[2 * nb] if got is not None else None
        o = refs[-1]
        c = meta[0, n + 1]
        at, gat = 0, 0
        for b, rv, (r, cs) in zip(bs, rs, sizes):
            h = r // 2
            for j in range(cs):
                col = slice(j * width, (j + 1) * width)
                if half:
                    mine = b[m * r : m * r + h, col].astype(F32)
                    theirs = rv[0:h, col].astype(F32)
                    o[at : at + h, :] = (mine + theirs).astype(BF)
                    at += h
                else:
                    base = h + (n - k - m - 1) * r
                    mine = b[k * r : (k + 1) * r, col].astype(F32)
                    theirs = rv[base : base + r, col].astype(F32)
                    v = mine + theirs
                    if g is not None and g.shape[0] == total:
                        v = v + g[at : at + r, :].astype(F32)
                        o[at : at + r, :] = v.astype(BF)
                    else:
                        top = jnp.where(c == 0, 1.0, 0.0)
                        gv = g[gat : gat + h, :].astype(F32)
                        o[at : at + h, :] = (v[:h] + gv * top).astype(BF)
                        o[at + h : at + r, :] = (v[h:] + gv * (1.0 - top)).astype(BF)
                        gat += h
                    at += r

    return kernel_call(body, [out((total, width), BF)], args, smem=(0,), name="ring_sum")[0]


def owner_sum(ring, bufs, got, meta):
    n = ring.n
    width = 1024
    sizes = [(b.shape[0] // n, b.shape[1] // width) for b in bufs]
    full = sum(r * c for r, c in sizes)
    nb = len(bufs)

    def body(meta, *refs):
        bs, g, keep, send = refs[:nb], refs[nb], refs[nb + 1], refs[nb + 2]
        c = meta[0, n + 1]
        at, to = 0, 0
        for b, (r, cs) in zip(bs, sizes):
            h = r // 2
            for j in range(cs):
                v = b[0:r, j * width : (j + 1) * width].astype(F32) + g[at : at + r, :].astype(F32)
                v = v.astype(BF)
                keep[to : to + h, :] = jnp.where(c == 0, v[:h], v[h:])
                send[to : to + h, :] = jnp.where(c == 0, v[h:], v[:h])
                at += r
                to += h

    o = out((full // 2, width), BF)
    return kernel_call(body, [o, o], [meta, *bufs, got], smem=(0,), name="owner_sum")


def add_kernel(a_ref, b_ref, o_ref):
    o_ref[...] = (a_ref[...].astype(F32) + b_ref[...].astype(F32)).astype(BF)


def add2(a, b):
    return kernel_call(add_kernel, [out(a.shape, BF)], [a, b], name="pair_sum")[0]


def finish(ring, mine, theirs, sizes, meta):
    n = ring.n
    width = 1024

    def body(meta, a_ref, b_ref, *outs):
        c = meta[0, n + 1]
        to = 0
        for o, (r, cs) in zip(outs, sizes):
            h = r // 2
            for j in range(cs):
                col = slice(j * width, (j + 1) * width)
                a = a_ref[to : to + h, :].astype(F32)
                b = b_ref[to : to + h, :].astype(F32)
                o[0:h, col] = jnp.where(c == 0, a, b)
                o[h:r, col] = jnp.where(c == 0, b, a)
                to += h

    outs = [out((r, cs * width), F32) for r, cs in sizes]
    return kernel_call(body, outs, [meta, mine, theirs], smem=(0,), name="halves_joined")


def reduce_group(ring, bufs, recvs, meta):
    m, n = ring.half, ring.n
    got = None
    for k in range(m, 0, -1):
        got = ring.along(reduce_step(ring, bufs, recvs, k, got, meta))
    keep, send = owner_sum(ring, bufs, got, meta)
    u = add2(keep, ring.core(send))
    bit = 2
    while bit < ring.reps:
        u = add2(u, ring.send(u, lambda r, f, bit=bit: (r ^ bit, f)))
        bit *= 2
    sizes = [(b.shape[0] // n, b.shape[1] // 1024) for b in bufs]
    return finish(ring, u, ring.core(u), sizes, meta)


def step_fn(mesh):
    ring = Ring(mesh)
    n, m = ring.n, ring.half
    rows_tab, slot_tab = ring.tables()

    def on_device(
        layer_input, item_ids, norm_gain, norm_bias, joint_weight, joint_bias, out_weight, out_bias,
        second_gain, second_bias, up_weight, up_bias, down_weight, down_bias, output_grad,
    ):
        rows, width = layer_input.shape
        ff = up_weight.shape[1]
        rps = width // n
        r_id, f_id = lax.axis_index("rep"), lax.axis_index("fsdp")
        cbit, xbit = r_id % 2, (r_id // 2) % 2
        line = cbit * n + f_id
        idx = jnp.asarray(rows_tab, jnp.int32)[line]
        slots = jnp.asarray(slot_tab, jnp.int32)[line]
        meta = jnp.concatenate([idx, xbit[None].astype(jnp.int32), cbit[None].astype(jnp.int32)])[None]

        t = (rps // 4) // 16 * 16
        left = xbit == 0
        qa, ka, va = (joint_weight[:, i * width : (i + 1) * width] for i in range(3))
        a1 = jnp.concatenate([qa, out_weight[:t]])
        b1 = jnp.concatenate([ka, out_weight[t : rps - t]])
        c1 = jnp.concatenate([va, out_weight[rps - t :]])
        ext1, opp1 = jnp.where(left, a1, c1), jnp.where(left, c1, a1)
        a2 = jnp.concatenate([up_weight[:, :width], down_weight[:t]])
        b2 = down_weight[t : 2 * rps - t]
        c2 = jnp.concatenate([up_weight[:, width:], down_weight[2 * rps - t :]])
        ext2, opp2 = jnp.where(left, a2, c2), jnp.where(left, c2, a2)
        na, nb = rps + t, 2 * rps - 2 * t

        def placed(v):
            full = jnp.tile(v.astype(F32), n)
            return jnp.where(jnp.arange(full.shape[0]) // v.shape[0] == f_id, full, 0.0)

        small = jnp.concatenate(
            [placed(v) for v in (norm_gain, norm_bias, joint_bias, out_bias, second_gain, second_bias, up_bias, down_bias)]
            + [jnp.zeros((6 * width,), F32)]
        ).reshape(16, width)
        bit = 1
        while bit < n:
            small = small + ring.send(small, lambda r, f, bit=bit: (r, f ^ bit))
            bit *= 2

        nr = 2 * (m - 1)
        g1 = gather(ring, ext1, b1, xbit, cbit)
        g2 = gather(ring, ext2, b2, xbit, cbit)

        def flat(own, g):
            return [*own, *g[0], *g[1], *g[2]]

        args = [meta, layer_input, small, *flat((ext1, b1, opp1), g1)]
        anys = tuple(range(3, len(args)))
        first, proj, wj, wo = kernel_call(
            functools.partial(qkv_kernel, ring, na, nb, t, nr),
            [out((rows, width), BF), out((rows, 3 * width), BF), out((width, 3 * width), BF), out((width, width), BF)],
            args, anys=anys, smem=(0,), scratch=[pltpu.SemaphoreType.DMA((6 * n,))],
            flops=6 * rows * width * width, name="projection",
        )
        col_ids, row_ids = item_ids[:, None], item_ids[None, :]
        (attended,) = kernel_call(
            attend_kernel, [out((rows, width), BF)], [proj, col_ids, row_ids],
            flops=4 * rows * 256 * width, name="attend",
        )
        middle, second = kernel_call(
            out_kernel, [out((rows, width), F32), out((rows, width), BF)],
            [attended, wo, layer_input, small], flops=2 * rows * width * width, name="out_projection",
        )
        args = [meta, second, small, *flat((ext2, b2, opp2), g2)]
        active, slope, wu, wd = kernel_call(
            functools.partial(up_kernel, ring, na, nb, t, nr),
            [out((rows, ff), BF), out((rows, ff), BF), out((width, ff), BF), out((ff, width), BF)],
            args, anys=tuple(range(3, len(args))), smem=(0,), scratch=[pltpu.SemaphoreType.DMA((6 * n,))],
            flops=2 * rows * width * ff, name="up_projection",
        )
        (dhidden,) = kernel_call(
            dact_kernel, [out((rows, ff), BF)], [output_grad, wd, slope],
            flops=2 * rows * width * ff, name="hidden_grad",
        )

        def offsets(r):
            h = r // 2
            q = jnp.arange(2)[None, :]
            swap = jnp.where((slots == m) & (cbit == 1), 1, 0)[:, None]
            return (slots[:, None] * r + (q ^ swap) * h).reshape(1, 2 * n).astype(jnp.int32)

        def weight_grad(l, r, tl=512, tn=512, name=None):
            kl, kr = l.shape[1], r.shape[1]
            buf, sums = kernel_call(
                functools.partial(weight_grad_kernel, n, tn, tl),
                [out((kl, kr), BF), out((8, kr), F32)],
                [offsets(kl // n), l, r], smem=(0,), flops=2 * kl * kr * rows, name=name,
            )
            sent = m * (kl // n) + kl // n // 2
            return buf, ring.core(buf[sent:]), sums[0]

        down_buf, down_recv, s_down = weight_grad(active, output_grad, name="down_grad")
        up_buf, up_recv, s_up = weight_grad(second, dhidden, name="up_grad")
        dmid, dbranch, datt, sg2, sb2 = kernel_call(
            dsecond_kernel,
            [out((rows, width), F32), out((rows, width), BF), out((rows, width), BF), out((8, width), F32), out((8, width), F32)],
            [dhidden, wu, wo, middle, output_grad, small],
            flops=2 * rows * width * (ff + width), name="second_norm_grad",
        )
        out_buf, out_recv, s_out = weight_grad(attended, dbranch, name="out_grad")
        g_down, g_up, g_out = reduce_group(ring, [down_buf, up_buf, out_buf], [down_recv, up_recv, out_recv], meta)

        (dproj,) = kernel_call(
            attend_back_kernel, [out((rows, 3 * width), BF)], [proj, datt, col_ids, row_ids],
            scratch=[VM((rows, width), F32), VM((rows, width), F32)],
            flops=10 * rows * 256 * width, name="attend_grad",
        )
        joint_buf, joint_recv, s_joint = weight_grad(first, dproj, name="joint_grad")
        (g_joint,) = reduce_group(ring, [joint_buf], [joint_recv], meta)
        input_grad, sg1, sb1 = kernel_call(
            dfirst_kernel, [out((rows, width), BF), out((8, width), F32), out((8, width), F32)],
            [dproj, wj, layer_input, dmid, small], scratch=[VM((rows, width), F32)],
            flops=6 * rows * width * width, name="first_norm_grad",
        )
        (layer_output,) = kernel_call(
            down_kernel, [out((rows, width), BF)], [active, wd, middle, small],
            flops=2 * rows * width * ff, name="down_projection",
        )

        vec = jnp.concatenate(
            [jnp.sum(sg1, 0), jnp.sum(sb1, 0), s_joint[:width], s_joint[2 * width :], s_out,
             jnp.sum(sg2, 0), jnp.sum(sb2, 0), s_up, s_down]
        ).reshape(10, width)
        bit = 1
        while bit < n:
            vec = vec + ring.send(vec, lambda r, f, bit=bit: (r, f ^ bit))
            bit *= 2
        bit = 1
        while bit < ring.reps:
            vec = vec + ring.send(vec, lambda r, f, bit=bit: (r ^ bit, f))
            bit *= 2
        vec = vec.reshape(-1)

        def mine(row, count):
            size = count * width // n
            return lax.dynamic_slice_in_dim(vec[row * width : (row + count) * width], f_id * size, size)

        return (
            layer_output, input_grad, mine(GAIN1, 1), mine(BIAS1, 1), g_joint, mine(JB_Q, 2), g_out, mine(OUT_B, 1),
            mine(GAIN2, 1), mine(BIAS2, 1), g_up, mine(UP_B, 2), g_down, mine(DOWN_B, 1),
        )

    return on_device


def solution(mesh):
    row, vecs, mat = P(("rep", "fsdp"), None), P("fsdp"), P("fsdp", None)
    placed = (
        row, P(("rep", "fsdp")), vecs, vecs, mat, vecs, mat, vecs, vecs, vecs, mat, vecs, mat, vecs, row,
    )
    return jax.shard_map(
        step_fn(mesh),
        mesh=mesh,
        in_specs=placed,
        out_specs=(row, row, vecs, vecs, mat, vecs, mat, vecs, vecs, vecs, mat, vecs, mat, vecs),
        check_vma=False,
    )
```

```python
import functools
import math

import jax
import jax.numpy as jnp
from jax import lax
from jax.experimental import pallas as pl
from jax.experimental.pallas import tpu as pltpu
from jax.sharding import PartitionSpec as P

H = 8
HD = 128
HALF = H // 2
EPS = 1e-05
MASKED = -1e30
LOG2E = 1.4426950408889634
C0 = math.sqrt(2.0 / math.pi)
BF = jnp.bfloat16
F32 = jnp.float32
VM = pltpu.VMEM
MAIN = 60 * 10**9
MIB = 2**20

GAIN1, BIAS1, JB_Q, JB_V, OUT_B, GAIN2, BIAS2, UP_B, DOWN_B = 0, 1, 2, 3, 4, 5, 6, 7, 9
SMALL_ROWS = 16


def nbytes(a):
    return math.prod(a.shape) * jnp.dtype(a.dtype).itemsize


def kernel_call(body, outs, args, deps=(), smem=(), anys=(), far=(), scratch=(), extra=8, name=None):
    own = sum(nbytes(s) for s in scratch if getattr(s, "dtype", None) in (BF, F32))
    count, made = len(args), len(outs)
    deps = [d for d in deps if d is not None]

    def space(i):
        return pl.ANY if i in anys else pltpu.HBM if i in far else pltpu.SMEM if i in smem else VM

    args = [pltpu.with_memory_space_constraint(v, pltpu.HBM) if i in far else v for i, v in enumerate(args)]

    def run(*refs):
        body(*refs[:count], *refs[count + len(deps) :])

    return pl.pallas_call(
        run,
        out_shape=list(outs),
        in_specs=[pl.BlockSpec(memory_space=space(i)) for i in range(count)]
        + [pl.BlockSpec(memory_space=pl.ANY) for _ in deps],
        out_specs=[pl.BlockSpec(memory_space=VM) for _ in outs],
        scratch_shapes=list(scratch),
        compiler_params=pltpu.CompilerParams(vmem_limit_bytes=own + int(extra * MIB)),
        cost_estimate=pl.CostEstimate(flops=MAIN, bytes_accessed=0, transcendentals=0),
        name=name,
    )(*args, *deps)


def out(shape, dtype):
    return jax.ShapeDtypeStruct(shape, dtype)


class Line:
    def __init__(self):
        self.mark = None

    def call(self, body, outs, args, deps=(), **kw):
        made = kernel_call(body, outs, args, deps=(self.mark, *deps), **kw)
        self.mark = min(made, key=nbytes)
        return made


def dot(a, b):
    return jnp.dot(a, b, preferred_element_type=F32)


def dot_tn(a, b):
    return lax.dot_general(a, b, (((0,), (0,)), ((), ())), preferred_element_type=F32)


def dot_nt(a, b):
    return lax.dot_general(a, b, (((1,), (1,)), ((), ())), preferred_element_type=F32)


def loop(count, step):
    lax.fori_loop(0, count, lambda i, z: (step(i), z)[1], 0)


def span(i, size):
    return pl.ds(pl.multiple_of(i * size, size), size)


def normalized(values):
    center = values - jnp.mean(values, axis=-1, keepdims=True)
    spread = jnp.mean(center * center, axis=-1, keepdims=True)
    factor = lax.rsqrt(spread + EPS)
    return center * factor, factor


class Ring:
    def __init__(self, mesh):
        self.axes = ("rep", "fsdp")
        self.n = mesh.shape["fsdp"]
        self.reps = mesh.shape["rep"]
        n = self.n
        self.order = list(range(0, n, 2)) + list(range(n - 1, 0, -2))
        self.place = [self.order.index(f) for f in range(n)]
        self.half = n // 2

    def send(self, v, target, keep=lambda r, f: True):
        n = self.n
        pairs = []
        for r in range(self.reps):
            for f in range(n):
                if keep(r, f):
                    r2, f2 = target(r, f)
                    pairs.append((r * n + f, r2 * n + f2))
        return lax.ppermute(v, self.axes, pairs)

    def along(self, v):
        def target(r, f):
            step = 1 if r % 2 == 0 else -1
            return r, self.order[(self.place[f] + step) % self.n]

        return self.send(v, target)

    def core(self, v):
        return self.send(v, lambda r, f: (r ^ 1, f))

    def across(self, v, keep=lambda r, f: True):
        return self.send(v, lambda r, f: (r ^ 2, f), keep)

    def here(self):
        r = lax.axis_index("rep")
        return r % 2, (r // 2) % 2, lax.axis_index("fsdp")

    def own_place(self):
        n, (c, _, f) = self.n, self.here()
        return jnp.where(f % 2 == 0, f // 2, n - 1 - f // 2), 1 - 2 * c

    def shard_back(self, h):
        n, (p, d) = self.n, self.own_place()
        q = lax.rem(p - d * h + 2 * n, n)
        return jnp.where(q < n // 2, 2 * q, 2 * (n - 1 - q) + 1)

    def slot(self, j):
        n, (p, d) = self.n, self.own_place()
        return lax.rem((self.place[j] - p) * d + n, n)


def cut_kernel(ring, a, v, ext, *more):
    ext[...] = v[0:a, :]
    if more:
        (rest,) = more
        if rest.shape == v.shape:
            rest[...] = v[...]
        else:
            rest[...] = v[pl.ds(pl.multiple_of(ring.here()[0] * a, 16), rest.shape[0]), :]


def gather(ring, firsts, a, extras):
    m = ring.half
    b, width = firsts[0].shape[0] - a, firsts[0].shape[1]
    groups = [dict(ring=[], out=[], pring=[], pout=[], due=[]) for _ in firsts]
    for h in range(1, m + 2):
        for i, g in enumerate(groups):
            if h == 1:
                g["ring"].append(ring.along(firsts[i]))
                continue
            v = g["ring"][-1]
            shapes = [out((a, width), BF)]
            if h <= m:
                shapes.append(out(v.shape if h < m else (b, width), BF))
            ext, *rest = kernel_call(functools.partial(cut_kernel, ring, a), shapes, [v], deps=g["due"], name="cut")
            if rest:
                g["ring"].append(ring.along(rest[0]))
            even = (lambda r, f: r % 2 == 0) if h > m else (lambda r, f: True)
            g["due"] = [ring.across(ext, even), ring.core(v)]
            if h > 2:
                g["pout"].append(ring.core(g["out"][-1]))
                g["due"].append(g["pout"][-1])
            g["out"].append(g["due"][0])
            g["pring"].append(g["due"][1])
            more = extras.send(ext)
            if more is not None:
                g["due"].append(more)
    for g in groups:
        g["pout"].append(ring.core(g["out"][-1]))
    return groups


def flat(own, opp, g):
    return [own, opp, *g["ring"], *g["pring"], *g["out"], *g["pout"]]


def place_parts(ring, a, refs, put):
    n, m = ring.n, ring.half
    own, opp, refs = refs[0], refs[1], refs[2:]
    rings, prings, outs, pouts = (refs[i * m : (i + 1) * m] for i in range(4))

    def all_parts(step, ext, mid, mid0, other):
        s = ring.shard_back(step)
        put("mid", s, mid, mid0)
        put("ext", s, ext, 0)
        put("opp", s, other, 0)

    all_parts(0, own, own, a, opp)
    for h in range(1, m):
        all_parts(h, rings[h - 1], rings[h - 1], a, outs[h - 1])
        all_parts(n - h, prings[h - 1], prings[h - 1], a, pouts[h - 1])

    c = ring.here()[0]

    @pl.when(c == 0)
    def _():
        all_parts(m, rings[-1], prings[-1], 0, outs[-1])

    @pl.when(c == 1)
    def _():
        all_parts(m, prings[-1], rings[-1], 0, pouts[-1])


def ln_rows(x_ref, gain, bias, o_ref, rows=384):
    def step(i):
        at = span(i, rows)
        n, _ = normalized(x_ref[at, :].astype(F32))
        o_ref[at, :] = (n * gain + bias).astype(BF)

    loop(x_ref.shape[0] // rows, step)


def split_kernel(ring, t, jw, ow, first, opp, sems):
    width = ow.shape[1]
    rps = ow.shape[0]
    a = rps + t
    x = ring.here()[1]
    made = []

    def copy(src, dst):
        c = pltpu.make_async_copy(src, dst, sems.at[len(made)])
        c.start()
        made.append(c)

    def cols(side):
        return jw.at[:, pl.ds(pl.multiple_of(side * 2 * width, width), width)]

    copy(cols(x), first.at[pl.ds(0, rps), :])
    copy(jw.at[:, pl.ds(width, width)], first.at[pl.ds(a, rps), :])
    copy(ow.at[pl.ds(t, rps - 2 * t), :], first.at[pl.ds(a + rps, rps - 2 * t), :])
    copy(cols(1 - x), opp.at[pl.ds(0, rps), :])
    if t:
        copy(ow.at[pl.ds(pl.multiple_of(x * (rps - t), 16), t), :], first.at[pl.ds(rps, t), :])
        copy(ow.at[pl.ds(pl.multiple_of((1 - x) * (rps - t), 16), t), :], opp.at[pl.ds(rps, t), :])
    for c in made:
        c.wait()


def split_ff_kernel(ring, t, uw, dw, first, opp, sems):
    width = dw.shape[1]
    rps = uw.shape[0]
    a = rps + t
    x = ring.here()[1]
    made = []

    def copy(src, dst):
        c = pltpu.make_async_copy(src, dst, sems.at[len(made)])
        c.start()
        made.append(c)

    def cols(side):
        return uw.at[:, pl.ds(pl.multiple_of(side * width, width), width)]

    copy(cols(x), first.at[pl.ds(0, rps), :])
    copy(dw.at[pl.ds(t, 2 * rps - 2 * t), :], first.at[pl.ds(a, 2 * rps - 2 * t), :])
    copy(cols(1 - x), opp.at[pl.ds(0, rps), :])
    if t:
        copy(dw.at[pl.ds(pl.multiple_of(x * (2 * rps - t), 16), t), :], first.at[pl.ds(rps, t), :])
        copy(dw.at[pl.ds(pl.multiple_of((1 - x) * (2 * rps - t), 16), t), :], opp.at[pl.ds(rps, t), :])
    for c in made:
        c.wait()


def small_kernel(ring, *refs):
    parts, o_ref = refs[:-1], refs[-1]
    width = o_ref.shape[1]
    n, f = ring.n, ring.here()[2]
    row = 0
    o_ref[...] = jnp.zeros_like(o_ref)
    for part in parts:
        size = part.shape[0]
        full = size * n
        i = lax.broadcasted_iota(jnp.int32, (size, full), 0)
        j = lax.broadcasted_iota(jnp.int32, (size, full), 1)
        hot = jnp.where(j == i + f * size, 1.0, 0.0).astype(BF)
        placed = dot(jnp.broadcast_to(part[...].astype(F32)[None, :], (8, size)).astype(BF), hot)
        for k in range(full // width):
            o_ref[row : row + 1, :] = placed[0:1, k * width : (k + 1) * width]
            row += 1


def add_f32_kernel(a_ref, b_ref, o_ref):
    o_ref[...] = a_ref[...] + b_ref[...]


def own_small_kernel(ring, vec, *outs):
    n, f = ring.n, ring.here()[2]
    width = vec.shape[1]
    row = 0
    for o in outs:
        size = o.shape[1]
        count = size * n // width
        got = jnp.zeros((1, size), F32)
        for k in range(count):
            for j in range(width // size):
                part = vec[row + k : row + k + 1, j * size : (j + 1) * size]
                got = got + part * jnp.where(f == k * (width // size) + j, 1.0, 0.0)
        o[...] = got
        row += count


def ln_kernel(x_ref, small, o_ref):
    ln_rows(x_ref, small[pl.ds(GAIN1, 1), :], small[pl.ds(BIAS1, 1), :], o_ref)


def qkv_kernel(ring, a, t, first, small, *refs):
    refs, outs = refs[:-5], refs[-5:]
    proj, ws, wo = outs[:2], outs[2:4], outs[4]
    width = first.shape[1]
    rps = width // ring.n
    hw = width // 2
    xb = ring.here()[1]

    def put(part, s, ref, r0):
        row = pl.multiple_of(s * rps, rps)
        if part == "mid":
            for k in range(2):
                ws[k][pl.ds(row, rps), hw : 2 * hw] = ref[r0 : r0 + rps, k * hw : (k + 1) * hw]
            wo[pl.ds(pl.multiple_of(row + t, 16), rps - 2 * t), :] = ref[r0 + rps : r0 + 2 * rps - 2 * t, :]
        else:
            side = xb if part == "ext" else 1 - xb
            col = pl.multiple_of(side * 2 * hw, hw)
            for k in range(2):
                ws[k][pl.ds(row, rps), pl.ds(col, hw)] = ref[0:rps, k * hw : (k + 1) * hw]
            if t:
                wo[pl.ds(pl.multiple_of(row + side * (rps - t), 16), t), :] = ref[rps : rps + t, :]

    place_parts(ring, a, refs, put)
    for k in range(2):

        def tile(i, k=k):
            at = span(i, hw)
            v = dot(first[...], ws[k][:, at])
            use = jnp.where(i == 0, 1.0, 0.0), jnp.where(i == 2, 1.0, 0.0)
            shift = small[pl.ds(JB_Q, 1), k * hw : (k + 1) * hw] * use[0]
            shift = shift + small[pl.ds(JB_V, 1), k * hw : (k + 1) * hw] * use[1]
            proj[k][:, at] = (v + shift).astype(BF)

        loop(3, tile)


def mask(col_ids, row_ids, q0, k0, queries, keys):
    same = col_ids[k0 : k0 + keys, :] == row_ids[:, q0 : q0 + queries]
    kpos = lax.broadcasted_iota(jnp.int32, (keys, queries), 0) + k0
    qpos = lax.broadcasted_iota(jnp.int32, (keys, queries), 1) + q0
    return jnp.where(same & (kpos <= qpos), 0.0, MASKED).astype(F32)


def soft(q, k, bias):
    s = dot_nt(k, q) * (HD ** (-0.5) * LOG2E) + bias
    p = jnp.exp2(s - jnp.max(s, axis=0, keepdims=True))
    return p * (1.0 / jnp.sum(p, axis=0, keepdims=True))


def head_cols(part, h):
    return slice((part * HALF + h) * HD, (part * HALF + h + 1) * HD)


def tiles(rows, queries, back):
    for q0 in range(0, rows, queries):
        lo = min(q0, back)
        yield q0, q0 - lo, queries + lo


def attend_kernel(proj_a, proj_b, col_ids, row_ids, o_ref):
    nq = 256
    for q0, k0, nk in tiles(o_ref.shape[0], nq, 128):
        at_q, at_k = slice(q0, q0 + nq), slice(k0, k0 + nk)
        bias = mask(col_ids, row_ids, q0, k0, nq, nk)
        for k, proj in enumerate((proj_a, proj_b)):
            for h in range(HALF):
                w = soft(proj[at_q, head_cols(0, h)], proj[at_k, head_cols(1, h)], bias).astype(BF)
                col = (k * HALF + h) * HD
                o_ref[at_q, col : col + HD] = dot_tn(w, proj[at_k, head_cols(2, h)]).astype(BF)


def out_kernel(att, wo, x_ref, small, middle, second):
    tn = 512

    def step(i):
        at = span(i, tn)
        middle[:, at] = x_ref[:, at].astype(F32) + dot(att[...], wo[:, at]) + small[pl.ds(OUT_B, 1), at]

    loop(wo.shape[1] // tn, step)
    ln_rows(middle, small[pl.ds(GAIN2, 1), :], small[pl.ds(BIAS2, 1), :], second)


def gelu_both(h):
    h2 = h * h
    half = 0.5 + 0.5 * jnp.tanh(h * (C0 + (C0 * 0.044715) * h2))
    act = h * half
    return act, half + act * (1.0 - half) * (2.0 * C0 + (6.0 * C0 * 0.044715) * h2)


def up_kernel(ring, a, t, second, small, *refs):
    refs, outs = refs[:-4], refs[-4:]
    active, slope, wu, wd = outs
    width = second.shape[1]
    rps = width // ring.n
    xb = ring.here()[1]

    def put(part, s, ref, r0):
        row = pl.multiple_of(s * rps, rps)
        drow = pl.multiple_of(s * 2 * rps, 2 * rps)
        if part == "mid":
            wd[pl.ds(pl.multiple_of(drow + t, 16), 2 * rps - 2 * t), :] = ref[r0 : r0 + 2 * rps - 2 * t, :]
        else:
            side = xb if part == "ext" else 1 - xb
            wu[pl.ds(row, rps), pl.ds(pl.multiple_of(side * width, width), width)] = ref[0:rps, :]
            if t:
                wd[pl.ds(pl.multiple_of(drow + side * (2 * rps - t), 16), t), :] = ref[rps : rps + t, :]

    place_parts(ring, a, refs, put)
    tn = 512
    per = width // tn

    def step(i):
        at = span(i, tn)
        shift = small[pl.ds(UP_B + i // per, 1), span(i % per, tn)]
        act, s = gelu_both(dot(second[...], wu[:, at]) + shift)
        active[:, at] = act.astype(BF)
        slope[:, at] = s.astype(BF)

    loop(2 * per, step)


def dact_kernel(og, wd, slope, o_ref):
    tn = 256

    def step(i):
        at = span(i, tn)
        o_ref[:, at] = (dot_nt(og[...], wd[at, :]) * slope[:, at].astype(F32)).astype(BF)

    loop(o_ref.shape[1] // tn, step)


def down_kernel(active, wd, middle, small, o_ref):
    tn = 512

    def step(i):
        at = span(i, tn)
        o_ref[:, at] = (middle[:, at] + dot(active[...], wd[:, at]) + small[pl.ds(DOWN_B, 1), at]).astype(BF)

    loop(o_ref.shape[1] // tn, step)


def weight_grad_kernel(ring, tn, tl, left, right, buf, sent, sums):
    n, m = ring.n, ring.half
    half = left.shape[1] // n // 2
    slots = [ring.slot(j) for j in range(n)]
    swap = [jnp.where(k == m, ring.here()[0], 0) for k in slots]
    ones = jnp.ones((8, right.shape[0]), BF)
    per = tl // half

    def step(i):
        at = span(i, tn)
        r = right[:, at]
        sums[:, at] = dot(ones, r)
        for l in range(left.shape[1] // tl):
            v = dot_tn(left[:, l * tl : (l + 1) * tl], r).astype(BF)
            for s in range(per):
                j, q = divmod(l * per + s, 2)
                row = pl.multiple_of((2 * slots[j] + (swap[j] + q) % 2) * half, half)
                buf[pl.ds(row, half), at] = v[s * half : (s + 1) * half, :]
        sent[:, at] = buf[buf.shape[0] - sent.shape[0] :, at]

    loop(right.shape[1] // tn, step)


def norm_back(values, d, gain):
    n, r = normalized(values)
    g = d * gain
    t = r * (g - jnp.mean(g, axis=-1, keepdims=True) - n * jnp.mean(g * n, axis=-1, keepdims=True))
    return t, d * n


def group_sum(v):
    return jnp.sum(v.reshape(v.shape[0] // 8, 8, v.shape[1]), axis=0)


def dsecond_kernel(dh, wu, wo, middle, og, small, dmid, dbranch, datt, sg, sb):
    g = small[pl.ds(GAIN2, 1), :]
    sg[...] = jnp.zeros_like(sg)
    sb[...] = jnp.zeros_like(sb)
    tn = 512

    def step(i):
        at = span(i, tn)
        dmid[:, at] = dot_nt(dh[...], wu[at, :])

    loop(dmid.shape[1] // tn, step)
    rows = 256

    def norm(i):
        at = span(i, rows)
        d = dmid[at, :]
        t, dn = norm_back(middle[at, :], d, g)
        sg[...] += group_sum(dn)
        sb[...] += group_sum(d)
        v = og[at, :].astype(F32) + t
        dmid[at, :] = v
        dbranch[at, :] = v.astype(BF)

    loop(dh.shape[0] // rows, norm)

    def back(i):
        at = span(i, tn)
        datt[:, at] = dot_nt(dbranch[...], wo[at, :]).astype(BF)

    loop(datt.shape[1] // tn, back)


def attend_back_kernel(part, proj, datt, col_ids, row_ids, o_ref, acc_k, acc_v):
    rows, hw = acc_k.shape
    scale = HD ** (-0.5)
    nq = 128
    heads = range(HALF)
    acc_k[...] = jnp.zeros_like(acc_k)
    acc_v[...] = jnp.zeros_like(acc_v)
    for q0, k0, nk in tiles(rows, nq, 64):
        at_q, at_k = slice(q0, q0 + nq), slice(k0, k0 + nk)
        bias = mask(col_ids, row_ids, q0, k0, nq, nk)
        q = [proj[at_q, head_cols(0, h)] for h in heads]
        k = [proj[at_k, head_cols(1, h)] for h in heads]
        do = [datt[at_q, head_cols(part, h)] for h in heads]
        dw = [dot_nt(proj[at_k, head_cols(2, h)], do[h]) for h in heads]
        p = [soft(q[h], k[h], bias) for h in heads]
        for h in heads:
            acc_v[at_k, head_cols(0, h)] += dot(p[h].astype(BF), do[h])
        ds = [(p[h] * (dw[h] - jnp.sum(p[h] * dw[h], axis=0, keepdims=True))).astype(BF) for h in heads]
        for h in heads:
            acc_k[at_k, head_cols(0, h)] += dot(ds[h], q[h])
            o_ref[at_q, head_cols(0, h)] = (dot_tn(ds[h], k[h]) * scale).astype(BF)
    o_ref[:, hw : 2 * hw] = (acc_k[...] * scale).astype(BF)
    o_ref[:, 2 * hw :] = acc_v[...].astype(BF)


def dfirst_kernel(da, db, wa, wb, acc):
    tn = 512

    def step(i):
        at = span(i, tn)
        acc[:, at] = dot_nt(da[...], wa[at, :]) + dot_nt(db[...], wb[at, :])

    loop(acc.shape[1] // tn, step)


def first_norm_back_kernel(acc, x_ref, dmid, small, o_ref, sg, sb):
    g = small[pl.ds(GAIN1, 1), :]
    sg[...] = jnp.zeros_like(sg)
    sb[...] = jnp.zeros_like(sb)
    rows = 256

    def norm(i):
        at = span(i, rows)
        d = acc[at, :]
        t, dn = norm_back(x_ref[at, :].astype(F32), d, g)
        sg[...] += group_sum(dn)
        sb[...] += group_sum(d)
        o_ref[at, :] = (dmid[at, :] + t).astype(BF)

    loop(x_ref.shape[0] // rows, norm)


def gather_small_kernel(sg1, sb1, ja, jb, so, sg2, sb2, su, sd, o_ref):
    hw = ja.shape[1] // 3
    o_ref[...] = jnp.zeros_like(o_ref)

    def put(row, v):
        o_ref[row : row + 1, :] = v

    put(GAIN1, jnp.sum(sg1[...], axis=0, keepdims=True))
    put(BIAS1, jnp.sum(sb1[...], axis=0, keepdims=True))
    for k, s in enumerate((ja, jb)):
        o_ref[JB_Q : JB_Q + 1, k * hw : (k + 1) * hw] = s[0:1, 0:hw]
        o_ref[JB_V : JB_V + 1, k * hw : (k + 1) * hw] = s[0:1, 2 * hw :]
    put(OUT_B, so[0:1, :])
    put(GAIN2, jnp.sum(sg2[...], axis=0, keepdims=True))
    put(BIAS2, jnp.sum(sb2[...], axis=0, keepdims=True))
    for k in range(2):
        put(UP_B + k, su[0:1, k * 2 * hw : (k + 1) * 2 * hw])
    put(DOWN_B, sd[0:1, :])


class Grads:
    def __init__(self, n, bufs, recvs, width):
        self.bufs, self.recvs, self.width = bufs, recvs, width
        self.sizes = [(b.shape[0] // n, b.shape[1] // width) for b in bufs]
        self.rows = sum(r * c for r, c in self.sizes)


def reduce_step(ring, gr, k, got):
    m, n = ring.half, ring.n
    width = gr.width
    half = k == m
    total = gr.rows // 2 if half else gr.rows
    args = [*gr.bufs, *gr.recvs] + ([got] if got is not None else [])
    nb = len(gr.bufs)

    def body(*refs):
        bs, rs = refs[:nb], refs[nb : 2 * nb]
        g = refs[2 * nb] if got is not None else None
        o = refs[-1]
        c = ring.here()[0]
        at, gat = 0, 0
        for b, rv, (r, cs) in zip(bs, rs, gr.sizes):
            h = r // 2
            for j in range(cs):
                col = slice(j * width, (j + 1) * width)
                if half:
                    v = b[m * r : m * r + h, col].astype(F32) + rv[0:h, col].astype(F32)
                    o[at : at + h, :] = v.astype(BF)
                    at += h
                else:
                    base = h + (n - k - m - 1) * r
                    v = b[k * r : (k + 1) * r, col].astype(F32) + rv[base : base + r, col].astype(F32)
                    if g.shape[0] == total:
                        o[at : at + r, :] = (v + g[at : at + r, :].astype(F32)).astype(BF)
                    else:
                        top = jnp.where(c == 0, 1.0, 0.0)
                        gv = g[gat : gat + h, :].astype(F32)
                        o[at : at + h, :] = (v[:h] + gv * top).astype(BF)
                        o[at + h : at + r, :] = (v[h:] + gv * (1.0 - top)).astype(BF)
                        gat += h
                    at += r

    return body, [out((total, width), BF)], args


def owner_sum(ring, gr, got):
    nb = len(gr.bufs)

    def body(*refs):
        bs, g, keep, send = refs[:nb], refs[nb], refs[nb + 1], refs[nb + 2]
        c = ring.here()[0]
        at, to = 0, 0
        for b, (r, cs) in zip(bs, gr.sizes):
            h = r // 2
            for j in range(cs):
                v = b[0:r, j * gr.width : (j + 1) * gr.width].astype(F32) + g[at : at + r, :].astype(F32)
                v = v.astype(BF)
                keep[to : to + h, :] = jnp.where(c == 0, v[:h], v[h:])
                send[to : to + h, :] = jnp.where(c == 0, v[h:], v[:h])
                at += r
                to += h

    o = out((gr.rows // 2, gr.width), BF)
    return body, [o, o], [*gr.bufs, got]


def add_kernel(a_ref, b_ref, o_ref):
    o_ref[...] = (a_ref[...].astype(F32) + b_ref[...].astype(F32)).astype(o_ref.dtype)


def add2(a, b):
    return add_kernel, [out(a.shape, a.dtype)], [a, b]


def reduce_group(ring, gr):
    got = None
    for k in range(ring.half, 0, -1):
        (part,) = yield reduce_step(ring, gr, k, got)
        got = ring.along(part)
    keep, send = yield owner_sum(ring, gr, got)
    (u,) = yield add2(keep, ring.core(send))
    bit = 2
    while bit < ring.reps:
        (u,) = yield add2(u, ring.send(u, lambda r, f, bit=bit: (r ^ bit, f)))
        bit *= 2
    return u, ring.core(u)


class Rounds:
    def __init__(self, line):
        self.line = line
        self.live = {}
        self.jobs = {}
        self.done = {}

    def _advance(self, name, results):
        try:
            self.jobs[name] = next(self.live[name]) if results is None else self.live[name].send(results)
        except StopIteration as stop:
            self.done[name] = stop.value
            del self.live[name]
            self.jobs.pop(name, None)

    def add(self, name, chain):
        self.live[name] = chain
        self._advance(name, None)

    def turn(self):
        names = list(self.jobs)
        if not names:
            return
        jobs = [self.jobs[k] for k in names]
        args = [a for _, _, given in jobs for a in given]
        outs = [o for _, made, _ in jobs for o in made]

        def body(*refs):
            i, j = 0, len(args)
            for run, made, given in jobs:
                run(*refs[i : i + len(given)], *refs[j : j + len(made)])
                i, j = i + len(given), j + len(made)

        got = list(self.line.call(body, outs, args, name="sums"))
        for name, (_, made, _) in zip(names, jobs):
            self._advance(name, got[: len(made)])
            got = got[len(made) :]


def join_halves(c, parts, sizes, width, place):
    a_ref, b_ref = parts
    to = 0
    for i, (r, cs) in enumerate(sizes):
        h = r // 2
        for j in range(cs):
            a = a_ref[to : to + h, :].astype(F32)
            b = b_ref[to : to + h, :].astype(F32)
            place(i, slice(0, h), j, jnp.where(c == 0, a, b))
            place(i, slice(h, r), j, jnp.where(c == 0, b, a))
            to += h


def last_sum(job):
    return (yield job)


def finish(ring, gr, parts):
    def body(a_ref, b_ref, *outs):
        def place(i, rows, j, v):
            outs[i][rows, j * gr.width : (j + 1) * gr.width] = v

        join_halves(ring.here()[0], (a_ref, b_ref), gr.sizes, gr.width, place)

    return body, [out((r, cs * gr.width), F32) for r, cs in gr.sizes], list(parts)


def finish_joint(ring, gr, parts_a, parts_b):
    (r, cs), width = gr.sizes[0], gr.width
    _, ocs = gr.sizes[1]

    def body(a1, a2, b1, b2, o, o2):
        for k, pair in enumerate(((a1, a2), (b1, b2))):
            def place(i, rows, j, v, k=k):
                if i == 0:
                    at = (2 * j + k) * width
                    o[rows, at : at + width] = v
                else:
                    o2[rows, j * width : (j + 1) * width] = v

            join_halves(ring.here()[0], pair, gr.sizes[: 2 - k], width, place)

    return body, [out((r, 2 * cs * width), F32), out((r, ocs * width), F32)], [*parts_a, *parts_b]


def step_fn(mesh):
    ring = Ring(mesh)
    n, m = ring.n, ring.half

    def on_device(
        layer_input, item_ids, norm_gain, norm_bias, joint_weight, joint_bias, out_weight, out_bias,
        second_gain, second_bias, up_weight, up_bias, down_weight, down_bias, output_grad,
    ):
        rows, width = layer_input.shape
        ff = up_weight.shape[1]
        hw = width // 2
        rps = width // n
        t = (rps // 4) // 16 * 16
        a, b = rps + t, 2 * rps - 2 * t
        dma = pltpu.SemaphoreType.DMA
        shapes = [out((a + b, width), BF), out((a, width), BF)]
        line = Line()
        first1, opp1 = line.call(
            functools.partial(split_kernel, ring, t), shapes, [joint_weight, out_weight],
            far=(0, 1), scratch=[dma((6,))], name="split",
        )
        ids = [item_ids[:, None], item_ids[None, :]]
        first2, opp2 = line.call(
            functools.partial(split_ff_kernel, ring, t), shapes, [up_weight, down_weight], deps=ids,
            far=(0, 1), scratch=[dma((5,))], name="split_ff",
        )
        vectors = (norm_gain, norm_bias, joint_bias, out_bias, second_gain, second_bias, up_bias, down_bias)
        shared = {}

        def small_parts():
            (small,) = line.call(
                functools.partial(small_kernel, ring), [out((SMALL_ROWS, width), F32)], vectors, name="small",
            )
            mark = yield
            bit = 1
            while bit < n:
                other = ring.send(small, lambda r, f, bit=bit: (r, f ^ bit))
                mark = yield (small if bit > 1 else None)
                (small,) = kernel_call(add_f32_kernel, [out(small.shape, F32)], [small, other], deps=[mark], name="small_sum")
                bit *= 2
            shared["small"] = small
            (shared["first"],) = kernel_call(
                ln_kernel, [out((rows, width), BF)], [layer_input, small], deps=[mark], name="first_norm",
            )
            mark = yield shared["first"]
            while True:
                yield

        extras = small_parts()
        next(extras)
        g1, g2 = gather(ring, [first1, first2], a, extras)
        small, first = shared["small"], shared["first"]

        args = [first, small, *flat(first1, opp1, g1)]
        halves = [out((rows, 3 * hw), BF)] * 2
        proj_a, proj_b, wa, wb, wo = line.call(
            functools.partial(qkv_kernel, ring, a, t),
            halves + [out((width, 3 * hw), BF)] * 2 + [out((width, width), BF)],
            args, name="projection",
        )
        (attended,) = line.call(attend_kernel, [out((rows, width), BF)], [proj_a, proj_b, *ids], name="attend")
        middle, second = line.call(
            out_kernel, [out((rows, width), F32), out((rows, width), BF)],
            [attended, wo, layer_input, small], name="out_projection",
        )
        args = [second, small, *flat(first2, opp2, g2)]
        active, slope, wu, wd = line.call(
            functools.partial(up_kernel, ring, a, t),
            [out((rows, ff), BF), out((rows, ff), BF), out((width, ff), BF), out((ff, width), BF)],
            args, name="up_projection",
        )

        def weight_grad(l, r, tl=512, tn=512, name=None):
            kl, kr = l.shape[1], r.shape[1]
            kept = m * (kl // n) + kl // n // 2
            buf, sent, sums = line.call(
                functools.partial(weight_grad_kernel, ring, tn, tl),
                [out((kl, kr), BF), out((kl - kept, kr), BF), out((8, kr), F32)], [l, r], name=name,
            )
            return buf, ring.core(sent), sums

        rounds = Rounds(line)

        def begin(name, bufs, recvs, w):
            gr = Grads(n, bufs, recvs, w)
            rounds.add(name, reduce_group(ring, gr))
            return gr

        down_buf, down_recv, s_down = weight_grad(active, output_grad, name="down_grad")
        (dhidden,) = line.call(
            dact_kernel, [out((rows, ff), BF)], [output_grad, wd, slope], name="hidden_grad",
        )
        gr_down = begin("down", [down_buf], [down_recv], width)
        rounds.turn()
        up_buf, up_recv, s_up = weight_grad(second, dhidden, name="up_grad")
        rounds.turn()
        dmid, dbranch, datt, sg2, sb2 = line.call(
            dsecond_kernel,
            [out((rows, width), F32), out((rows, width), BF), out((rows, width), BF), out((8, width), F32), out((8, width), F32)],
            [dhidden, wu, wo, middle, output_grad, small], name="second_norm_grad",
        )
        gr_up = begin("up", [up_buf], [up_recv], width)
        rounds.turn()
        out_buf, out_recv, s_out = weight_grad(attended, dbranch, name="out_grad")

        def attend_back(part, proj):
            return line.call(
                functools.partial(attend_back_kernel, part), [out((rows, 3 * hw), BF)], [proj, datt, *ids],
                scratch=[VM((rows, hw), F32), VM((rows, hw), F32)], name="attend_grad",
            )[0]

        da = attend_back(0, proj_a)
        rounds.turn()
        ja_buf, ja_recv, s_ja = weight_grad(first, da, name="joint_grad")
        rounds.turn()
        db = attend_back(1, proj_b)
        gr_ja = begin("ja", [ja_buf, out_buf], [ja_recv, out_recv], hw)
        rounds.turn()
        jb_buf, jb_recv, s_jb = weight_grad(first, db, name="joint_grad")
        (dfirst,) = line.call(dfirst_kernel, [out((rows, width), F32)], [da, db, wa, wb], name="dfirst")
        gr_jb = begin("jb", [jb_buf], [jb_recv], hw)
        rounds.turn()
        input_grad, sg1, sb1 = line.call(
            first_norm_back_kernel, [out((rows, width), BF), out((8, width), F32), out((8, width), F32)],
            [dfirst, layer_input, dmid, small], name="first_norm_grad",
        )

        def small_grads():
            partial = [sg1, sb1, s_ja, s_jb, s_out, sg2, sb2, s_up, s_down]
            (vec,) = yield gather_small_kernel, [out((SMALL_ROWS, width), F32)], partial
            for axis, count in ((1, n), (0, ring.reps)):
                bit = 1
                while bit < count:
                    def target(r, f, bit=bit, axis=axis):
                        return (r, f ^ bit) if axis else (r ^ bit, f)

                    (vec,) = yield add2(vec, ring.send(vec, target))
                    bit *= 2
            outs = [out((1, v.shape[0]), F32) for v in vectors]
            return (yield functools.partial(own_small_kernel, ring), outs, [vec])

        rounds.add("small", small_grads())
        rounds.turn()
        (layer_output,) = line.call(
            down_kernel, [out((rows, width), BF)], [active, wd, middle, small], name="down_projection",
        )

        done, ready = rounds.done, {}
        while rounds.jobs:
            rounds.turn()
            for name, gr in (("down", gr_down), ("up", gr_up)):
                if name in done and name not in ready:
                    ready[name] = True
                    rounds.add("got " + name, last_sum(finish(ring, gr, done[name])))
            if "ja" in done and "jb" in done and "joint" not in ready:
                ready["joint"] = True
                rounds.add("got joint", last_sum(finish_joint(ring, gr_ja, done["ja"], done["jb"])))
        (g_down,), (g_up,), (g_joint, g_out) = (done["got " + k] for k in ("down", "up", "joint"))
        v = [v.reshape(-1) for v in done["small"]]
        return (
            layer_output, input_grad, v[0], v[1], g_joint, v[2], g_out, v[3], v[4], v[5], g_up, v[6], g_down, v[7],
        )

    return on_device


def solution(mesh):
    row, vecs, mat = P(("rep", "fsdp"), None), P("fsdp"), P("fsdp", None)
    placed = (
        row, P(("rep", "fsdp")), vecs, vecs, mat, vecs, mat, vecs, vecs, vecs, mat, vecs, mat, vecs, row,
    )
    return jax.shard_map(
        step_fn(mesh),
        mesh=mesh,
        in_specs=placed,
        out_specs=(row, row, vecs, vecs, mat, vecs, mat, vecs, vecs, vecs, mat, vecs, mat, vecs),
        check_vma=False,
    )
```

```python
import functools
import math

import jax
import jax.numpy as jnp
from jax import lax
from jax.experimental import pallas as pl
from jax.experimental.pallas import tpu as pltpu
from jax.sharding import PartitionSpec as P

H = 8
HD = 128
HALF = H // 2
EPS = 1e-05
MASKED = -1e30
LOG2E = 1.4426950408889634
C0 = math.sqrt(2.0 / math.pi)
BF = jnp.bfloat16
F32 = jnp.float32
VM = pltpu.VMEM
MAIN = 60 * 10**9
MIB = 2**20

GAIN1, BIAS1, JB_Q, JB_V, OUT_B, GAIN2, BIAS2, UP_B, DOWN_B = 0, 1, 2, 3, 4, 5, 6, 7, 9
SMALL_ROWS = 16


def nbytes(a):
    return math.prod(a.shape) * jnp.dtype(a.dtype).itemsize


def kernel_call(body, outs, args, deps=(), smem=(), anys=(), far=(), scratch=(), extra=8, name=None):
    own = sum(nbytes(s) for s in scratch if getattr(s, "dtype", None) in (BF, F32))
    count, made = len(args), len(outs)
    deps = [d for d in deps if d is not None]

    def space(i):
        return pl.ANY if i in anys else pltpu.HBM if i in far else pltpu.SMEM if i in smem else VM

    args = [pltpu.with_memory_space_constraint(v, pltpu.HBM) if i in far else v for i, v in enumerate(args)]

    def run(*refs):
        body(*refs[:count], *refs[count + len(deps) :])

    return pl.pallas_call(
        run,
        out_shape=list(outs),
        in_specs=[pl.BlockSpec(memory_space=space(i)) for i in range(count)]
        + [pl.BlockSpec(memory_space=pl.ANY) for _ in deps],
        out_specs=[pl.BlockSpec(memory_space=VM) for _ in outs],
        scratch_shapes=list(scratch),
        compiler_params=pltpu.CompilerParams(vmem_limit_bytes=own + int(extra * MIB)),
        cost_estimate=pl.CostEstimate(flops=MAIN, bytes_accessed=0, transcendentals=0),
        name=name,
    )(*args, *deps)


def out(shape, dtype):
    return jax.ShapeDtypeStruct(shape, dtype)


class Line:
    def __init__(self):
        self.mark = None

    def call(self, body, outs, args, deps=(), **kw):
        made = kernel_call(body, outs, args, deps=(self.mark, *deps), **kw)
        self.mark = min(made, key=nbytes)
        return made


def dot(a, b):
    return jnp.dot(a, b, preferred_element_type=F32)


def dot_tn(a, b):
    return lax.dot_general(a, b, (((0,), (0,)), ((), ())), preferred_element_type=F32)


def dot_nt(a, b):
    return lax.dot_general(a, b, (((1,), (1,)), ((), ())), preferred_element_type=F32)


def loop(count, step):
    lax.fori_loop(0, count, lambda i, z: (step(i), z)[1], 0)


def span(i, size):
    return pl.ds(pl.multiple_of(i * size, size), size)


def normalized(values):
    center = values - jnp.mean(values, axis=-1, keepdims=True)
    spread = jnp.mean(center * center, axis=-1, keepdims=True)
    factor = lax.rsqrt(spread + EPS)
    return center * factor, factor


class Ring:
    def __init__(self, mesh):
        self.axes = ("rep", "fsdp")
        self.n = mesh.shape["fsdp"]
        self.reps = mesh.shape["rep"]
        n = self.n
        self.order = list(range(0, n, 2)) + list(range(n - 1, 0, -2))
        self.place = [self.order.index(f) for f in range(n)]
        self.half = n // 2

    def send(self, v, target, keep=lambda r, f: True):
        n = self.n
        pairs = []
        for r in range(self.reps):
            for f in range(n):
                if keep(r, f):
                    r2, f2 = target(r, f)
                    pairs.append((r * n + f, r2 * n + f2))
        return lax.ppermute(v, self.axes, pairs)

    def along(self, v):
        def target(r, f):
            step = 1 if r % 2 == 0 else -1
            return r, self.order[(self.place[f] + step) % self.n]

        return self.send(v, target)

    def core(self, v):
        return self.send(v, lambda r, f: (r ^ 1, f))

    def across(self, v, keep=lambda r, f: True):
        return self.send(v, lambda r, f: (r ^ 2, f), keep)

    def here(self):
        r = lax.axis_index("rep")
        return r % 2, (r // 2) % 2, lax.axis_index("fsdp")

    def own_place(self):
        n, (c, _, f) = self.n, self.here()
        return jnp.where(f % 2 == 0, f // 2, n - 1 - f // 2), 1 - 2 * c

    def shard_back(self, h):
        n, (p, d) = self.n, self.own_place()
        q = lax.rem(p - d * h + 2 * n, n)
        return jnp.where(q < n // 2, 2 * q, 2 * (n - 1 - q) + 1)

    def slot(self, j):
        n, (p, d) = self.n, self.own_place()
        return lax.rem((self.place[j] - p) * d + n, n)


def cut_kernel(ring, a, v, ext, *more):
    ext[...] = v[0:a, :]
    if more:
        (rest,) = more
        if rest.shape == v.shape:
            rest[...] = v[...]
        else:
            rest[...] = v[pl.ds(pl.multiple_of(ring.here()[0] * a, 16), rest.shape[0]), :]


def gather(ring, firsts, a, extras):
    m = ring.half
    b, width = firsts[0].shape[0] - a, firsts[0].shape[1]
    groups = [dict(ring=[], out=[], pring=[], pout=[], due=[]) for _ in firsts]
    for h in range(1, m + 2):
        for i, g in enumerate(groups):
            if h == 1:
                g["ring"].append(ring.along(firsts[i]))
                continue
            v = g["ring"][-1]
            shapes = [out((a, width), BF)]
            if h <= m:
                shapes.append(out(v.shape if h < m else (b, width), BF))
            ext, *rest = kernel_call(functools.partial(cut_kernel, ring, a), shapes, [v], deps=g["due"], name="cut")
            if rest:
                g["ring"].append(ring.along(rest[0]))
            even = (lambda r, f: r % 2 == 0) if h > m else (lambda r, f: True)
            g["due"] = [ring.across(ext, even), ring.core(v)]
            if h > 2:
                g["pout"].append(ring.core(g["out"][-1]))
                g["due"].append(g["pout"][-1])
            g["out"].append(g["due"][0])
            g["pring"].append(g["due"][1])
            more = extras.send(ext)
            if more is not None:
                g["due"].append(more)
    for g in groups:
        g["pout"].append(ring.core(g["out"][-1]))
    return groups


def flat(own, opp, g):
    return [own, opp, *g["ring"], *g["pring"], *g["out"], *g["pout"]]


def place_parts(ring, a, refs, put):
    n, m = ring.n, ring.half
    own, opp, refs = refs[0], refs[1], refs[2:]
    rings, prings, outs, pouts = (refs[i * m : (i + 1) * m] for i in range(4))

    def all_parts(step, ext, mid, mid0, other):
        s = ring.shard_back(step)
        put("mid", s, mid, mid0)
        put("ext", s, ext, 0)
        put("opp", s, other, 0)

    all_parts(0, own, own, a, opp)
    for h in range(1, m):
        all_parts(h, rings[h - 1], rings[h - 1], a, outs[h - 1])
        all_parts(n - h, prings[h - 1], prings[h - 1], a, pouts[h - 1])

    c = ring.here()[0]

    @pl.when(c == 0)
    def _():
        all_parts(m, rings[-1], prings[-1], 0, outs[-1])

    @pl.when(c == 1)
    def _():
        all_parts(m, prings[-1], rings[-1], 0, pouts[-1])


def ln_rows(x_ref, gain, bias, o_ref, rows=384):
    def step(i):
        at = span(i, rows)
        n, _ = normalized(x_ref[at, :].astype(F32))
        o_ref[at, :] = (n * gain + bias).astype(BF)

    loop(x_ref.shape[0] // rows, step)


def split_kernel(ring, t, jw, ow, first, opp, sems):
    width = ow.shape[1]
    rps = ow.shape[0]
    a = rps + t
    x = ring.here()[1]
    made = []

    def copy(src, dst):
        c = pltpu.make_async_copy(src, dst, sems.at[len(made)])
        c.start()
        made.append(c)

    def cols(side):
        return jw.at[:, pl.ds(pl.multiple_of(side * 2 * width, width), width)]

    copy(cols(x), first.at[pl.ds(0, rps), :])
    copy(jw.at[:, pl.ds(width, width)], first.at[pl.ds(a, rps), :])
    copy(ow.at[pl.ds(t, rps - 2 * t), :], first.at[pl.ds(a + rps, rps - 2 * t), :])
    copy(cols(1 - x), opp.at[pl.ds(0, rps), :])
    if t:
        copy(ow.at[pl.ds(pl.multiple_of(x * (rps - t), 16), t), :], first.at[pl.ds(rps, t), :])
        copy(ow.at[pl.ds(pl.multiple_of((1 - x) * (rps - t), 16), t), :], opp.at[pl.ds(rps, t), :])
    for c in made:
        c.wait()


def split_ff_kernel(ring, t, uw, dw, first, opp, sems):
    width = dw.shape[1]
    rps = uw.shape[0]
    a = rps + t
    x = ring.here()[1]
    made = []

    def copy(src, dst):
        c = pltpu.make_async_copy(src, dst, sems.at[len(made)])
        c.start()
        made.append(c)

    def cols(side):
        return uw.at[:, pl.ds(pl.multiple_of(side * width, width), width)]

    copy(cols(x), first.at[pl.ds(0, rps), :])
    copy(dw.at[pl.ds(t, 2 * rps - 2 * t), :], first.at[pl.ds(a, 2 * rps - 2 * t), :])
    copy(cols(1 - x), opp.at[pl.ds(0, rps), :])
    if t:
        copy(dw.at[pl.ds(pl.multiple_of(x * (2 * rps - t), 16), t), :], first.at[pl.ds(rps, t), :])
        copy(dw.at[pl.ds(pl.multiple_of((1 - x) * (2 * rps - t), 16), t), :], opp.at[pl.ds(rps, t), :])
    for c in made:
        c.wait()


def small_kernel(ring, *refs):
    parts, o_ref = refs[:-1], refs[-1]
    width = o_ref.shape[1]
    n, f = ring.n, ring.here()[2]
    row = 0
    o_ref[...] = jnp.zeros_like(o_ref)
    for part in parts:
        size = part.shape[0]
        full = size * n
        i = lax.broadcasted_iota(jnp.int32, (size, full), 0)
        j = lax.broadcasted_iota(jnp.int32, (size, full), 1)
        hot = jnp.where(j == i + f * size, 1.0, 0.0).astype(BF)
        placed = dot(jnp.broadcast_to(part[...].astype(F32)[None, :], (8, size)).astype(BF), hot)
        for k in range(full // width):
            o_ref[row : row + 1, :] = placed[0:1, k * width : (k + 1) * width]
            row += 1


def add_f32_kernel(a_ref, b_ref, o_ref):
    o_ref[...] = a_ref[...] + b_ref[...]


def own_small_kernel(ring, vec, *outs):
    n, f = ring.n, ring.here()[2]
    width = vec.shape[1]
    row = 0
    for o in outs:
        size = o.shape[1]
        count = size * n // width
        got = jnp.zeros((1, size), F32)
        for k in range(count):
            for j in range(width // size):
                part = vec[row + k : row + k + 1, j * size : (j + 1) * size]
                got = got + part * jnp.where(f == k * (width // size) + j, 1.0, 0.0)
        o[...] = got
        row += count


def ln_kernel(x_ref, small, o_ref):
    ln_rows(x_ref, small[pl.ds(GAIN1, 1), :], small[pl.ds(BIAS1, 1), :], o_ref)


def qkv_kernel(ring, a, t, first, small, *refs):
    refs, outs = refs[:-5], refs[-5:]
    proj, ws, wo = outs[:2], outs[2:4], outs[4]
    width = first.shape[1]
    rps = width // ring.n
    hw = width // 2
    xb = ring.here()[1]

    def put(part, s, ref, r0):
        row = pl.multiple_of(s * rps, rps)
        if part == "mid":
            for k in range(2):
                ws[k][pl.ds(row, rps), hw : 2 * hw] = ref[r0 : r0 + rps, k * hw : (k + 1) * hw]
            wo[pl.ds(pl.multiple_of(row + t, 16), rps - 2 * t), :] = ref[r0 + rps : r0 + 2 * rps - 2 * t, :]
        else:
            side = xb if part == "ext" else 1 - xb
            col = pl.multiple_of(side * 2 * hw, hw)
            for k in range(2):
                ws[k][pl.ds(row, rps), pl.ds(col, hw)] = ref[0:rps, k * hw : (k + 1) * hw]
            if t:
                wo[pl.ds(pl.multiple_of(row + side * (rps - t), 16), t), :] = ref[rps : rps + t, :]

    place_parts(ring, a, refs, put)
    for k in range(2):

        def tile(i, k=k):
            at = span(i, hw)
            v = dot(first[...], ws[k][:, at])
            use = jnp.where(i == 0, 1.0, 0.0), jnp.where(i == 2, 1.0, 0.0)
            shift = small[pl.ds(JB_Q, 1), k * hw : (k + 1) * hw] * use[0]
            shift = shift + small[pl.ds(JB_V, 1), k * hw : (k + 1) * hw] * use[1]
            proj[k][:, at] = (v + shift).astype(BF)

        loop(3, tile)


def mask(col_ids, row_ids, q0, k0, queries, keys):
    same = col_ids[k0 : k0 + keys, :] == row_ids[:, q0 : q0 + queries]
    kpos = lax.broadcasted_iota(jnp.int32, (keys, queries), 0) + k0
    qpos = lax.broadcasted_iota(jnp.int32, (keys, queries), 1) + q0
    return jnp.where(same & (kpos <= qpos), 0.0, MASKED).astype(F32)


def soft(q, k, bias):
    s = dot_nt(k, q) * (HD ** (-0.5) * LOG2E) + bias
    p = jnp.exp2(s - jnp.max(s, axis=0, keepdims=True))
    return p * (1.0 / jnp.sum(p, axis=0, keepdims=True))


def head_cols(part, h):
    return slice((part * HALF + h) * HD, (part * HALF + h + 1) * HD)


def tiles(rows, queries, back):
    for q0 in range(0, rows, queries):
        lo = min(q0, back)
        yield q0, q0 - lo, queries + lo


def attend_kernel(proj_a, proj_b, col_ids, row_ids, o_ref):
    nq = 256
    for q0, k0, nk in tiles(o_ref.shape[0], nq, 128):
        at_q, at_k = slice(q0, q0 + nq), slice(k0, k0 + nk)
        bias = mask(col_ids, row_ids, q0, k0, nq, nk)
        for k, proj in enumerate((proj_a, proj_b)):
            for h in range(HALF):
                w = soft(proj[at_q, head_cols(0, h)], proj[at_k, head_cols(1, h)], bias).astype(BF)
                col = (k * HALF + h) * HD
                o_ref[at_q, col : col + HD] = dot_tn(w, proj[at_k, head_cols(2, h)]).astype(BF)


def out_kernel(att, wo, x_ref, small, middle, second):
    tn = 512

    def step(i):
        at = span(i, tn)
        middle[:, at] = x_ref[:, at].astype(F32) + dot(att[...], wo[:, at]) + small[pl.ds(OUT_B, 1), at]

    loop(wo.shape[1] // tn, step)
    ln_rows(middle, small[pl.ds(GAIN2, 1), :], small[pl.ds(BIAS2, 1), :], second)


def gelu_both(h):
    h2 = h * h
    half = 0.5 + 0.5 * jnp.tanh(h * (C0 + (C0 * 0.044715) * h2))
    act = h * half
    return act, half + act * (1.0 - half) * (2.0 * C0 + (6.0 * C0 * 0.044715) * h2)


def up_kernel(ring, a, t, second, small, *refs):
    refs, outs = refs[:-4], refs[-4:]
    active, slope, wu, wd = outs
    width = second.shape[1]
    rps = width // ring.n
    xb = ring.here()[1]

    def put(part, s, ref, r0):
        row = pl.multiple_of(s * rps, rps)
        drow = pl.multiple_of(s * 2 * rps, 2 * rps)
        if part == "mid":
            wd[pl.ds(pl.multiple_of(drow + t, 16), 2 * rps - 2 * t), :] = ref[r0 : r0 + 2 * rps - 2 * t, :]
        else:
            side = xb if part == "ext" else 1 - xb
            wu[pl.ds(row, rps), pl.ds(pl.multiple_of(side * width, width), width)] = ref[0:rps, :]
            if t:
                wd[pl.ds(pl.multiple_of(drow + side * (2 * rps - t), 16), t), :] = ref[rps : rps + t, :]

    place_parts(ring, a, refs, put)
    tn = 512
    per = width // tn

    def step(i):
        at = span(i, tn)
        shift = small[pl.ds(UP_B + i // per, 1), span(i % per, tn)]
        act, s = gelu_both(dot(second[...], wu[:, at]) + shift)
        active[:, at] = act.astype(BF)
        slope[:, at] = s.astype(BF)

    loop(2 * per, step)


def dact_kernel(og, wd, slope, o_ref):
    tn = 256

    def step(i):
        at = span(i, tn)
        o_ref[:, at] = (dot_nt(og[...], wd[at, :]) * slope[:, at].astype(F32)).astype(BF)

    loop(o_ref.shape[1] // tn, step)


def down_kernel(active, wd, middle, small, o_ref):
    tn = 512

    def step(i):
        at = span(i, tn)
        o_ref[:, at] = (middle[:, at] + dot(active[...], wd[:, at]) + small[pl.ds(DOWN_B, 1), at]).astype(BF)

    loop(o_ref.shape[1] // tn, step)


def weight_grad_kernel(ring, tn, tl, left, right, buf, sent, sums):
    n, m = ring.n, ring.half
    half = left.shape[1] // n // 2
    slots = [ring.slot(j) for j in range(n)]
    swap = [jnp.where(k == m, ring.here()[0], 0) for k in slots]
    ones = jnp.ones((8, right.shape[0]), BF)
    per = tl // half

    def step(i):
        at = span(i, tn)
        r = right[:, at]
        sums[:, at] = dot(ones, r)
        for l in range(left.shape[1] // tl):
            v = dot_tn(left[:, l * tl : (l + 1) * tl], r).astype(BF)
            for s in range(per):
                j, q = divmod(l * per + s, 2)
                row = pl.multiple_of((2 * slots[j] + (swap[j] + q) % 2) * half, half)
                buf[pl.ds(row, half), at] = v[s * half : (s + 1) * half, :]
        sent[:, at] = buf[buf.shape[0] - sent.shape[0] :, at]

    loop(right.shape[1] // tn, step)


def norm_back(values, d, gain):
    n, r = normalized(values)
    g = d * gain
    t = r * (g - jnp.mean(g, axis=-1, keepdims=True) - n * jnp.mean(g * n, axis=-1, keepdims=True))
    return t, d * n


def group_sum(v):
    return jnp.sum(v.reshape(v.shape[0] // 8, 8, v.shape[1]), axis=0)


def dsecond_kernel(dh, wu, acc):
    tn = 256

    def step(i):
        at = span(i, tn)
        acc[:, at] = dot_nt(dh[...], wu[at, :])

    loop(acc.shape[1] // tn, step)


def second_norm_back_kernel(acc, wo, middle, og, small, dmid, dbranch, datt, sg, sb):
    g = small[pl.ds(GAIN2, 1), :]
    sg[...] = jnp.zeros_like(sg)
    sb[...] = jnp.zeros_like(sb)
    rows = 256

    def norm(i):
        at = span(i, rows)
        d = acc[at, :]
        t, dn = norm_back(middle[at, :], d, g)
        sg[...] += group_sum(dn)
        sb[...] += group_sum(d)
        v = og[at, :].astype(F32) + t
        dmid[at, :] = v
        dbranch[at, :] = v.astype(BF)

    loop(acc.shape[0] // rows, norm)
    tn = 256

    def back(i):
        at = span(i, tn)
        datt[:, at] = dot_nt(dbranch[...], wo[at, :]).astype(BF)

    loop(datt.shape[1] // tn, back)


def attend_back_kernel(part, proj, datt, col_ids, row_ids, o_ref, acc_k, acc_v):
    rows, hw = acc_k.shape
    scale = HD ** (-0.5)
    nq = 128
    heads = range(HALF)
    acc_k[...] = jnp.zeros_like(acc_k)
    acc_v[...] = jnp.zeros_like(acc_v)
    for q0, k0, nk in tiles(rows, nq, 64):
        at_q, at_k = slice(q0, q0 + nq), slice(k0, k0 + nk)
        bias = mask(col_ids, row_ids, q0, k0, nq, nk)
        q = [proj[at_q, head_cols(0, h)] for h in heads]
        k = [proj[at_k, head_cols(1, h)] for h in heads]
        do = [datt[at_q, head_cols(part, h)] for h in heads]
        dw = [dot_nt(proj[at_k, head_cols(2, h)], do[h]) for h in heads]
        p = [soft(q[h], k[h], bias) for h in heads]
        for h in heads:
            acc_v[at_k, head_cols(0, h)] += dot(p[h].astype(BF), do[h])
        ds = [(p[h] * (dw[h] - jnp.sum(p[h] * dw[h], axis=0, keepdims=True))).astype(BF) for h in heads]
        for h in heads:
            acc_k[at_k, head_cols(0, h)] += dot(ds[h], q[h])
            o_ref[at_q, head_cols(0, h)] = (dot_tn(ds[h], k[h]) * scale).astype(BF)
    o_ref[:, hw : 2 * hw] = (acc_k[...] * scale).astype(BF)
    o_ref[:, 2 * hw :] = acc_v[...].astype(BF)


def dfirst_kernel(da, db, wa, wb, acc):
    tn = 512

    def step(i):
        at = span(i, tn)
        acc[:, at] = dot_nt(da[...], wa[at, :]) + dot_nt(db[...], wb[at, :])

    loop(acc.shape[1] // tn, step)


def first_norm_back_kernel(acc, x_ref, dmid, small, o_ref, sg, sb):
    g = small[pl.ds(GAIN1, 1), :]
    sg[...] = jnp.zeros_like(sg)
    sb[...] = jnp.zeros_like(sb)
    rows = 256

    def norm(i):
        at = span(i, rows)
        d = acc[at, :]
        t, dn = norm_back(x_ref[at, :].astype(F32), d, g)
        sg[...] += group_sum(dn)
        sb[...] += group_sum(d)
        o_ref[at, :] = (dmid[at, :] + t).astype(BF)

    loop(x_ref.shape[0] // rows, norm)


def gather_small_kernel(sg1, sb1, ja, jb, so, sg2, sb2, su, sd, o_ref):
    hw = ja.shape[1] // 3
    o_ref[...] = jnp.zeros_like(o_ref)

    def put(row, v):
        o_ref[row : row + 1, :] = v

    put(GAIN1, jnp.sum(sg1[...], axis=0, keepdims=True))
    put(BIAS1, jnp.sum(sb1[...], axis=0, keepdims=True))
    for k, s in enumerate((ja, jb)):
        o_ref[JB_Q : JB_Q + 1, k * hw : (k + 1) * hw] = s[0:1, 0:hw]
        o_ref[JB_V : JB_V + 1, k * hw : (k + 1) * hw] = s[0:1, 2 * hw :]
    put(OUT_B, so[0:1, :])
    put(GAIN2, jnp.sum(sg2[...], axis=0, keepdims=True))
    put(BIAS2, jnp.sum(sb2[...], axis=0, keepdims=True))
    for k in range(2):
        put(UP_B + k, su[0:1, k * 2 * hw : (k + 1) * 2 * hw])
    put(DOWN_B, sd[0:1, :])


class Grads:
    def __init__(self, n, bufs, recvs, width):
        self.bufs, self.recvs, self.width = bufs, recvs, width
        self.sizes = [(b.shape[0] // n, b.shape[1] // width) for b in bufs]
        self.rows = sum(r * c for r, c in self.sizes)


def reduce_step(ring, gr, k, got):
    m, n = ring.half, ring.n
    width = gr.width
    half = k == m
    total = gr.rows // 2 if half else gr.rows
    args = [*gr.bufs, *gr.recvs] + ([got] if got is not None else [])
    nb = len(gr.bufs)

    def body(*refs):
        bs, rs = refs[:nb], refs[nb : 2 * nb]
        g = refs[2 * nb] if got is not None else None
        o = refs[-1]
        c = ring.here()[0]
        at, gat = 0, 0
        for b, rv, (r, cs) in zip(bs, rs, gr.sizes):
            h = r // 2
            for j in range(cs):
                col = slice(j * width, (j + 1) * width)
                if half:
                    v = b[m * r : m * r + h, col].astype(F32) + rv[0:h, col].astype(F32)
                    o[at : at + h, :] = v.astype(BF)
                    at += h
                else:
                    base = h + (n - k - m - 1) * r
                    v = b[k * r : (k + 1) * r, col].astype(F32) + rv[base : base + r, col].astype(F32)
                    if g.shape[0] == total:
                        o[at : at + r, :] = (v + g[at : at + r, :].astype(F32)).astype(BF)
                    else:
                        top = jnp.where(c == 0, 1.0, 0.0)
                        gv = g[gat : gat + h, :].astype(F32)
                        o[at : at + h, :] = (v[:h] + gv * top).astype(BF)
                        o[at + h : at + r, :] = (v[h:] + gv * (1.0 - top)).astype(BF)
                        gat += h
                    at += r

    return body, [out((total, width), BF)], args


def owner_sum(ring, gr, got):
    nb = len(gr.bufs)

    def body(*refs):
        bs, g, keep, send = refs[:nb], refs[nb], refs[nb + 1], refs[nb + 2]
        c = ring.here()[0]
        at, to = 0, 0
        for b, (r, cs) in zip(bs, gr.sizes):
            h = r // 2
            for j in range(cs):
                v = b[0:r, j * gr.width : (j + 1) * gr.width].astype(F32) + g[at : at + r, :].astype(F32)
                v = v.astype(BF)
                keep[to : to + h, :] = jnp.where(c == 0, v[:h], v[h:])
                send[to : to + h, :] = jnp.where(c == 0, v[h:], v[:h])
                at += r
                to += h

    o = out((gr.rows // 2, gr.width), BF)
    return body, [o, o], [*gr.bufs, got]


def add_kernel(a_ref, b_ref, o_ref):
    o_ref[...] = (a_ref[...].astype(F32) + b_ref[...].astype(F32)).astype(o_ref.dtype)


def add2(a, b):
    return add_kernel, [out(a.shape, a.dtype)], [a, b]


def reduce_group(ring, gr):
    got = None
    for k in range(ring.half, 0, -1):
        (part,) = yield reduce_step(ring, gr, k, got)
        got = ring.along(part)
    keep, send = yield owner_sum(ring, gr, got)
    (u,) = yield add2(keep, ring.core(send))
    bit = 2
    while bit < ring.reps:
        (u,) = yield add2(u, ring.send(u, lambda r, f, bit=bit: (r ^ bit, f)))
        bit *= 2
    return u, ring.core(u)


class Rounds:
    def __init__(self, line):
        self.line = line
        self.live = {}
        self.jobs = {}
        self.done = {}

    def _advance(self, name, results):
        try:
            self.jobs[name] = next(self.live[name]) if results is None else self.live[name].send(results)
        except StopIteration as stop:
            self.done[name] = stop.value
            del self.live[name]
            self.jobs.pop(name, None)

    def add(self, name, chain):
        self.live[name] = chain
        self._advance(name, None)

    def turn(self, *names):
        names = [k for k in names or self.jobs if k in self.jobs]
        if not names:
            return
        jobs = [self.jobs[k] for k in names]
        args = [a for _, _, given in jobs for a in given]
        outs = [o for _, made, _ in jobs for o in made]

        def body(*refs):
            i, j = 0, len(args)
            for run, made, given in jobs:
                run(*refs[i : i + len(given)], *refs[j : j + len(made)])
                i, j = i + len(given), j + len(made)

        got = list(self.line.call(body, outs, args, name="sums"))
        for name, (_, made, _) in zip(names, jobs):
            self._advance(name, got[: len(made)])
            got = got[len(made) :]


def join_halves(c, parts, sizes, width, place):
    a_ref, b_ref = parts
    to = 0
    for i, (r, cs) in enumerate(sizes):
        h = r // 2
        for j in range(cs):
            a = a_ref[to : to + h, :].astype(F32)
            b = b_ref[to : to + h, :].astype(F32)
            place(i, slice(0, h), j, jnp.where(c == 0, a, b))
            place(i, slice(h, r), j, jnp.where(c == 0, b, a))
            to += h


def last_sum(job):
    return (yield job)


def finish(ring, gr, parts):
    def body(a_ref, b_ref, *outs):
        def place(i, rows, j, v):
            outs[i][rows, j * gr.width : (j + 1) * gr.width] = v

        join_halves(ring.here()[0], (a_ref, b_ref), gr.sizes, gr.width, place)

    return body, [out((r, cs * gr.width), F32) for r, cs in gr.sizes], list(parts)


def finish_joint(ring, gr, parts_a, parts_b):
    (r, cs), width = gr.sizes[0], gr.width
    _, ocs = gr.sizes[1]

    def body(a1, a2, b1, b2, o, o2):
        for k, pair in enumerate(((a1, a2), (b1, b2))):
            def place(i, rows, j, v, k=k):
                if i == 0:
                    at = (2 * j + k) * width
                    o[rows, at : at + width] = v
                else:
                    o2[rows, j * width : (j + 1) * width] = v

            join_halves(ring.here()[0], pair, gr.sizes[: 2 - k], width, place)

    return body, [out((r, 2 * cs * width), F32), out((r, ocs * width), F32)], [*parts_a, *parts_b]


def step_fn(mesh):
    ring = Ring(mesh)
    n, m = ring.n, ring.half

    def on_device(
        layer_input, item_ids, norm_gain, norm_bias, joint_weight, joint_bias, out_weight, out_bias,
        second_gain, second_bias, up_weight, up_bias, down_weight, down_bias, output_grad,
    ):
        rows, width = layer_input.shape
        ff = up_weight.shape[1]
        hw = width // 2
        rps = width // n
        t = (rps // 4) // 16 * 16
        a, b = rps + t, 2 * rps - 2 * t
        dma = pltpu.SemaphoreType.DMA
        shapes = [out((a + b, width), BF), out((a, width), BF)]
        line = Line()
        first1, opp1 = line.call(
            functools.partial(split_kernel, ring, t), shapes, [joint_weight, out_weight],
            far=(0, 1), scratch=[dma((6,))], name="split",
        )
        ids = [item_ids[:, None], item_ids[None, :]]
        first2, opp2 = line.call(
            functools.partial(split_ff_kernel, ring, t), shapes, [up_weight, down_weight], deps=ids,
            far=(0, 1), scratch=[dma((5,))], name="split_ff",
        )
        vectors = (norm_gain, norm_bias, joint_bias, out_bias, second_gain, second_bias, up_bias, down_bias)
        shared = {}

        def small_parts():
            (small,) = line.call(
                functools.partial(small_kernel, ring), [out((SMALL_ROWS, width), F32)], vectors, name="small",
            )
            mark = yield
            bit = 1
            while bit < n:
                other = ring.send(small, lambda r, f, bit=bit: (r, f ^ bit))
                yield (small if bit > 1 else None)
                mark = yield
                (small,) = kernel_call(add_f32_kernel, [out(small.shape, F32)], [small, other], deps=[mark], name="small_sum")
                bit *= 2
            shared["small"] = small
            (shared["first"],) = kernel_call(
                ln_kernel, [out((rows, width), BF)], [layer_input, small], deps=[mark], name="first_norm",
            )
            mark = yield shared["first"]
            while True:
                yield

        extras = small_parts()
        next(extras)
        g1, g2 = gather(ring, [first1, first2], a, extras)
        small, first = shared["small"], shared["first"]

        args = [first, small, *flat(first1, opp1, g1)]
        halves = [out((rows, 3 * hw), BF)] * 2
        proj_a, proj_b, wa, wb, wo = line.call(
            functools.partial(qkv_kernel, ring, a, t),
            halves + [out((width, 3 * hw), BF)] * 2 + [out((width, width), BF)],
            args, name="projection",
        )
        (attended,) = line.call(attend_kernel, [out((rows, width), BF)], [proj_a, proj_b, *ids], name="attend")
        middle, second = line.call(
            out_kernel, [out((rows, width), F32), out((rows, width), BF)],
            [attended, wo, layer_input, small], name="out_projection",
        )
        args = [second, small, *flat(first2, opp2, g2)]
        active, slope, wu, wd = line.call(
            functools.partial(up_kernel, ring, a, t),
            [out((rows, ff), BF), out((rows, ff), BF), out((width, ff), BF), out((ff, width), BF)],
            args, name="up_projection",
        )

        def weight_grad(l, r, tl=512, tn=512, name=None):
            kl, kr = l.shape[1], r.shape[1]
            kept = m * (kl // n) + kl // n // 2
            buf, sent, sums = line.call(
                functools.partial(weight_grad_kernel, ring, tn, tl),
                [out((kl, kr), BF), out((kl - kept, kr), BF), out((8, kr), F32)], [l, r], name=name,
            )
            return buf, ring.core(sent), sums

        rounds = Rounds(line)

        def begin(name, bufs, recvs, w):
            gr = Grads(n, bufs, recvs, w)
            rounds.add(name, reduce_group(ring, gr))
            return gr

        down_buf, down_recv, s_down = weight_grad(active, output_grad, name="down_grad")
        (dhidden,) = line.call(
            dact_kernel, [out((rows, ff), BF)], [output_grad, wd, slope], name="hidden_grad",
        )
        gr_down = begin("down", [down_buf], [down_recv], width)
        rounds.turn("down")
        up_buf, up_recv, s_up = weight_grad(second, dhidden, name="up_grad")
        rounds.turn("down")
        (dsecond,) = line.call(dsecond_kernel, [out((rows, width), F32)], [dhidden, wu], name="dsecond")
        gr_up = begin("up", [up_buf], [up_recv], width)
        rounds.turn("up")
        dmid, dbranch, datt, sg2, sb2 = line.call(
            second_norm_back_kernel,
            [out((rows, width), F32), out((rows, width), BF), out((rows, width), BF), out((8, width), F32), out((8, width), F32)],
            [dsecond, wo, middle, output_grad, small], name="second_norm_grad",
        )
        rounds.turn("down")
        out_buf, out_recv, s_out = weight_grad(attended, dbranch, name="out_grad")
        rounds.turn("up")

        def attend_back(part, proj):
            return line.call(
                functools.partial(attend_back_kernel, part), [out((rows, 3 * hw), BF)], [proj, datt, *ids],
                scratch=[VM((rows, hw), F32), VM((rows, hw), F32)], name="attend_grad",
            )[0]

        da = attend_back(0, proj_a)
        rounds.turn("down")
        ja_buf, ja_recv, s_ja = weight_grad(first, da, name="joint_grad")
        rounds.turn("up")
        db = attend_back(1, proj_b)
        gr_ja = begin("ja", [ja_buf, out_buf], [ja_recv, out_recv], hw)
        rounds.turn("ja", "down")
        jb_buf, jb_recv, s_jb = weight_grad(first, db, name="joint_grad")
        rounds.turn("up")
        (dfirst,) = line.call(dfirst_kernel, [out((rows, width), F32)], [da, db, wa, wb], name="dfirst")
        gr_jb = begin("jb", [jb_buf], [jb_recv], hw)
        rounds.turn("ja")
        rounds.turn("jb", "down")
        input_grad, sg1, sb1 = line.call(
            first_norm_back_kernel, [out((rows, width), BF), out((8, width), F32), out((8, width), F32)],
            [dfirst, layer_input, dmid, small], name="first_norm_grad",
        )

        def small_grads():
            partial = [sg1, sb1, s_ja, s_jb, s_out, sg2, sb2, s_up, s_down]
            (vec,) = yield gather_small_kernel, [out((SMALL_ROWS, width), F32)], partial
            for axis, count in ((1, n), (0, ring.reps)):
                bit = 1
                while bit < count:
                    def target(r, f, bit=bit, axis=axis):
                        return (r, f ^ bit) if axis else (r ^ bit, f)

                    (vec,) = yield add2(vec, ring.send(vec, target))
                    bit *= 2
            outs = [out((1, v.shape[0]), F32) for v in vectors]
            return (yield functools.partial(own_small_kernel, ring), outs, [vec])

        rounds.add("small", small_grads())
        rounds.turn("ja", "small")
        rounds.turn("jb", "up")
        (layer_output,) = line.call(
            down_kernel, [out((rows, width), BF)], [active, wd, middle, small], name="down_projection",
        )
        done, ready = rounds.done, set()
        pairs = ("ja", "down", "got down"), ("jb", "up", "small", "got up")
        k = 0
        while rounds.jobs:
            rounds.turn(*(pairs[k % 2] if "ja" in rounds.jobs or "jb" in rounds.jobs else ()))
            k += 1
            for name, gr in (("down", gr_down), ("up", gr_up)):
                if name in done and name not in ready:
                    ready.add(name)
                    rounds.add("got " + name, last_sum(finish(ring, gr, done[name])))
            if "ja" in done and "jb" in done and "joint" not in ready:
                ready.add("joint")
                rounds.add("got joint", last_sum(finish_joint(ring, gr_ja, done["ja"], done["jb"])))
        (g_down,), (g_up,), (g_joint, g_out) = (done["got " + k] for k in ("down", "up", "joint"))
        v = [v.reshape(-1) for v in done["small"]]
        return (
            layer_output, input_grad, v[0], v[1], g_joint, v[2], g_out, v[3], v[4], v[5], g_up, v[6], g_down, v[7],
        )

    return on_device


def solution(mesh):
    row, vecs, mat = P(("rep", "fsdp"), None), P("fsdp"), P("fsdp", None)
    placed = (
        row, P(("rep", "fsdp")), vecs, vecs, mat, vecs, mat, vecs, vecs, vecs, mat, vecs, mat, vecs, row,
    )
    return jax.shard_map(
        step_fn(mesh),
        mesh=mesh,
        in_specs=placed,
        out_specs=(row, row, vecs, vecs, mat, vecs, mat, vecs, vecs, vecs, mat, vecs, mat, vecs),
        check_vma=False,
    )
```

```python
import functools
import math

import jax
import jax.numpy as jnp
from jax import lax
from jax.experimental import pallas as pl
from jax.experimental.pallas import tpu as pltpu
from jax.sharding import PartitionSpec as P

H = 8
HD = 128
HALF = H // 2
EPS = 1e-05
MASKED = -1e30
LOG2E = 1.4426950408889634
C0 = math.sqrt(2.0 / math.pi)
BF = jnp.bfloat16
F32 = jnp.float32
VM = pltpu.VMEM
MAIN = 60 * 10**9
MIB = 2**20

GAIN1, BIAS1, JB_Q, JB_V, OUT_B, GAIN2, BIAS2, UP_B, DOWN_B = 0, 1, 2, 3, 4, 5, 6, 7, 9
SMALL_ROWS = 16
SMALL_SHARD, SMALL_COL = 32, 256


def nbytes(a):
    return math.prod(a.shape) * jnp.dtype(a.dtype).itemsize


def kernel_call(body, outs, args, deps=(), smem=(), anys=(), far=(), scratch=(), extra=4, long=True, name=None):
    own = sum(nbytes(s) for s in scratch if getattr(s, "dtype", None) in (BF, F32))
    count, made = len(args), len(outs)
    deps = [d for d in deps if d is not None]

    def space(i):
        return pl.ANY if i in anys else pltpu.HBM if i in far else pltpu.SMEM if i in smem else VM

    args = [pltpu.with_memory_space_constraint(v, pltpu.HBM) if i in far else v for i, v in enumerate(args)]

    def run(*refs):
        body(*refs[:count], *refs[count + len(deps) :])

    return pl.pallas_call(
        run,
        out_shape=list(outs),
        in_specs=[pl.BlockSpec(memory_space=space(i)) for i in range(count)]
        + [pl.BlockSpec(memory_space=pl.ANY) for _ in deps],
        out_specs=[pl.BlockSpec(memory_space=VM) for _ in outs],
        scratch_shapes=list(scratch),
        compiler_params=pltpu.CompilerParams(vmem_limit_bytes=own + int(extra * MIB)),
        cost_estimate=pl.CostEstimate(flops=MAIN if long else 0, bytes_accessed=0, transcendentals=0),
        name=name,
    )(*args, *deps)


def out(shape, dtype):
    return jax.ShapeDtypeStruct(shape, dtype)


class Line:
    def __init__(self):
        self.mark = None

    def call(self, body, outs, args, deps=(), **kw):
        made = kernel_call(body, outs, args, deps=(self.mark, *deps), **kw)
        self.mark = min(made, key=nbytes)
        return made


def dot(a, b):
    return jnp.dot(a, b, preferred_element_type=F32)


def dot_tn(a, b):
    return lax.dot_general(a, b, (((0,), (0,)), ((), ())), preferred_element_type=F32)


def dot_nt(a, b):
    return lax.dot_general(a, b, (((1,), (1,)), ((), ())), preferred_element_type=F32)


def loop(count, step):
    lax.fori_loop(0, count, lambda i, z: (step(i), z)[1], 0)


def span(i, size):
    return pl.ds(pl.multiple_of(i * size, size), size)


def normalized(values):
    center = values - jnp.mean(values, axis=-1, keepdims=True)
    spread = jnp.mean(center * center, axis=-1, keepdims=True)
    factor = lax.rsqrt(spread + EPS)
    return center * factor, factor


class Ring:
    def __init__(self, mesh):
        self.axes = ("rep", "fsdp")
        self.n = mesh.shape["fsdp"]
        self.reps = mesh.shape["rep"]
        n = self.n
        self.order = list(range(0, n, 2)) + list(range(n - 1, 0, -2))
        self.place = [self.order.index(f) for f in range(n)]
        self.half = n // 2

    def send(self, v, target, keep=lambda r, f: True):
        n = self.n
        pairs = []
        for r in range(self.reps):
            for f in range(n):
                if keep(r, f):
                    r2, f2 = target(r, f)
                    pairs.append((r * n + f, r2 * n + f2))
        return lax.ppermute(v, self.axes, pairs)

    def along(self, v):
        def target(r, f):
            step = 1 if r % 2 == 0 else -1
            return r, self.order[(self.place[f] + step) % self.n]

        return self.send(v, target)

    def core(self, v):
        return self.send(v, lambda r, f: (r ^ 1, f))

    def across(self, v, keep=lambda r, f: True):
        return self.send(v, lambda r, f: (r ^ 2, f), keep)

    def here(self):
        r = lax.axis_index("rep")
        return r % 2, (r // 2) % 2, lax.axis_index("fsdp")

    def own_place(self):
        n, (c, _, f) = self.n, self.here()
        return jnp.where(f % 2 == 0, f // 2, n - 1 - f // 2), 1 - 2 * c

    def shard_back(self, h):
        n, (p, d) = self.n, self.own_place()
        q = lax.rem(p - d * h + 2 * n, n)
        return jnp.where(q < n // 2, 2 * q, 2 * (n - 1 - q) + 1)

    def slot(self, j):
        n, (p, d) = self.n, self.own_place()
        return lax.rem((self.place[j] - p) * d + n, n)


def cut_kernel(ring, a, v, ext, *more):
    ext[...] = v[0:a, :]
    if more:
        (rest,) = more
        if rest.shape == v.shape:
            rest[...] = v[...]
        else:
            rest[...] = v[pl.ds(pl.multiple_of(ring.here()[0] * a, 16), rest.shape[0]), :]


def there_first(x, other):
    return lax.optimization_barrier((x, other))


def gather(ring, firsts, a, extras):
    m = ring.half
    b, width = firsts[0].shape[0] - a, firsts[0].shape[1]
    groups = [dict(ring=[], out=[], pring=[], pout=[], due=[]) for _ in firsts]
    for h in range(1, m + 2):
        for i, g in enumerate(groups):
            if h == 1:
                g["ring"].append(ring.along(firsts[i]))
                continue
            v = g["ring"][-1]
            shapes = [out((a, width), BF)]
            if h <= m:
                shapes.append(out(v.shape if h < m else (b, width), BF))
            deps = g["due"] + (groups[0]["due"] if i and h > m else [])
            ext, *rest = kernel_call(functools.partial(cut_kernel, ring, a), shapes, [v], deps=deps, name="cut")
            if h > 2:
                x = rest if rest else [ext]
                x[0], g["out"][-1] = there_first(x[0], g["out"][-1])
                ext = ext if rest else x[0]
            if rest:
                g["ring"].append(ring.along(rest[0]))
            even = (lambda r, f: r % 2 == 0) if h > m else (lambda r, f: True)
            g["due"] = [ring.across(ext, even), ring.core(v)]
            if h > 2:
                g["pout"].append(ring.core(g["out"][-1]))
                g["due"].append(g["pout"][-1])
            g["out"].append(g["due"][0])
            g["pring"].append(g["due"][1])
            more = extras.send(ext)
            if more is not None:
                g["due"].append(more)
    groups[0]["pout"].append(ring.core(groups[0]["out"][-1]))
    return groups


def flat(own, opp, g):
    return [own, opp, *g["ring"], *g["pring"], *g["out"], *g["pout"]]


def place_parts(ring, a, refs, put):
    n, m = ring.n, ring.half
    own, opp, refs = refs[0], refs[1], refs[2:]
    rings, prings, outs, pouts = (refs[i * m : (i + 1) * m] for i in range(4))

    def all_parts(step, ext, mid, mid0, other):
        s = ring.shard_back(step)
        put("mid", s, mid, mid0)
        put("ext", s, ext, 0)
        put("opp", s, other, 0)

    all_parts(0, own, own, a, opp)
    for h in range(1, m):
        all_parts(h, rings[h - 1], rings[h - 1], a, outs[h - 1])
        all_parts(n - h, prings[h - 1], prings[h - 1], a, pouts[h - 1])

    c = ring.here()[0]

    @pl.when(c == 0)
    def _():
        all_parts(m, rings[-1], prings[-1], 0, outs[-1])

    @pl.when(c == 1)
    def _():
        all_parts(m, prings[-1], rings[-1], 0, pouts[-1])


def ln_rows(x_ref, gain, bias, o_ref, rows=384):
    def step(i):
        at = span(i, rows)
        n, _ = normalized(x_ref[at, :].astype(F32))
        o_ref[at, :] = (n * gain + bias).astype(BF)

    loop(x_ref.shape[0] // rows, step)


def split_kernel(ring, t, jw, ow, first, opp, sems):
    width = ow.shape[1]
    rps = ow.shape[0]
    a = rps + t
    x = ring.here()[1]
    made = []

    def copy(src, dst):
        c = pltpu.make_async_copy(src, dst, sems.at[len(made)])
        c.start()
        made.append(c)

    def cols(side):
        return jw.at[:, pl.ds(pl.multiple_of(side * 2 * width, width), width)]

    copy(cols(x), first.at[pl.ds(0, rps), :])
    copy(jw.at[:, pl.ds(width, width)], first.at[pl.ds(a, rps), :])
    copy(ow.at[pl.ds(t, rps - 2 * t), :], first.at[pl.ds(a + rps, rps - 2 * t), :])
    copy(cols(1 - x), opp.at[pl.ds(0, rps), :])
    if t:
        copy(ow.at[pl.ds(pl.multiple_of(x * (rps - t), 16), t), :], first.at[pl.ds(rps, t), :])
        copy(ow.at[pl.ds(pl.multiple_of((1 - x) * (rps - t), 16), t), :], opp.at[pl.ds(rps, t), :])
    for c in made:
        c.wait()


def split_ff_kernel(ring, t, uw, dw, first, opp, sems):
    width = dw.shape[1]
    rps = uw.shape[0]
    a = rps + t
    x = ring.here()[1]
    made = []

    def copy(src, dst):
        c = pltpu.make_async_copy(src, dst, sems.at[len(made)])
        c.start()
        made.append(c)

    def cols(side):
        return uw.at[:, pl.ds(pl.multiple_of(side * width, width), width)]

    copy(cols(x), first.at[pl.ds(0, rps), :])
    copy(dw.at[pl.ds(t, 2 * rps - 2 * t), :], first.at[pl.ds(a, 2 * rps - 2 * t), :])
    copy(cols(1 - x), opp.at[pl.ds(0, rps), :])
    if t:
        copy(dw.at[pl.ds(pl.multiple_of(x * (2 * rps - t), 16), t), :], first.at[pl.ds(rps, t), :])
        copy(dw.at[pl.ds(pl.multiple_of((1 - x) * (2 * rps - t), 16), t), :], opp.at[pl.ds(rps, t), :])
    for c in made:
        c.wait()


def small_kernel(ring, *refs):
    parts, o_ref = refs[:-1], refs[-1]
    width = o_ref.shape[1]
    n, f = ring.n, ring.here()[2]
    row = 0
    o_ref[...] = jnp.zeros_like(o_ref)
    for part in parts:
        size = part.shape[0]
        full = size * n
        i = lax.broadcasted_iota(jnp.int32, (size, full), 0)
        j = lax.broadcasted_iota(jnp.int32, (size, full), 1)
        hot = jnp.where(j == i + f * size, 1.0, 0.0).astype(BF)
        placed = dot(jnp.broadcast_to(part[...].astype(F32)[None, :], (8, size)).astype(BF), hot)
        for k in range(full // width):
            o_ref[row : row + 1, :] = placed[0:1, k * width : (k + 1) * width]
            row += 1


def add_f32_kernel(a_ref, b_ref, o_ref):
    o_ref[...] = a_ref[...] + b_ref[...]


def ln_kernel(x_ref, small, o_ref):
    ln_rows(x_ref, small[pl.ds(GAIN1, 1), :], small[pl.ds(BIAS1, 1), :], o_ref)


def qkv_kernel(ring, a, t, first, small, *refs):
    refs, outs = refs[:-5], refs[-5:]
    proj, ws, wo = outs[:2], outs[2:4], outs[4]
    width = first.shape[1]
    rps = width // ring.n
    hw = width // 2
    xb = ring.here()[1]

    def put(part, s, ref, r0):
        row = pl.multiple_of(s * rps, rps)
        if part == "mid":
            for k in range(2):
                ws[k][pl.ds(row, rps), hw : 2 * hw] = ref[r0 : r0 + rps, k * hw : (k + 1) * hw]
            wo[pl.ds(pl.multiple_of(row + t, 16), rps - 2 * t), :] = ref[r0 + rps : r0 + 2 * rps - 2 * t, :]
        else:
            side = xb if part == "ext" else 1 - xb
            col = pl.multiple_of(side * 2 * hw, hw)
            for k in range(2):
                ws[k][pl.ds(row, rps), pl.ds(col, hw)] = ref[0:rps, k * hw : (k + 1) * hw]
            if t:
                wo[pl.ds(pl.multiple_of(row + side * (rps - t), 16), t), :] = ref[rps : rps + t, :]

    place_parts(ring, a, refs, put)
    for k in range(2):

        def tile(i, k=k):
            at = span(i, hw)
            v = dot(first[...], ws[k][:, at])
            use = jnp.where(i == 0, 1.0, 0.0), jnp.where(i == 2, 1.0, 0.0)
            shift = small[pl.ds(JB_Q, 1), k * hw : (k + 1) * hw] * use[0]
            shift = shift + small[pl.ds(JB_V, 1), k * hw : (k + 1) * hw] * use[1]
            proj[k][:, at] = (v + shift).astype(BF)

        loop(3, tile)


def mask(col_ids, row_ids, q0, k0, queries, keys):
    same = col_ids[pl.ds(k0, keys), :] == row_ids[:, pl.ds(q0, queries)]
    kpos = lax.broadcasted_iota(jnp.int32, (keys, queries), 0) + k0
    qpos = lax.broadcasted_iota(jnp.int32, (keys, queries), 1) + q0
    return jnp.where(same & (kpos <= qpos), 0.0, MASKED).astype(F32)


def soft(q, k, bias):
    s = dot_nt(k, q) * (HD ** (-0.5) * LOG2E) + bias
    p = jnp.exp2(s - jnp.max(s, axis=0, keepdims=True))
    return p * (1.0 / jnp.sum(p, axis=0, keepdims=True))


def head_cols(part, h):
    return slice((part * HALF + h) * HD, (part * HALF + h + 1) * HD)


def tiles(rows, queries, back):
    for q0 in range(0, rows, queries):
        lo = min(q0, back)
        yield q0, q0 - lo, queries + lo


def attend_kernel(proj_a, proj_b, col_ids, row_ids, o_ref):
    nq = 256
    for q0, k0, nk in tiles(o_ref.shape[0], nq, 128):
        at_q, at_k = slice(q0, q0 + nq), slice(k0, k0 + nk)
        bias = mask(col_ids, row_ids, q0, k0, nq, nk)
        for k, proj in enumerate((proj_a, proj_b)):
            for h in range(HALF):
                w = soft(proj[at_q, head_cols(0, h)], proj[at_k, head_cols(1, h)], bias).astype(BF)
                col = (k * HALF + h) * HD
                o_ref[at_q, col : col + HD] = dot_tn(w, proj[at_k, head_cols(2, h)]).astype(BF)


def out_kernel(att, wo, x_ref, small, middle, second):
    tn = 512

    def step(i):
        at = span(i, tn)
        middle[:, at] = x_ref[:, at].astype(F32) + dot(att[...], wo[:, at]) + small[pl.ds(OUT_B, 1), at]

    loop(wo.shape[1] // tn, step)
    ln_rows(middle, small[pl.ds(GAIN2, 1), :], small[pl.ds(BIAS2, 1), :], second)


def gelu_both(h):
    h2 = h * h
    half = 0.5 + 0.5 * jnp.tanh(h * (C0 + (C0 * 0.044715) * h2))
    act = h * half
    return act, half + act * (1.0 - half) * (2.0 * C0 + (6.0 * C0 * 0.044715) * h2)


def up_kernel(ring, a, t, second, small, *refs):
    refs, outs = refs[:-4], refs[-4:]
    active, slope, wu, wd = outs
    width = second.shape[1]
    rps = width // ring.n
    xb = ring.here()[1]

    def put(part, s, ref, r0):
        row = pl.multiple_of(s * rps, rps)
        drow = pl.multiple_of(s * 2 * rps, 2 * rps)
        if part == "mid":
            wd[pl.ds(pl.multiple_of(drow + t, 16), 2 * rps - 2 * t), :] = ref[r0 : r0 + 2 * rps - 2 * t, :]
        else:
            side = xb if part == "ext" else 1 - xb
            wu[pl.ds(row, rps), pl.ds(pl.multiple_of(side * width, width), width)] = ref[0:rps, :]
            if t:
                wd[pl.ds(pl.multiple_of(drow + side * (2 * rps - t), 16), t), :] = ref[rps : rps + t, :]

    place_parts(ring, a, refs, put)
    tn = 512
    per = width // tn

    def step(i):
        at = span(i, tn)
        shift = small[pl.ds(UP_B + i // per, 1), span(i % per, tn)]
        act, s = gelu_both(dot(second[...], wu[:, at]) + shift)
        active[:, at] = act.astype(BF)
        slope[:, at] = s.astype(BF)

    loop(2 * per, step)


def dact_kernel(og, wd, slope, o_ref):
    tn = 256

    def step(i):
        at = span(i, tn)
        o_ref[:, at] = (dot_nt(og[...], wd[at, :]) * slope[:, at].astype(F32)).astype(BF)

    loop(o_ref.shape[1] // tn, step)


def down_kernel(active, wd, middle, small, o_ref):
    tn = 256

    def step(i):
        at = span(i, tn)
        o_ref[:, at] = (middle[:, at] + dot(active[...], wd[:, at]) + small[pl.ds(DOWN_B, 1), at]).astype(BF)

    loop(o_ref.shape[1] // tn, step)


def weight_grad_kernel(ring, tn, tl, left, right, buf, sent, sums):
    n, m = ring.n, ring.half
    half = left.shape[1] // n // 2
    slots = [ring.slot(j) for j in range(n)]
    swap = [jnp.where(k == m, ring.here()[0], 0) for k in slots]
    ones = jnp.ones((8, right.shape[0]), BF)
    per = tl // half

    def step(i):
        at = span(i, tn)
        r = right[:, at]
        sums[:, at] = dot(ones, r)
        for l in range(left.shape[1] // tl):
            v = dot_tn(left[:, l * tl : (l + 1) * tl], r).astype(BF)
            for s in range(per):
                j, q = divmod(l * per + s, 2)
                row = pl.multiple_of((2 * slots[j] + (swap[j] + q) % 2) * half, half)
                buf[pl.ds(row, half), at] = v[s * half : (s + 1) * half, :]
        sent[:, at] = buf[buf.shape[0] - sent.shape[0] :, at]

    loop(right.shape[1] // tn, step)


def norm_back(values, d, gain):
    n, r = normalized(values)
    g = d * gain
    t = r * (g - jnp.mean(g, axis=-1, keepdims=True) - n * jnp.mean(g * n, axis=-1, keepdims=True))
    return t, d * n


def group_sum(v):
    return jnp.sum(v.reshape(v.shape[0] // 8, 8, v.shape[1]), axis=0)


def dsecond_kernel(dh, wu, acc):
    tn = 256

    def step(i):
        at = span(i, tn)
        acc[:, at] = dot_nt(dh[...], wu[at, :])

    loop(acc.shape[1] // tn, step)


def second_norm_back_kernel(acc, wo, middle, og, small, dmid, dbranch, datt, sg, sb):
    g = small[pl.ds(GAIN2, 1), :]
    sg[...] = jnp.zeros_like(sg)
    sb[...] = jnp.zeros_like(sb)
    rows = 256

    def norm(i):
        at = span(i, rows)
        d = acc[at, :]
        t, dn = norm_back(middle[at, :], d, g)
        sg[...] += group_sum(dn)
        sb[...] += group_sum(d)
        v = og[at, :].astype(F32) + t
        dmid[at, :] = v
        dbranch[at, :] = v.astype(BF)

    loop(acc.shape[0] // rows, norm)
    tn = 256

    def back(i):
        at = span(i, tn)
        datt[:, at] = dot_nt(dbranch[...], wo[at, :]).astype(BF)

    loop(datt.shape[1] // tn, back)


def attend_back_kernel(part, proj, datt, col_ids, row_ids, o_ref, acc_k, acc_v):
    rows, hw = acc_k.shape
    scale = HD ** (-0.5)
    nq, back = 128, 64
    heads = range(HALF)
    acc_k[...] = jnp.zeros_like(acc_k)
    acc_v[...] = jnp.zeros_like(acc_v)

    def tile(q0, k0, nk):
        at_q, at_k = pl.ds(q0, nq), pl.ds(k0, nk)
        bias = mask(col_ids, row_ids, q0, k0, nq, nk)
        q = [proj[at_q, head_cols(0, h)] for h in heads]
        k = [proj[at_k, head_cols(1, h)] for h in heads]
        do = [datt[at_q, head_cols(part, h)] for h in heads]
        dw = [dot_nt(proj[at_k, head_cols(2, h)], do[h]) for h in heads]
        p = [soft(q[h], k[h], bias) for h in heads]
        for h in heads:
            acc_v[at_k, head_cols(0, h)] += dot(p[h].astype(BF), do[h])
        ds = [(p[h] * (dw[h] - jnp.sum(p[h] * dw[h], axis=0, keepdims=True))).astype(BF) for h in heads]
        for h in heads:
            acc_k[at_k, head_cols(0, h)] += dot(ds[h], q[h])
            o_ref[at_q, head_cols(0, h)] = (dot_tn(ds[h], k[h]) * scale).astype(BF)

    tile(0, 0, nq)

    def step(i):
        q0 = pl.multiple_of((i + 1) * nq, nq)
        tile(q0, pl.multiple_of(q0 - back, back), nq + back)

    loop(rows // nq - 1, step)
    o_ref[:, hw : 2 * hw] = (acc_k[...] * scale).astype(BF)
    o_ref[:, 2 * hw :] = acc_v[...].astype(BF)


def dfirst_kernel(da, db, wa, wb, acc):
    tn = 256

    def step(i):
        at = span(i, tn)
        acc[:, at] = dot_nt(da[...], wa[at, :]) + dot_nt(db[...], wb[at, :])

    loop(acc.shape[1] // tn, step)


def first_norm_back_kernel(acc, x_ref, dmid, small, o_ref, sg, sb):
    g = small[pl.ds(GAIN1, 1), :]
    sg[...] = jnp.zeros_like(sg)
    sb[...] = jnp.zeros_like(sb)
    rows = 256

    def norm(i):
        at = span(i, rows)
        d = acc[at, :]
        t, dn = norm_back(x_ref[at, :].astype(F32), d, g)
        sg[...] += group_sum(dn)
        sb[...] += group_sum(d)
        o_ref[at, :] = (dmid[at, :] + t).astype(BF)

    loop(x_ref.shape[0] // rows, norm)


def small_grads_kernel(ring, sizes, sg1, sb1, ja, jb, so, sg2, sb2, su, sd, buf, sent):
    n, m = ring.n, ring.half
    hw = ja.shape[1] // 3
    rows = buf.shape[0] // n

    def whole(ref):
        return jnp.sum(ref[...], axis=0, keepdims=True)

    queries = jnp.concatenate([ja[0:1, 0:hw], jb[0:1, 0:hw]], axis=1)
    values = jnp.concatenate([ja[0:1, 2 * hw :], jb[0:1, 2 * hw :]], axis=1)
    vectors = [
        whole(sg1), whole(sb1), jnp.concatenate([queries, values], axis=1), so[0:1, :],
        whole(sg2), whole(sb2), su[0:1, :], sd[0:1, :],
    ]
    buf[...] = jnp.zeros_like(buf)
    c = ring.here()[0]
    for j in range(n):
        slot = ring.slot(j)
        top = pl.multiple_of((2 * slot + jnp.where(slot == m, c, 0)) * (rows // 2), rows // 2)
        for size in sorted(set(sizes)):
            parts = [v[:, j * size : (j + 1) * size] for v, k in zip(vectors, sizes) if k == size]
            parts.append(jnp.zeros((rows // 2 - len(parts), size), F32))
            block = jnp.concatenate(parts, axis=0).astype(BF)
            at = 0 if size == min(sizes) else SMALL_COL
            buf[pl.ds(top, rows // 2), at : at + size] = block
    sent[...] = buf[buf.shape[0] - sent.shape[0] :, :]


class Grads:
    def __init__(self, n, bufs, recvs, width):
        self.bufs, self.recvs, self.width = bufs, recvs, width
        self.sizes = [(b.shape[0] // n, b.shape[1] // width) for b in bufs]
        self.rows = sum(r * c for r, c in self.sizes)


def reduce_step(ring, gr, k, got):
    m, n = ring.half, ring.n
    width = gr.width
    half = k == m
    total = gr.rows // 2 if half else gr.rows
    args = [*gr.bufs, *gr.recvs] + ([got] if got is not None else [])
    nb = len(gr.bufs)

    def body(*refs):
        bs, rs = refs[:nb], refs[nb : 2 * nb]
        g = refs[2 * nb] if got is not None else None
        o = refs[-1]
        c = ring.here()[0]
        at, gat = 0, 0
        for b, rv, (r, cs) in zip(bs, rs, gr.sizes):
            h = r // 2
            for j in range(cs):
                col = slice(j * width, (j + 1) * width)
                if half:
                    v = b[m * r : m * r + h, col].astype(F32) + rv[0:h, col].astype(F32)
                    o[at : at + h, :] = v.astype(BF)
                    at += h
                else:
                    base = h + (n - k - m - 1) * r
                    v = b[k * r : (k + 1) * r, col].astype(F32) + rv[base : base + r, col].astype(F32)
                    if g.shape[0] == total:
                        o[at : at + r, :] = (v + g[at : at + r, :].astype(F32)).astype(BF)
                    else:
                        top = jnp.where(c == 0, 1.0, 0.0)
                        gv = g[gat : gat + h, :].astype(F32)
                        o[at : at + h, :] = (v[:h] + gv * top).astype(BF)
                        o[at + h : at + r, :] = (v[h:] + gv * (1.0 - top)).astype(BF)
                        gat += h
                    at += r

    return body, [out((total, width), BF)], args


def owner_sum(ring, gr, got):
    nb = len(gr.bufs)

    def body(*refs):
        bs, g, keep, send = refs[:nb], refs[nb], refs[nb + 1], refs[nb + 2]
        c = ring.here()[0]
        at, to = 0, 0
        for b, (r, cs) in zip(bs, gr.sizes):
            h = r // 2
            for j in range(cs):
                v = b[0:r, j * gr.width : (j + 1) * gr.width].astype(F32) + g[at : at + r, :].astype(F32)
                v = v.astype(BF)
                keep[to : to + h, :] = jnp.where(c == 0, v[:h], v[h:])
                send[to : to + h, :] = jnp.where(c == 0, v[h:], v[:h])
                at += r
                to += h

    o = out((gr.rows // 2, gr.width), BF)
    return body, [o, o], [*gr.bufs, got]


def add_kernel(a_ref, b_ref, o_ref):
    o_ref[...] = (a_ref[...].astype(F32) + b_ref[...].astype(F32)).astype(o_ref.dtype)


def add2(a, b):
    return add_kernel, [out(a.shape, a.dtype)], [a, b]


def reduce_group(ring, gr):
    got = None
    for k in range(ring.half, 0, -1):
        (part,) = yield reduce_step(ring, gr, k, got)
        got = ring.along(part)
    keep, send = yield owner_sum(ring, gr, got)
    (u,) = yield add2(keep, ring.core(send))
    bit = 2
    while bit < ring.reps:
        (u,) = yield add2(u, ring.send(u, lambda r, f, bit=bit: (r ^ bit, f)))
        bit *= 2
    return u, ring.core(u)


class Rounds:
    def __init__(self, line):
        self.line = line
        self.long = False
        self.live = {}
        self.jobs = {}
        self.done = {}

    def _advance(self, name, results):
        try:
            self.jobs[name] = next(self.live[name]) if results is None else self.live[name].send(results)
        except StopIteration as stop:
            self.done[name] = stop.value
            del self.live[name]
            self.jobs.pop(name, None)

    def add(self, name, chain):
        self.live[name] = chain
        self._advance(name, None)

    def turn(self, *names):
        names = [k for k in names or self.jobs if k in self.jobs]
        if not names:
            return
        jobs = [self.jobs[k] for k in names]
        args = [a for _, _, given in jobs for a in given]
        outs = [o for _, made, _ in jobs for o in made]

        def body(*refs):
            i, j = 0, len(args)
            for run, made, given in jobs:
                run(*refs[i : i + len(given)], *refs[j : j + len(made)])
                i, j = i + len(given), j + len(made)

        got = list(self.line.call(body, outs, args, long=self.long, name="sums"))
        for name, (_, made, _) in zip(names, jobs):
            self._advance(name, got[: len(made)])
            got = got[len(made) :]


def join_halves(c, parts, sizes, width, place):
    a_ref, b_ref = parts
    to = 0
    for i, (r, cs) in enumerate(sizes):
        h = r // 2
        for j in range(cs):
            a = a_ref[to : to + h, :].astype(F32)
            b = b_ref[to : to + h, :].astype(F32)
            place(i, slice(0, h), j, jnp.where(c == 0, a, b))
            place(i, slice(h, r), j, jnp.where(c == 0, b, a))
            to += h


def last_sum(job):
    return (yield job)


def finish(ring, gr, parts):
    def body(a_ref, b_ref, *outs):
        def place(i, rows, j, v):
            outs[i][rows, j * gr.width : (j + 1) * gr.width] = v

        join_halves(ring.here()[0], (a_ref, b_ref), gr.sizes, gr.width, place)

    return body, [out((r, cs * gr.width), F32) for r, cs in gr.sizes], list(parts)


def finish_joint(ring, gr_a, gr_b, parts_a, parts_b, sizes):
    (r, cs), (_, ocs), width = *gr_a.sizes, gr_a.width

    def body(a1, a2, b1, b2, o, o2, small, *outs):
        for k, pair in enumerate(((a1, a2), (b1, b2))):
            def place(i, rows, j, v, k=k):
                if i == 0:
                    at = (2 * j + k) * width
                    o[rows, at : at + width] = v
                elif k == 0:
                    o2[rows, j * width : (j + 1) * width] = v
                else:
                    small[rows, :] = v

            join_halves(ring.here()[0], pair, (gr_a, gr_b)[k].sizes, width, place)
        row = {}
        for size, got in zip(sizes, outs):
            k = row.setdefault(size, 0)
            row[size] += 1
            at = 0 if size == min(sizes) else SMALL_COL
            got[...] = small[k : k + 1, at : at + size]

    outs = [out((r, 2 * cs * width), F32), out((r, ocs * width), F32), out((SMALL_SHARD, width), F32)] + [out((1, k), F32) for k in sizes]
    return body, outs, [*parts_a, *parts_b]


def step_fn(mesh):
    ring = Ring(mesh)
    n, m = ring.n, ring.half

    def on_device(
        layer_input, item_ids, norm_gain, norm_bias, joint_weight, joint_bias, out_weight, out_bias,
        second_gain, second_bias, up_weight, up_bias, down_weight, down_bias, output_grad,
    ):
        rows, width = layer_input.shape
        ff = up_weight.shape[1]
        hw = width // 2
        rps = width // n
        t = (rps // 4) // 16 * 16
        a, b = rps + t, 2 * rps - 2 * t
        dma = pltpu.SemaphoreType.DMA
        shapes = [out((a + b, width), BF), out((a, width), BF)]
        line = Line()
        first1, opp1 = line.call(
            functools.partial(split_kernel, ring, t), shapes, [joint_weight, out_weight],
            far=(0, 1), scratch=[dma((6,))], name="split",
        )
        ids = [item_ids[:, None], item_ids[None, :]]
        first2, opp2 = line.call(
            functools.partial(split_ff_kernel, ring, t), shapes, [up_weight, down_weight], deps=ids,
            far=(0, 1), scratch=[dma((5,))], name="split_ff",
        )
        vectors = (norm_gain, norm_bias, joint_bias, out_bias, second_gain, second_bias, up_bias, down_bias)
        shared = {}

        def small_parts():
            (small,) = line.call(
                functools.partial(small_kernel, ring), [out((SMALL_ROWS, width), F32)], vectors, name="small",
            )
            mark = yield
            bit = 1
            while bit < n:
                other = ring.send(small, lambda r, f, bit=bit: (r, f ^ bit))
                yield (small if bit > 1 else None)
                mark = yield
                (small,) = kernel_call(add_f32_kernel, [out(small.shape, F32)], [small, other], deps=[mark], name="small_sum")
                bit *= 2
            shared["small"] = small
            (shared["first"],) = kernel_call(
                ln_kernel, [out((rows, width), BF)], [layer_input, small], deps=[mark], name="first_norm",
            )
            mark = yield shared["first"]
            while True:
                yield

        extras = small_parts()
        next(extras)
        g1, g2 = gather(ring, [first1, first2], a, extras)
        small, first = shared["small"], shared["first"]

        args = [first, small, *flat(first1, opp1, g1)]
        halves = [out((rows, 3 * hw), BF)] * 2
        proj_a, proj_b, wa, wb, wo = line.call(
            functools.partial(qkv_kernel, ring, a, t),
            halves + [out((width, 3 * hw), BF)] * 2 + [out((width, width), BF)],
            args, name="projection",
        )
        g2["out"][-1], wo = there_first(g2["out"][-1], wo)
        g2["pout"].append(ring.core(g2["out"][-1]))
        (attended,) = line.call(attend_kernel, [out((rows, width), BF)], [proj_a, proj_b, *ids], name="attend")
        middle, second = line.call(
            out_kernel, [out((rows, width), F32), out((rows, width), BF)],
            [attended, wo, layer_input, small], name="out_projection",
        )
        args = [second, small, *flat(first2, opp2, g2)]
        active, slope, wu, wd = line.call(
            functools.partial(up_kernel, ring, a, t),
            [out((rows, ff), BF), out((rows, ff), BF), out((width, ff), BF), out((ff, width), BF)],
            args, name="up_projection",
        )

        def weight_grad(l, r, tl=512, tn=512, name=None):
            kl, kr = l.shape[1], r.shape[1]
            kept = m * (kl // n) + kl // n // 2
            buf, sent, sums = line.call(
                functools.partial(weight_grad_kernel, ring, tn, tl),
                [out((kl, kr), BF), out((kl - kept, kr), BF), out((8, kr), F32)], [l, r], name=name,
            )
            return buf, ring.core(sent), sums

        rounds = Rounds(line)

        def begin(name, bufs, recvs, w):
            gr = Grads(n, bufs, recvs, w)
            rounds.add(name, reduce_group(ring, gr))
            return gr

        down_buf, down_recv, s_down = weight_grad(active, output_grad, name="down_grad")
        (dhidden,) = line.call(
            dact_kernel, [out((rows, ff), BF)], [output_grad, wd, slope], name="hidden_grad",
        )
        gr_down = begin("down", [down_buf], [down_recv], width)
        rounds.turn("down")
        up_buf, up_recv, s_up = weight_grad(second, dhidden, name="up_grad")
        rounds.turn("down")
        (dsecond,) = line.call(dsecond_kernel, [out((rows, width), F32)], [dhidden, wu], name="dsecond")
        gr_up = begin("up", [up_buf], [up_recv], width)
        rounds.turn("up")
        dmid, dbranch, datt, sg2, sb2 = line.call(
            second_norm_back_kernel,
            [out((rows, width), F32), out((rows, width), BF), out((rows, width), BF), out((8, width), F32), out((8, width), F32)],
            [dsecond, wo, middle, output_grad, small], name="second_norm_grad",
        )
        rounds.turn("down")
        out_buf, out_recv, s_out = weight_grad(attended, dbranch, name="out_grad")
        rounds.turn("up")

        def attend_back(part, proj):
            return line.call(
                functools.partial(attend_back_kernel, part), [out((rows, 3 * hw), BF)], [proj, datt, *ids],
                scratch=[VM((rows, hw), F32), VM((rows, hw), F32)], name="attend_grad",
            )[0]

        da = attend_back(0, proj_a)
        rounds.turn("down")
        ja_buf, ja_recv, s_ja = weight_grad(first, da, name="joint_grad")
        rounds.turn("up")
        db = attend_back(1, proj_b)
        gr_ja = begin("ja", [ja_buf, out_buf], [ja_recv, out_recv], hw)
        rounds.turn("ja", "down")
        jb_buf, jb_recv, s_jb = weight_grad(first, db, name="joint_grad")
        rounds.turn("up")
        (dfirst,) = line.call(dfirst_kernel, [out((rows, width), F32)], [da, db, wa, wb], name="dfirst")
        rounds.turn("ja")
        input_grad, sg1, sb1 = line.call(
            first_norm_back_kernel, [out((rows, width), BF), out((8, width), F32), out((8, width), F32)],
            [dfirst, layer_input, dmid, small], name="first_norm_grad",
        )
        small_sizes = [v.shape[0] for v in vectors]
        small_kept = m * SMALL_SHARD + SMALL_SHARD // 2
        small_buf, small_sent = line.call(
            functools.partial(small_grads_kernel, ring, small_sizes),
            [out((n * SMALL_SHARD, hw), BF), out((n * SMALL_SHARD - small_kept, hw), BF)],
            [sg1, sb1, s_ja, s_jb, s_out, sg2, sb2, s_up, s_down], long=False, name="small_grads",
        )
        (layer_output,) = line.call(
            down_kernel, [out((rows, width), BF)], [active, wd, middle, small], name="down_projection",
        )
        gr_jb = begin("jb", [jb_buf, small_buf], [jb_recv, ring.core(small_sent)], hw)
        rounds.turn("jb", "down")
        rounds.long = True
        rounds.turn("ja", "up")
        done, ready = rounds.done, set()
        pairs = ("jb", "up", "got up"), ("ja", "down", "got down")
        k = 0
        while rounds.jobs:
            rounds.turn(*(pairs[k % 2] if "ja" in rounds.jobs or "jb" in rounds.jobs else ()))
            k += 1
            for name, gr in (("down", gr_down), ("up", gr_up)):
                if name in done and name not in ready:
                    ready.add(name)
                    rounds.add("got " + name, last_sum(finish(ring, gr, done[name])))
            if "ja" in done and "jb" in done and "joint" not in ready:
                ready.add("joint")
                rounds.add("got joint", last_sum(finish_joint(ring, gr_ja, gr_jb, done["ja"], done["jb"], small_sizes)))
        (g_down,), (g_up,), (g_joint, g_out, _, *v) = (done["got " + k] for k in ("down", "up", "joint"))
        v = [k.reshape(-1) for k in v]
        return (
            layer_output, input_grad, v[0], v[1], g_joint, v[2], g_out, v[3], v[4], v[5], g_up, v[6], g_down, v[7],
        )

    return on_device


def solution(mesh):
    row, vecs, mat = P(("rep", "fsdp"), None), P("fsdp"), P("fsdp", None)
    placed = (
        row, P(("rep", "fsdp")), vecs, vecs, mat, vecs, mat, vecs, vecs, vecs, mat, vecs, mat, vecs, row,
    )
    return jax.shard_map(
        step_fn(mesh),
        mesh=mesh,
        in_specs=placed,
        out_specs=(row, row, vecs, vecs, mat, vecs, mat, vecs, vecs, vecs, mat, vecs, mat, vecs),
        check_vma=False,
    )
```

```python
import functools
import math

import jax
import jax.numpy as jnp
from jax import lax
from jax.experimental import pallas as pl
from jax.experimental.pallas import tpu as pltpu
from jax.sharding import PartitionSpec as P

H = 8
HD = 128
HALF = H // 2
EPS = 1e-05
MASKED = -1e30
LOG2E = 1.4426950408889634
C0 = math.sqrt(2.0 / math.pi)
BF = jnp.bfloat16
F32 = jnp.float32
VM = pltpu.VMEM
MAIN = 60 * 10**9
MIB = 2**20

GAIN1, BIAS1, JB_Q, JB_V, OUT_B, GAIN2, BIAS2, UP_B, DOWN_B = 0, 1, 2, 3, 4, 5, 6, 7, 9
SMALL_ROWS = 16
SMALL_SHARD, SMALL_COL = 32, 256


def nbytes(a):
    return math.prod(a.shape) * jnp.dtype(a.dtype).itemsize


def kernel_call(body, outs, args, deps=(), smem=(), anys=(), far=(), scratch=(), straight=(), extra=4, long=True, name=None):
    own = sum(nbytes(s) for s in scratch if getattr(s, "dtype", None) in (BF, F32))
    count, made = len(args), len(outs)
    deps = [d for d in deps if d is not None]

    def space(i):
        return pl.ANY if i in anys else pltpu.HBM if i in far else pltpu.SMEM if i in smem else VM

    args = [pltpu.with_memory_space_constraint(v, pltpu.HBM) if i in far else v for i, v in enumerate(args)]

    def run(*refs):
        body(*refs[:count], *refs[count + len(deps) :])

    return pl.pallas_call(
        run,
        out_shape=[pltpu.HBM(o.shape, o.dtype) if i in straight else o for i, o in enumerate(outs)],
        in_specs=[pl.BlockSpec(memory_space=space(i)) for i in range(count)]
        + [pl.BlockSpec(memory_space=pl.ANY) for _ in deps],
        out_specs=[pl.BlockSpec(memory_space=pltpu.HBM if i in straight else VM) for i in range(len(outs))],
        scratch_shapes=list(scratch),
        compiler_params=pltpu.CompilerParams(vmem_limit_bytes=own + int(extra * MIB)),
        cost_estimate=pl.CostEstimate(flops=MAIN if long else 0, bytes_accessed=0, transcendentals=0),
        name=name,
    )(*args, *deps)


def out(shape, dtype):
    return jax.ShapeDtypeStruct(shape, dtype)


class Line:
    def __init__(self):
        self.mark = None

    def call(self, body, outs, args, deps=(), **kw):
        made = kernel_call(body, outs, args, deps=(self.mark, *deps), **kw)
        self.mark = min(made, key=nbytes)
        return made


def dot(a, b):
    return jnp.dot(a, b, preferred_element_type=F32)


def dot_tn(a, b):
    return lax.dot_general(a, b, (((0,), (0,)), ((), ())), preferred_element_type=F32)


def dot_nt(a, b):
    return lax.dot_general(a, b, (((1,), (1,)), ((), ())), preferred_element_type=F32)


def loop(count, step):
    lax.fori_loop(0, count, lambda i, z: (step(i), z)[1], 0)


def span(i, size):
    return pl.ds(pl.multiple_of(i * size, size), size)


def normalized(values):
    center = values - jnp.mean(values, axis=-1, keepdims=True)
    spread = jnp.mean(center * center, axis=-1, keepdims=True)
    factor = lax.rsqrt(spread + EPS)
    return center * factor, factor


class Ring:
    def __init__(self, mesh):
        self.axes = ("rep", "fsdp")
        self.n = mesh.shape["fsdp"]
        self.reps = mesh.shape["rep"]
        n = self.n
        self.order = list(range(0, n, 2)) + list(range(n - 1, 0, -2))
        self.place = [self.order.index(f) for f in range(n)]
        self.half = n // 2

    def send(self, v, target, keep=lambda r, f: True):
        n = self.n
        pairs = []
        for r in range(self.reps):
            for f in range(n):
                if keep(r, f):
                    r2, f2 = target(r, f)
                    pairs.append((r * n + f, r2 * n + f2))
        return lax.ppermute(v, self.axes, pairs)

    def along(self, v):
        def target(r, f):
            step = 1 if r % 2 == 0 else -1
            return r, self.order[(self.place[f] + step) % self.n]

        return self.send(v, target)

    def core(self, v):
        return self.send(v, lambda r, f: (r ^ 1, f))

    def across(self, v, keep=lambda r, f: True):
        return self.send(v, lambda r, f: (r ^ 2, f), keep)

    def here(self):
        r = lax.axis_index("rep")
        return r % 2, (r // 2) % 2, lax.axis_index("fsdp")

    def own_place(self):
        n, (c, _, f) = self.n, self.here()
        return jnp.where(f % 2 == 0, f // 2, n - 1 - f // 2), 1 - 2 * c

    def shard_back(self, h):
        n, (p, d) = self.n, self.own_place()
        q = lax.rem(p - d * h + 2 * n, n)
        return jnp.where(q < n // 2, 2 * q, 2 * (n - 1 - q) + 1)

    def slot(self, j):
        n, (p, d) = self.n, self.own_place()
        return lax.rem((self.place[j] - p) * d + n, n)


def cut_kernel(ring, a, v, ext, *more):
    ext[...] = v[0:a, :]
    if more:
        (rest,) = more
        if rest.shape == v.shape:
            rest[...] = v[...]
        else:
            rest[...] = v[pl.ds(pl.multiple_of(ring.here()[0] * a, 16), rest.shape[0]), :]


def there_first(x, other):
    return lax.optimization_barrier((x, other))


def gather(ring, firsts, a, extras):
    m = ring.half
    b, width = firsts[0].shape[0] - a, firsts[0].shape[1]
    groups = [dict(ring=[], out=[], pring=[], pout=[], due=[]) for _ in firsts]
    for h in range(1, m + 2):
        for i, g in enumerate(groups):
            if h == 1:
                g["ring"].append(ring.along(firsts[i]))
                continue
            v = g["ring"][-1]
            shapes = [out((a, width), BF)]
            if h <= m:
                shapes.append(out(v.shape if h < m else (b, width), BF))
            deps = g["due"] + (groups[0]["due"] if i and h > m else [])
            ext, *rest = kernel_call(functools.partial(cut_kernel, ring, a), shapes, [v], deps=deps, name="cut")
            if h > 2:
                x = rest if rest else [ext]
                x[0], g["out"][-1] = there_first(x[0], g["out"][-1])
                ext = ext if rest else x[0]
            if rest:
                g["ring"].append(ring.along(rest[0]))
            even = (lambda r, f: r % 2 == 0) if h > m else (lambda r, f: True)
            g["due"] = [ring.across(ext, even), ring.core(v)]
            if h > 2:
                g["pout"].append(ring.core(g["out"][-1]))
                g["due"].append(g["pout"][-1])
            g["out"].append(g["due"][0])
            g["pring"].append(g["due"][1])
            more = extras.send(ext)
            if more is not None:
                g["due"].append(more)
    groups[0]["pout"].append(ring.core(groups[0]["out"][-1]))
    return groups


def flat(own, opp, g):
    return [own, opp, *g["ring"], *g["pring"], *g["out"], *g["pout"]]


def place_parts(ring, a, refs, put):
    n, m = ring.n, ring.half
    own, opp, refs = refs[0], refs[1], refs[2:]
    rings, prings, outs, pouts = (refs[i * m : (i + 1) * m] for i in range(4))

    def all_parts(step, ext, mid, mid0, other):
        s = ring.shard_back(step)
        put("mid", s, mid, mid0)
        put("ext", s, ext, 0)
        put("opp", s, other, 0)

    all_parts(0, own, own, a, opp)
    for h in range(1, m):
        all_parts(h, rings[h - 1], rings[h - 1], a, outs[h - 1])
        all_parts(n - h, prings[h - 1], prings[h - 1], a, pouts[h - 1])

    c = ring.here()[0]

    @pl.when(c == 0)
    def _():
        all_parts(m, rings[-1], prings[-1], 0, outs[-1])

    @pl.when(c == 1)
    def _():
        all_parts(m, prings[-1], rings[-1], 0, pouts[-1])


def ln_rows(x_ref, gain, bias, o_ref, rows=384):
    def step(i):
        at = span(i, rows)
        n, _ = normalized(x_ref[at, :].astype(F32))
        o_ref[at, :] = (n * gain + bias).astype(BF)

    loop(x_ref.shape[0] // rows, step)


def split_kernel(ring, t, jw, ow, first, opp, sems):
    width = ow.shape[1]
    rps = ow.shape[0]
    a = rps + t
    x = ring.here()[1]
    made = []

    def copy(src, dst):
        c = pltpu.make_async_copy(src, dst, sems.at[len(made)])
        c.start()
        made.append(c)

    def cols(side):
        return jw.at[:, pl.ds(pl.multiple_of(side * 2 * width, width), width)]

    copy(cols(x), first.at[pl.ds(0, rps), :])
    copy(jw.at[:, pl.ds(width, width)], first.at[pl.ds(a, rps), :])
    copy(ow.at[pl.ds(t, rps - 2 * t), :], first.at[pl.ds(a + rps, rps - 2 * t), :])
    copy(cols(1 - x), opp.at[pl.ds(0, rps), :])
    if t:
        copy(ow.at[pl.ds(pl.multiple_of(x * (rps - t), 16), t), :], first.at[pl.ds(rps, t), :])
        copy(ow.at[pl.ds(pl.multiple_of((1 - x) * (rps - t), 16), t), :], opp.at[pl.ds(rps, t), :])
    for c in made:
        c.wait()


def split_ff_kernel(ring, t, uw, dw, first, opp, sems):
    width = dw.shape[1]
    rps = uw.shape[0]
    a = rps + t
    x = ring.here()[1]
    made = []

    def copy(src, dst):
        c = pltpu.make_async_copy(src, dst, sems.at[len(made)])
        c.start()
        made.append(c)

    def cols(side):
        return uw.at[:, pl.ds(pl.multiple_of(side * width, width), width)]

    copy(cols(x), first.at[pl.ds(0, rps), :])
    copy(dw.at[pl.ds(t, 2 * rps - 2 * t), :], first.at[pl.ds(a, 2 * rps - 2 * t), :])
    copy(cols(1 - x), opp.at[pl.ds(0, rps), :])
    if t:
        copy(dw.at[pl.ds(pl.multiple_of(x * (2 * rps - t), 16), t), :], first.at[pl.ds(rps, t), :])
        copy(dw.at[pl.ds(pl.multiple_of((1 - x) * (2 * rps - t), 16), t), :], opp.at[pl.ds(rps, t), :])
    for c in made:
        c.wait()


def small_kernel(ring, *refs):
    parts, o_ref = refs[:-1], refs[-1]
    width = o_ref.shape[1]
    n, f = ring.n, ring.here()[2]
    row = 0
    o_ref[...] = jnp.zeros_like(o_ref)
    for part in parts:
        size = part.shape[0]
        full = size * n
        i = lax.broadcasted_iota(jnp.int32, (size, full), 0)
        j = lax.broadcasted_iota(jnp.int32, (size, full), 1)
        hot = jnp.where(j == i + f * size, 1.0, 0.0).astype(BF)
        placed = dot(jnp.broadcast_to(part[...].astype(F32)[None, :], (8, size)).astype(BF), hot)
        for k in range(full // width):
            o_ref[row : row + 1, :] = placed[0:1, k * width : (k + 1) * width]
            row += 1


def add_f32_kernel(a_ref, b_ref, o_ref):
    o_ref[...] = a_ref[...] + b_ref[...]


def ln_kernel(x_ref, small, o_ref):
    ln_rows(x_ref, small[pl.ds(GAIN1, 1), :], small[pl.ds(BIAS1, 1), :], o_ref)


def qkv_kernel(ring, a, t, first, small, *refs):
    refs, outs = refs[:-5], refs[-5:]
    proj, ws, wo = outs[:2], outs[2:4], outs[4]
    width = first.shape[1]
    rps = width // ring.n
    hw = width // 2
    xb = ring.here()[1]

    def put(part, s, ref, r0):
        row = pl.multiple_of(s * rps, rps)
        if part == "mid":
            for k in range(2):
                ws[k][pl.ds(row, rps), hw : 2 * hw] = ref[r0 : r0 + rps, k * hw : (k + 1) * hw]
            wo[pl.ds(pl.multiple_of(row + t, 16), rps - 2 * t), :] = ref[r0 + rps : r0 + 2 * rps - 2 * t, :]
        else:
            side = xb if part == "ext" else 1 - xb
            col = pl.multiple_of(side * 2 * hw, hw)
            for k in range(2):
                ws[k][pl.ds(row, rps), pl.ds(col, hw)] = ref[0:rps, k * hw : (k + 1) * hw]
            if t:
                wo[pl.ds(pl.multiple_of(row + side * (rps - t), 16), t), :] = ref[rps : rps + t, :]

    place_parts(ring, a, refs, put)
    for k in range(2):

        def tile(i, k=k):
            at = span(i, hw)
            v = dot(first[...], ws[k][:, at])
            use = jnp.where(i == 0, 1.0, 0.0), jnp.where(i == 2, 1.0, 0.0)
            shift = small[pl.ds(JB_Q, 1), k * hw : (k + 1) * hw] * use[0]
            shift = shift + small[pl.ds(JB_V, 1), k * hw : (k + 1) * hw] * use[1]
            proj[k][:, at] = (v + shift).astype(BF)

        loop(3, tile)


def mask(col_ids, row_ids, q0, k0, queries, keys):
    same = col_ids[pl.ds(k0, keys), :] == row_ids[:, pl.ds(q0, queries)]
    kpos = lax.broadcasted_iota(jnp.int32, (keys, queries), 0) + k0
    qpos = lax.broadcasted_iota(jnp.int32, (keys, queries), 1) + q0
    return jnp.where(same & (kpos <= qpos), 0.0, MASKED).astype(F32)


def soft(q, k, bias):
    s = dot_nt(k, q) * (HD ** (-0.5) * LOG2E) + bias
    p = jnp.exp2(s - jnp.max(s, axis=0, keepdims=True))
    return p * (1.0 / jnp.sum(p, axis=0, keepdims=True))


def head_cols(part, h):
    return slice((part * HALF + h) * HD, (part * HALF + h + 1) * HD)


def tiles(rows, queries, back):
    for q0 in range(0, rows, queries):
        lo = min(q0, back)
        yield q0, q0 - lo, queries + lo


def attend_kernel(proj_a, proj_b, col_ids, row_ids, o_ref):
    nq = 256
    for q0, k0, nk in tiles(o_ref.shape[0], nq, 128):
        at_q, at_k = slice(q0, q0 + nq), slice(k0, k0 + nk)
        bias = mask(col_ids, row_ids, q0, k0, nq, nk)
        for k, proj in enumerate((proj_a, proj_b)):
            for h in range(HALF):
                w = soft(proj[at_q, head_cols(0, h)], proj[at_k, head_cols(1, h)], bias).astype(BF)
                col = (k * HALF + h) * HD
                o_ref[at_q, col : col + HD] = dot_tn(w, proj[at_k, head_cols(2, h)]).astype(BF)


def out_kernel(att, wo, x_ref, small, middle, second):
    tn = 512

    def step(i):
        at = span(i, tn)
        middle[:, at] = x_ref[:, at].astype(F32) + dot(att[...], wo[:, at]) + small[pl.ds(OUT_B, 1), at]

    loop(wo.shape[1] // tn, step)
    ln_rows(middle, small[pl.ds(GAIN2, 1), :], small[pl.ds(BIAS2, 1), :], second)


def gelu_both(h):
    h2 = h * h
    half = 0.5 + 0.5 * jnp.tanh(h * (C0 + (C0 * 0.044715) * h2))
    act = h * half
    return act, half + act * (1.0 - half) * (2.0 * C0 + (6.0 * C0 * 0.044715) * h2)


def up_kernel(ring, a, t, second, small, *refs):
    refs, outs = refs[:-4], refs[-4:]
    active, slope, wu, wd = outs
    width = second.shape[1]
    rps = width // ring.n
    xb = ring.here()[1]

    def put(part, s, ref, r0):
        row = pl.multiple_of(s * rps, rps)
        drow = pl.multiple_of(s * 2 * rps, 2 * rps)
        if part == "mid":
            wd[pl.ds(pl.multiple_of(drow + t, 16), 2 * rps - 2 * t), :] = ref[r0 : r0 + 2 * rps - 2 * t, :]
        else:
            side = xb if part == "ext" else 1 - xb
            wu[pl.ds(row, rps), pl.ds(pl.multiple_of(side * width, width), width)] = ref[0:rps, :]
            if t:
                wd[pl.ds(pl.multiple_of(drow + side * (2 * rps - t), 16), t), :] = ref[rps : rps + t, :]

    place_parts(ring, a, refs, put)
    tn = 512
    per = width // tn

    def step(i):
        at = span(i, tn)
        shift = small[pl.ds(UP_B + i // per, 1), span(i % per, tn)]
        act, s = gelu_both(dot(second[...], wu[:, at]) + shift)
        active[:, at] = act.astype(BF)
        slope[:, at] = s.astype(BF)

    loop(2 * per, step)


def dact_kernel(og, wd, slope, o_ref):
    tn = 256

    def step(i):
        at = span(i, tn)
        o_ref[:, at] = (dot_nt(og[...], wd[at, :]) * slope[:, at].astype(F32)).astype(BF)

    loop(o_ref.shape[1] // tn, step)


def down_kernel(active, wd, middle, small, far, mark, o_ref, sems):
    tn = 256
    count = o_ref.shape[1] // tn

    def leave(i):
        at = span(i, tn)
        return pltpu.make_async_copy(o_ref.at[:, at], far.at[:, at], sems.at[i])

    def step(i):
        at = span(i, tn)
        o_ref[:, at] = (middle[:, at] + dot(active[...], wd[:, at]) + small[pl.ds(DOWN_B, 1), at]).astype(BF)
        leave(i).start()

    mark[...] = jnp.zeros_like(mark)
    loop(count, step)
    loop(count, lambda i: leave(i).wait())


def weight_grad_kernel(ring, tn, tl, left, right, buf, sent, sums):
    n, m = ring.n, ring.half
    half = left.shape[1] // n // 2
    slots = [ring.slot(j) for j in range(n)]
    swap = [jnp.where(k == m, ring.here()[0], 0) for k in slots]
    ones = jnp.ones((8, right.shape[0]), BF)
    per = tl // half

    def step(i):
        at = span(i, tn)
        r = right[:, at]
        sums[:, at] = dot(ones, r)
        for l in range(left.shape[1] // tl):
            v = dot_tn(left[:, l * tl : (l + 1) * tl], r).astype(BF)
            for s in range(per):
                j, q = divmod(l * per + s, 2)
                row = pl.multiple_of((2 * slots[j] + (swap[j] + q) % 2) * half, half)
                buf[pl.ds(row, half), at] = v[s * half : (s + 1) * half, :]
        sent[:, at] = buf[buf.shape[0] - sent.shape[0] :, at]

    loop(right.shape[1] // tn, step)


def norm_back(values, d, gain):
    n, r = normalized(values)
    g = d * gain
    t = r * (g - jnp.mean(g, axis=-1, keepdims=True) - n * jnp.mean(g * n, axis=-1, keepdims=True))
    return t, d * n


def group_sum(v):
    return jnp.sum(v.reshape(v.shape[0] // 8, 8, v.shape[1]), axis=0)


def dsecond_kernel(dh, wu, acc):
    tn = 256

    def step(i):
        at = span(i, tn)
        acc[:, at] = dot_nt(dh[...], wu[at, :])

    loop(acc.shape[1] // tn, step)


def second_norm_back_kernel(acc, wo, middle, og, small, dmid, dbranch, datt, sg, sb):
    g = small[pl.ds(GAIN2, 1), :]
    sg[...] = jnp.zeros_like(sg)
    sb[...] = jnp.zeros_like(sb)
    rows = 256

    def norm(i):
        at = span(i, rows)
        d = acc[at, :]
        t, dn = norm_back(middle[at, :], d, g)
        sg[...] += group_sum(dn)
        sb[...] += group_sum(d)
        v = og[at, :].astype(F32) + t
        dmid[at, :] = v
        dbranch[at, :] = v.astype(BF)

    loop(acc.shape[0] // rows, norm)
    tn = 256

    def back(i):
        at = span(i, tn)
        datt[:, at] = dot_nt(dbranch[...], wo[at, :]).astype(BF)

    loop(datt.shape[1] // tn, back)


def attend_back_kernel(part, proj, datt, col_ids, row_ids, o_ref, acc_k, acc_v):
    rows, hw = acc_k.shape
    scale = HD ** (-0.5)
    nq, back = 128, 64
    heads = range(HALF)
    acc_k[...] = jnp.zeros_like(acc_k)
    acc_v[...] = jnp.zeros_like(acc_v)

    def tile(q0, k0, nk):
        at_q, at_k = pl.ds(q0, nq), pl.ds(k0, nk)
        bias = mask(col_ids, row_ids, q0, k0, nq, nk)
        q = [proj[at_q, head_cols(0, h)] for h in heads]
        k = [proj[at_k, head_cols(1, h)] for h in heads]
        do = [datt[at_q, head_cols(part, h)] for h in heads]
        dw = [dot_nt(proj[at_k, head_cols(2, h)], do[h]) for h in heads]
        p = [soft(q[h], k[h], bias) for h in heads]
        for h in heads:
            acc_v[at_k, head_cols(0, h)] += dot(p[h].astype(BF), do[h])
        ds = [(p[h] * (dw[h] - jnp.sum(p[h] * dw[h], axis=0, keepdims=True))).astype(BF) for h in heads]
        for h in heads:
            acc_k[at_k, head_cols(0, h)] += dot(ds[h], q[h])
            o_ref[at_q, head_cols(0, h)] = (dot_tn(ds[h], k[h]) * scale).astype(BF)

    def step(i):
        for q0 in (pl.multiple_of(2 * i * nq, nq), pl.multiple_of((2 * i + 1) * nq, nq)):
            tile(q0, pl.multiple_of(jnp.maximum(q0 - back, 0), back), nq + back)

    loop(rows // nq // 2, step)
    o_ref[:, hw : 2 * hw] = (acc_k[...] * scale).astype(BF)
    o_ref[:, 2 * hw :] = acc_v[...].astype(BF)


def dfirst_kernel(da, db, wa, wb, acc):
    tn = 256

    def step(i):
        at = span(i, tn)
        acc[:, at] = dot_nt(da[...], wa[at, :]) + dot_nt(db[...], wb[at, :])

    loop(acc.shape[1] // tn, step)


def first_norm_back_kernel(acc, x_ref, dmid, small, far, sg, sb, o_ref, sems):
    g = small[pl.ds(GAIN1, 1), :]
    sg[...] = jnp.zeros_like(sg)
    sb[...] = jnp.zeros_like(sb)
    rows = 256
    count = x_ref.shape[0] // rows

    def leave(i):
        at = span(i, rows)
        return pltpu.make_async_copy(o_ref.at[at, :], far.at[at, :], sems.at[i])

    def norm(i):
        at = span(i, rows)
        d = acc[at, :]
        t, dn = norm_back(x_ref[at, :].astype(F32), d, g)
        sg[...] += group_sum(dn)
        sb[...] += group_sum(d)
        o_ref[at, :] = (dmid[at, :] + t).astype(BF)
        leave(i).start()

    loop(count, norm)
    loop(count, lambda i: leave(i).wait())


def small_grads_kernel(ring, sizes, sg1, sb1, ja, jb, so, sg2, sb2, su, sd, buf, sent):
    n, m = ring.n, ring.half
    hw = ja.shape[1] // 3
    rows = buf.shape[0] // n

    def whole(ref):
        return jnp.sum(ref[...], axis=0, keepdims=True)

    queries = jnp.concatenate([ja[0:1, 0:hw], jb[0:1, 0:hw]], axis=1)
    values = jnp.concatenate([ja[0:1, 2 * hw :], jb[0:1, 2 * hw :]], axis=1)
    vectors = [
        whole(sg1), whole(sb1), jnp.concatenate([queries, values], axis=1), so[0:1, :],
        whole(sg2), whole(sb2), su[0:1, :], sd[0:1, :],
    ]
    buf[...] = jnp.zeros_like(buf)
    c = ring.here()[0]
    for j in range(n):
        slot = ring.slot(j)
        top = pl.multiple_of((2 * slot + jnp.where(slot == m, c, 0)) * (rows // 2), rows // 2)
        for size in sorted(set(sizes)):
            parts = [v[:, j * size : (j + 1) * size] for v, k in zip(vectors, sizes) if k == size]
            parts.append(jnp.zeros((rows // 2 - len(parts), size), F32))
            block = jnp.concatenate(parts, axis=0).astype(BF)
            at = 0 if size == min(sizes) else SMALL_COL
            buf[pl.ds(top, rows // 2), at : at + size] = block
    sent[...] = buf[buf.shape[0] - sent.shape[0] :, :]


class Grads:
    def __init__(self, n, bufs, recvs, width):
        self.bufs, self.recvs, self.width = bufs, recvs, width
        self.sizes = [(b.shape[0] // n, b.shape[1] // width) for b in bufs]
        self.rows = sum(r * c for r, c in self.sizes)


def reduce_step(ring, gr, k, got):
    m, n = ring.half, ring.n
    width = gr.width
    half = k == m
    total = gr.rows // 2 if half else gr.rows
    args = [*gr.bufs, *gr.recvs] + ([got] if got is not None else [])
    nb = len(gr.bufs)

    def body(*refs):
        bs, rs = refs[:nb], refs[nb : 2 * nb]
        g = refs[2 * nb] if got is not None else None
        o = refs[-1]
        c = ring.here()[0]
        at, gat = 0, 0
        for b, rv, (r, cs) in zip(bs, rs, gr.sizes):
            h = r // 2
            for j in range(cs):
                col = slice(j * width, (j + 1) * width)
                if half:
                    v = b[m * r : m * r + h, col].astype(F32) + rv[0:h, col].astype(F32)
                    o[at : at + h, :] = v.astype(BF)
                    at += h
                else:
                    base = h + (n - k - m - 1) * r
                    v = b[k * r : (k + 1) * r, col].astype(F32) + rv[base : base + r, col].astype(F32)
                    if g.shape[0] == total:
                        o[at : at + r, :] = (v + g[at : at + r, :].astype(F32)).astype(BF)
                    else:
                        top = jnp.where(c == 0, 1.0, 0.0)
                        gv = g[gat : gat + h, :].astype(F32)
                        o[at : at + h, :] = (v[:h] + gv * top).astype(BF)
                        o[at + h : at + r, :] = (v[h:] + gv * (1.0 - top)).astype(BF)
                        gat += h
                    at += r

    return body, [out((total, width), BF)], args


def owner_sum(ring, gr, got):
    nb = len(gr.bufs)

    def body(*refs):
        bs, g, keep, send = refs[:nb], refs[nb], refs[nb + 1], refs[nb + 2]
        c = ring.here()[0]
        at, to = 0, 0
        for b, (r, cs) in zip(bs, gr.sizes):
            h = r // 2
            for j in range(cs):
                v = b[0:r, j * gr.width : (j + 1) * gr.width].astype(F32) + g[at : at + r, :].astype(F32)
                v = v.astype(BF)
                keep[to : to + h, :] = jnp.where(c == 0, v[:h], v[h:])
                send[to : to + h, :] = jnp.where(c == 0, v[h:], v[:h])
                at += r
                to += h

    o = out((gr.rows // 2, gr.width), BF)
    return body, [o, o], [*gr.bufs, got]


def add_kernel(a_ref, b_ref, o_ref):
    o_ref[...] = (a_ref[...].astype(F32) + b_ref[...].astype(F32)).astype(o_ref.dtype)


def add2(a, b):
    return add_kernel, [out(a.shape, a.dtype)], [a, b]


def reduce_group(ring, gr):
    got = None
    for k in range(ring.half, 0, -1):
        (part,) = yield reduce_step(ring, gr, k, got)
        got = ring.along(part)
    keep, send = yield owner_sum(ring, gr, got)
    (u,) = yield add2(keep, ring.core(send))
    bit = 2
    while bit < ring.reps:
        (u,) = yield add2(u, ring.send(u, lambda r, f, bit=bit: (r ^ bit, f)))
        bit *= 2
    return u, ring.core(u)


class Rounds:
    def __init__(self, line):
        self.line = line
        self.long = False
        self.live = {}
        self.jobs = {}
        self.done = {}

    def _advance(self, name, results):
        try:
            self.jobs[name] = next(self.live[name]) if results is None else self.live[name].send(results)
        except StopIteration as stop:
            self.done[name] = stop.value
            del self.live[name]
            self.jobs.pop(name, None)

    def add(self, name, chain):
        self.live[name] = chain
        self._advance(name, None)

    def turn(self, *names):
        names = [k for k in names or self.jobs if k in self.jobs]
        if not names:
            return
        jobs = [self.jobs[k] for k in names]
        args = [a for _, _, given in jobs for a in given]
        outs = [o for _, made, _ in jobs for o in made]

        def body(*refs):
            i, j = 0, len(args)
            for run, made, given in jobs:
                run(*refs[i : i + len(given)], *refs[j : j + len(made)])
                i, j = i + len(given), j + len(made)

        got = list(self.line.call(body, outs, args, long=self.long, name="sums"))
        for name, (_, made, _) in zip(names, jobs):
            self._advance(name, got[: len(made)])
            got = got[len(made) :]


def join_halves(c, parts, sizes, width, place):
    a_ref, b_ref = parts
    to = 0
    for i, (r, cs) in enumerate(sizes):
        h = r // 2
        for j in range(cs):
            a = a_ref[to : to + h, :].astype(F32)
            b = b_ref[to : to + h, :].astype(F32)
            place(i, slice(0, h), j, jnp.where(c == 0, a, b))
            place(i, slice(h, r), j, jnp.where(c == 0, b, a))
            to += h


def last_sum(job):
    return (yield job)


def finish(ring, gr, parts):
    def body(a_ref, b_ref, *outs):
        def place(i, rows, j, v):
            outs[i][rows, j * gr.width : (j + 1) * gr.width] = v

        join_halves(ring.here()[0], (a_ref, b_ref), gr.sizes, gr.width, place)

    return body, [out((r, cs * gr.width), F32) for r, cs in gr.sizes], list(parts)


def finish_joint(ring, gr_a, gr_b, parts_a, parts_b, sizes):
    (r, cs), (_, ocs), width = *gr_a.sizes, gr_a.width

    def body(a1, a2, b1, b2, o, o2, small, *outs):
        for k, pair in enumerate(((a1, a2), (b1, b2))):
            def place(i, rows, j, v, k=k):
                if i == 0:
                    at = (2 * j + k) * width
                    o[rows, at : at + width] = v
                elif k == 0:
                    o2[rows, j * width : (j + 1) * width] = v
                else:
                    small[rows, :] = v

            join_halves(ring.here()[0], pair, (gr_a, gr_b)[k].sizes, width, place)
        row = {}
        for size, got in zip(sizes, outs):
            k = row.setdefault(size, 0)
            row[size] += 1
            at = 0 if size == min(sizes) else SMALL_COL
            got[...] = small[k : k + 1, at : at + size]

    outs = [out((r, 2 * cs * width), F32), out((r, ocs * width), F32), out((SMALL_SHARD, width), F32)] + [out((1, k), F32) for k in sizes]
    return body, outs, [*parts_a, *parts_b]


def step_fn(mesh):
    ring = Ring(mesh)
    n, m = ring.n, ring.half

    def on_device(
        layer_input, item_ids, norm_gain, norm_bias, joint_weight, joint_bias, out_weight, out_bias,
        second_gain, second_bias, up_weight, up_bias, down_weight, down_bias, output_grad,
    ):
        rows, width = layer_input.shape
        ff = up_weight.shape[1]
        hw = width // 2
        rps = width // n
        t = (rps // 4) // 16 * 16
        a, b = rps + t, 2 * rps - 2 * t
        dma = pltpu.SemaphoreType.DMA
        shapes = [out((a + b, width), BF), out((a, width), BF)]
        line = Line()
        first1, opp1 = line.call(
            functools.partial(split_kernel, ring, t), shapes, [joint_weight, out_weight],
            far=(0, 1), scratch=[dma((6,))], name="split",
        )
        ids = [item_ids[:, None], item_ids[None, :]]
        first2, opp2 = line.call(
            functools.partial(split_ff_kernel, ring, t), shapes, [up_weight, down_weight], deps=ids,
            far=(0, 1), scratch=[dma((5,))], name="split_ff",
        )
        vectors = (norm_gain, norm_bias, joint_bias, out_bias, second_gain, second_bias, up_bias, down_bias)
        shared = {}

        def small_parts():
            (small,) = line.call(
                functools.partial(small_kernel, ring), [out((SMALL_ROWS, width), F32)], vectors, name="small",
            )
            mark = yield
            bit = 1
            while bit < n:
                other = ring.send(small, lambda r, f, bit=bit: (r, f ^ bit))
                yield (small if bit > 1 else None)
                mark = yield
                (small,) = kernel_call(add_f32_kernel, [out(small.shape, F32)], [small, other], deps=[mark], name="small_sum")
                bit *= 2
            shared["small"] = small
            (shared["first"],) = kernel_call(
                ln_kernel, [out((rows, width), BF)], [layer_input, small], deps=[mark], name="first_norm",
            )
            mark = yield shared["first"]
            while True:
                yield

        extras = small_parts()
        next(extras)
        g1, g2 = gather(ring, [first1, first2], a, extras)
        small, first = shared["small"], shared["first"]

        args = [first, small, *flat(first1, opp1, g1)]
        halves = [out((rows, 3 * hw), BF)] * 2
        proj_a, proj_b, wa, wb, wo = line.call(
            functools.partial(qkv_kernel, ring, a, t),
            halves + [out((width, 3 * hw), BF)] * 2 + [out((width, width), BF)],
            args, name="projection",
        )
        g2["out"][-1], wo = there_first(g2["out"][-1], wo)
        g2["pout"].append(ring.core(g2["out"][-1]))
        (attended,) = line.call(attend_kernel, [out((rows, width), BF)], [proj_a, proj_b, *ids], name="attend")
        middle, second = line.call(
            out_kernel, [out((rows, width), F32), out((rows, width), BF)],
            [attended, wo, layer_input, small], name="out_projection",
        )
        args = [second, small, *flat(first2, opp2, g2)]
        active, slope, wu, wd = line.call(
            functools.partial(up_kernel, ring, a, t),
            [out((rows, ff), BF), out((rows, ff), BF), out((width, ff), BF), out((ff, width), BF)],
            args, name="up_projection",
        )

        def weight_grad(l, r, tl=512, tn=512, name=None):
            kl, kr = l.shape[1], r.shape[1]
            kept = m * (kl // n) + kl // n // 2
            buf, sent, sums = line.call(
                functools.partial(weight_grad_kernel, ring, tn, tl),
                [out((kl, kr), BF), out((kl - kept, kr), BF), out((8, kr), F32)], [l, r], name=name,
            )
            return buf, ring.core(sent), sums

        rounds = Rounds(line)

        def begin(name, bufs, recvs, w):
            gr = Grads(n, bufs, recvs, w)
            rounds.add(name, reduce_group(ring, gr))
            return gr

        down_buf, down_recv, s_down = weight_grad(active, output_grad, name="down_grad")
        (dhidden,) = line.call(
            dact_kernel, [out((rows, ff), BF)], [output_grad, wd, slope], name="hidden_grad",
        )
        gr_down = begin("down", [down_buf], [down_recv], width)
        rounds.turn("down")
        up_buf, up_recv, s_up = weight_grad(second, dhidden, name="up_grad")
        rounds.turn("down")
        (dsecond,) = line.call(dsecond_kernel, [out((rows, width), F32)], [dhidden, wu], name="dsecond")
        gr_up = begin("up", [up_buf], [up_recv], width)
        rounds.turn("up")
        dmid, dbranch, datt, sg2, sb2 = line.call(
            second_norm_back_kernel,
            [out((rows, width), F32), out((rows, width), BF), out((rows, width), BF), out((8, width), F32), out((8, width), F32)],
            [dsecond, wo, middle, output_grad, small], name="second_norm_grad",
        )
        rounds.turn("down")
        out_buf, out_recv, s_out = weight_grad(attended, dbranch, name="out_grad")
        rounds.turn("up")

        def attend_back(part, proj):
            return line.call(
                functools.partial(attend_back_kernel, part), [out((rows, 3 * hw), BF)], [proj, datt, *ids],
                scratch=[VM((rows, hw), F32), VM((rows, hw), F32)], name="attend_grad",
            )[0]

        da = attend_back(0, proj_a)
        rounds.turn("down")
        ja_buf, ja_recv, s_ja = weight_grad(first, da, name="joint_grad")
        rounds.turn("up")
        db = attend_back(1, proj_b)
        gr_ja = begin("ja", [ja_buf, out_buf], [ja_recv, out_recv], hw)
        rounds.turn("ja", "down")
        jb_buf, jb_recv, s_jb = weight_grad(first, db, name="joint_grad")
        rounds.turn("up")
        (dfirst,) = line.call(dfirst_kernel, [out((rows, width), F32)], [da, db, wa, wb], name="dfirst")
        rounds.turn("ja")
        input_grad, sg1, sb1 = line.call(
            first_norm_back_kernel, [out((rows, width), BF), out((8, width), F32), out((8, width), F32)],
            [dfirst, layer_input, dmid, small], straight=(0,),
            scratch=[VM((rows, width), BF), dma((rows // 256,))], name="first_norm_grad",
        )
        small_sizes = [v.shape[0] for v in vectors]
        small_kept = m * SMALL_SHARD + SMALL_SHARD // 2
        small_buf, small_sent = line.call(
            functools.partial(small_grads_kernel, ring, small_sizes),
            [out((n * SMALL_SHARD, hw), BF), out((n * SMALL_SHARD - small_kept, hw), BF)],
            [sg1, sb1, s_ja, s_jb, s_out, sg2, sb2, s_up, s_down], long=False, name="small_grads",
        )
        gr_jb = begin("jb", [jb_buf, small_buf], [jb_recv, ring.core(small_sent)], hw)
        rounds.turn("jb", "down")
        rounds.long = True
        rounds.turn("ja", "up")
        done, ready = rounds.done, set()
        pairs = ("jb", "up", "got up"), ("ja", "down", "got down")
        k = 0
        while rounds.jobs:
            if k == m + 1:
                rounds.long = False
                layer_output, _ = line.call(
                    down_kernel, [out((rows, width), BF), out((8, 128), F32)], [active, wd, middle, small],
                    straight=(0,), scratch=[VM((rows, width), BF), dma((width // 256,))], name="down_projection",
                )
            rounds.turn(*(pairs[k % 2] if k < m else ()))
            k += 1
            for name, gr in (("down", gr_down), ("up", gr_up)):
                if name in done and name not in ready:
                    ready.add(name)
                    rounds.add("got " + name, last_sum(finish(ring, gr, done[name])))
            if "ja" in done and "jb" in done and "joint" not in ready:
                ready.add("joint")
                rounds.add("got joint", last_sum(finish_joint(ring, gr_ja, gr_jb, done["ja"], done["jb"], small_sizes)))
        (g_down,), (g_up,), (g_joint, g_out, _, *v) = (done["got " + k] for k in ("down", "up", "joint"))
        v = [k.reshape(-1) for k in v]
        return (
            layer_output, input_grad, v[0], v[1], g_joint, v[2], g_out, v[3], v[4], v[5], g_up, v[6], g_down, v[7],
        )

    return on_device


def solution(mesh):
    row, vecs, mat = P(("rep", "fsdp"), None), P("fsdp"), P("fsdp", None)
    placed = (
        row, P(("rep", "fsdp")), vecs, vecs, mat, vecs, mat, vecs, vecs, vecs, mat, vecs, mat, vecs, row,
    )
    return jax.shard_map(
        step_fn(mesh),
        mesh=mesh,
        in_specs=placed,
        out_specs=(row, row, vecs, vecs, mat, vecs, mat, vecs, vecs, vecs, mat, vecs, mat, vecs),
        check_vma=False,
    )
```

```python
import functools
import math

import jax
import jax.numpy as jnp
from jax import lax
from jax.experimental import pallas as pl
from jax.experimental.pallas import tpu as pltpu
from jax.sharding import PartitionSpec as P

H = 8
HD = 128
HALF = H // 2
EPS = 1e-05
MASKED = -1e30
LOG2E = 1.4426950408889634
C0 = math.sqrt(2.0 / math.pi)
BF = jnp.bfloat16
F32 = jnp.float32
VM = pltpu.VMEM
MAIN = 60 * 10**9
MIB = 2**20

GAIN1, BIAS1, JB_Q, JB_V, OUT_B, GAIN2, BIAS2, UP_B, DOWN_B = 0, 1, 2, 3, 4, 5, 6, 7, 9
SMALL_ROWS = 16
SMALL_SHARD, SMALL_COL = 32, 256


def nbytes(a):
    return math.prod(a.shape) * jnp.dtype(a.dtype).itemsize


def kernel_call(body, outs, args, deps=(), smem=(), anys=(), far=(), scratch=(), straight=(), extra=4, long=True, name=None):
    own = sum(nbytes(s) for s in scratch if getattr(s, "dtype", None) in (BF, F32))
    count, made = len(args), len(outs)
    deps = [d for d in deps if d is not None]

    def space(i):
        return pl.ANY if i in anys else pltpu.HBM if i in far else pltpu.SMEM if i in smem else VM

    args = [pltpu.with_memory_space_constraint(v, pltpu.HBM) if i in far else v for i, v in enumerate(args)]

    def run(*refs):
        body(*refs[:count], *refs[count + len(deps) :])

    return pl.pallas_call(
        run,
        out_shape=[pltpu.HBM(o.shape, o.dtype) if i in straight else o for i, o in enumerate(outs)],
        in_specs=[pl.BlockSpec(memory_space=space(i)) for i in range(count)]
        + [pl.BlockSpec(memory_space=pl.ANY) for _ in deps],
        out_specs=[pl.BlockSpec(memory_space=pltpu.HBM if i in straight else VM) for i in range(len(outs))],
        scratch_shapes=list(scratch),
        compiler_params=pltpu.CompilerParams(vmem_limit_bytes=own + int(extra * MIB)),
        cost_estimate=pl.CostEstimate(flops=MAIN if long else 0, bytes_accessed=0, transcendentals=0),
        name=name,
    )(*args, *deps)


def out(shape, dtype):
    return jax.ShapeDtypeStruct(shape, dtype)


class Line:
    def __init__(self):
        self.mark = None

    def call(self, body, outs, args, deps=(), **kw):
        made = kernel_call(body, outs, args, deps=(self.mark, *deps), **kw)
        self.mark = min(made, key=nbytes)
        return made


def dot(a, b):
    return jnp.dot(a, b, preferred_element_type=F32)


def dot_tn(a, b):
    return lax.dot_general(a, b, (((0,), (0,)), ((), ())), preferred_element_type=F32)


def dot_nt(a, b):
    return lax.dot_general(a, b, (((1,), (1,)), ((), ())), preferred_element_type=F32)


def loop(count, step):
    lax.fori_loop(0, count, lambda i, z: (step(i), z)[1], 0)


def span(i, size):
    return pl.ds(pl.multiple_of(i * size, size), size)


def normalized(values):
    center = values - jnp.mean(values, axis=-1, keepdims=True)
    spread = jnp.mean(center * center, axis=-1, keepdims=True)
    factor = lax.rsqrt(spread + EPS)
    return center * factor, factor


class Ring:
    def __init__(self, mesh):
        self.axes = ("rep", "fsdp")
        self.n = mesh.shape["fsdp"]
        self.reps = mesh.shape["rep"]
        n = self.n
        self.order = list(range(0, n, 2)) + list(range(n - 1, 0, -2))
        self.place = [self.order.index(f) for f in range(n)]
        self.half = n // 2

    def send(self, v, target, keep=lambda r, f: True):
        n = self.n
        pairs = []
        for r in range(self.reps):
            for f in range(n):
                if keep(r, f):
                    r2, f2 = target(r, f)
                    pairs.append((r * n + f, r2 * n + f2))
        return lax.ppermute(v, self.axes, pairs)

    def along(self, v):
        def target(r, f):
            step = 1 if r % 2 == 0 else -1
            return r, self.order[(self.place[f] + step) % self.n]

        return self.send(v, target)

    def core(self, v):
        return self.send(v, lambda r, f: (r ^ 1, f))

    def across(self, v, keep=lambda r, f: True):
        return self.send(v, lambda r, f: (r ^ 2, f), keep)

    def here(self):
        r = lax.axis_index("rep")
        return r % 2, (r // 2) % 2, lax.axis_index("fsdp")

    def own_place(self):
        n, (c, _, f) = self.n, self.here()
        return jnp.where(f % 2 == 0, f // 2, n - 1 - f // 2), 1 - 2 * c

    def shard_back(self, h):
        n, (p, d) = self.n, self.own_place()
        q = lax.rem(p - d * h + 2 * n, n)
        return jnp.where(q < n // 2, 2 * q, 2 * (n - 1 - q) + 1)

    def slot(self, j):
        n, (p, d) = self.n, self.own_place()
        return lax.rem((self.place[j] - p) * d + n, n)


def cut_kernel(a, v, ext, *more):
    ext[...] = v[0:a, :]
    if more:
        more[0][...] = v[...]


def last_kernel(ring, a, v, other, o_ref):
    half = (v.shape[0] - a) // 2

    @pl.when(ring.here()[0] == 0)
    def _():
        o_ref[...] = v[0 : a + half, :]

    @pl.when(ring.here()[0] == 1)
    def _():
        o_ref[0:a, :] = other[...]
        o_ref[a:, :] = v[a + half :, :]


def there_first(x, other):
    return lax.optimization_barrier((x, other))


def gather(ring, firsts, a, extras):
    m = ring.half
    b, width = firsts[0].shape[0] - a, firsts[0].shape[1]
    groups = [dict(ring=[], out=[], pring=[], pout=[], due=[]) for _ in firsts]
    for h in range(1, m + 1):
        for i, g in enumerate(groups):
            if h == 1:
                g["ring"].append(ring.along(firsts[i]))
                continue
            v = g["ring"][-1]
            shapes = [out((a, width), BF)] + ([out(v.shape, BF)] if h < m else [])
            x = list(kernel_call(functools.partial(cut_kernel, a), shapes, [v], deps=g["due"], name="cut"))
            if h > 2:
                x[-1], g["out"][-1] = there_first(x[-1], g["out"][-1])
                g["pout"].append(ring.core(g["out"][-1]))
            if h < m:
                g["ring"].append(ring.along(x[1]))
            g["due"] = [ring.across(x[0]), ring.core(v)] + g["pout"][-1:]
            g["out"].append(g["due"][0])
            g["pring"].append(g["due"][1])
            more = extras.send(x[0])
            if more is not None:
                g["due"].append(more)
    more = None
    for i, g in enumerate(groups):
        (part,) = kernel_call(
            functools.partial(last_kernel, ring, a), [out((a + b // 2, width), BF)], [g["ring"][-1], g["out"][-1]],
            deps=[more], name="last",
        )
        g["ring"].append(ring.along(part))
        g["pout"].append(ring.core(g["out"][-1]))
        more = extras.send(part)
    groups[0]["pring"].append(ring.core(groups[0]["ring"][-1]))
    return groups


def flat(own, opp, g):
    return [own, opp, *g["ring"], *g["pring"], *g["out"], *g["pout"]]


def place_parts(ring, a, refs, middle, put):
    n, m = ring.n, ring.half
    own, opp, refs = refs[0], refs[1], refs[2:]
    rings, prings = refs[:m], refs[m : 2 * m]
    outs, pouts = refs[2 * m : 3 * m - 1], refs[3 * m - 1 :]

    def all_parts(step, ext, mid, mid0, other):
        s = ring.shard_back(step)
        put("mid", s, mid, mid0)
        put("ext", s, ext, 0)
        put("opp", s, other, 0)

    all_parts(0, own, own, a, opp)
    for h in range(1, m):
        all_parts(h, rings[h - 1], rings[h - 1], a, outs[h - 1])
        all_parts(n - h, prings[h - 1], prings[h - 1], a, pouts[h - 1])
    half = middle.shape[0] // 2

    def last(low, high):
        middle[0:half, :] = low[a:, :]
        middle[half:, :] = high[a:, :]
        all_parts(m, low, middle, 0, high)

    c = ring.here()[0]

    @pl.when(c == 0)
    def _():
        last(rings[-1], prings[-1])

    @pl.when(c == 1)
    def _():
        last(prings[-1], rings[-1])


def ln_rows(x_ref, gain, bias, o_ref, rows=384):
    def step(i):
        at = span(i, rows)
        n, _ = normalized(x_ref[at, :].astype(F32))
        o_ref[at, :] = (n * gain + bias).astype(BF)

    loop(x_ref.shape[0] // rows, step)


def split_kernel(ring, t, jw, ow, first, opp, sems):
    width = ow.shape[1]
    rps = ow.shape[0]
    a = rps + t
    x = ring.here()[1]
    made = []

    def copy(src, dst):
        c = pltpu.make_async_copy(src, dst, sems.at[len(made)])
        c.start()
        made.append(c)

    def cols(side):
        return jw.at[:, pl.ds(pl.multiple_of(side * 2 * width, width), width)]

    copy(cols(x), first.at[pl.ds(0, rps), :])
    copy(jw.at[:, pl.ds(width, width)], first.at[pl.ds(a, rps), :])
    copy(ow.at[pl.ds(t, rps - 2 * t), :], first.at[pl.ds(a + rps, rps - 2 * t), :])
    copy(cols(1 - x), opp.at[pl.ds(0, rps), :])
    if t:
        copy(ow.at[pl.ds(pl.multiple_of(x * (rps - t), 16), t), :], first.at[pl.ds(rps, t), :])
        copy(ow.at[pl.ds(pl.multiple_of((1 - x) * (rps - t), 16), t), :], opp.at[pl.ds(rps, t), :])
    for c in made:
        c.wait()


def split_ff_kernel(ring, t, uw, dw, first, opp, sems):
    width = dw.shape[1]
    rps = uw.shape[0]
    a = rps + t
    x = ring.here()[1]
    made = []

    def copy(src, dst):
        c = pltpu.make_async_copy(src, dst, sems.at[len(made)])
        c.start()
        made.append(c)

    def cols(side):
        return uw.at[:, pl.ds(pl.multiple_of(side * width, width), width)]

    copy(cols(x), first.at[pl.ds(0, rps), :])
    copy(dw.at[pl.ds(t, 2 * rps - 2 * t), :], first.at[pl.ds(a, 2 * rps - 2 * t), :])
    copy(cols(1 - x), opp.at[pl.ds(0, rps), :])
    if t:
        copy(dw.at[pl.ds(pl.multiple_of(x * (2 * rps - t), 16), t), :], first.at[pl.ds(rps, t), :])
        copy(dw.at[pl.ds(pl.multiple_of((1 - x) * (2 * rps - t), 16), t), :], opp.at[pl.ds(rps, t), :])
    for c in made:
        c.wait()


def small_kernel(ring, *refs):
    parts, o_ref = refs[:-1], refs[-1]
    width = o_ref.shape[1]
    n, f = ring.n, ring.here()[2]
    row = 0
    o_ref[...] = jnp.zeros_like(o_ref)
    for part in parts:
        size = part.shape[0]
        full = size * n
        i = lax.broadcasted_iota(jnp.int32, (size, full), 0)
        j = lax.broadcasted_iota(jnp.int32, (size, full), 1)
        hot = jnp.where(j == i + f * size, 1.0, 0.0).astype(BF)
        placed = dot(jnp.broadcast_to(part[...].astype(F32)[None, :], (8, size)).astype(BF), hot)
        for k in range(full // width):
            o_ref[row : row + 1, :] = placed[0:1, k * width : (k + 1) * width]
            row += 1


def add_f32_kernel(a_ref, b_ref, o_ref):
    o_ref[...] = a_ref[...] + b_ref[...]


def ln_kernel(x_ref, small, o_ref):
    ln_rows(x_ref, small[pl.ds(GAIN1, 1), :], small[pl.ds(BIAS1, 1), :], o_ref)


def qkv_kernel(ring, a, t, first, small, *refs):
    refs, outs, middle = refs[:-6], refs[-6:-1], refs[-1]
    proj, ws, wo = outs[:2], outs[2:4], outs[4]
    width = first.shape[1]
    rps = width // ring.n
    hw = width // 2
    xb = ring.here()[1]

    def put(part, s, ref, r0):
        row = pl.multiple_of(s * rps, rps)
        if part == "mid":
            for k in range(2):
                ws[k][pl.ds(row, rps), hw : 2 * hw] = ref[r0 : r0 + rps, k * hw : (k + 1) * hw]
            wo[pl.ds(pl.multiple_of(row + t, 16), rps - 2 * t), :] = ref[r0 + rps : r0 + 2 * rps - 2 * t, :]
        else:
            side = xb if part == "ext" else 1 - xb
            col = pl.multiple_of(side * 2 * hw, hw)
            for k in range(2):
                ws[k][pl.ds(row, rps), pl.ds(col, hw)] = ref[0:rps, k * hw : (k + 1) * hw]
            if t:
                wo[pl.ds(pl.multiple_of(row + side * (rps - t), 16), t), :] = ref[rps : rps + t, :]

    place_parts(ring, a, refs, middle, put)
    for k in range(2):

        def tile(i, k=k):
            at = span(i, hw)
            v = dot(first[...], ws[k][:, at])
            use = jnp.where(i == 0, 1.0, 0.0), jnp.where(i == 2, 1.0, 0.0)
            shift = small[pl.ds(JB_Q, 1), k * hw : (k + 1) * hw] * use[0]
            shift = shift + small[pl.ds(JB_V, 1), k * hw : (k + 1) * hw] * use[1]
            proj[k][:, at] = (v + shift).astype(BF)

        loop(3, tile)


def mask(col_ids, row_ids, q0, k0, queries, keys):
    same = col_ids[pl.ds(k0, keys), :] == row_ids[:, pl.ds(q0, queries)]
    kpos = lax.broadcasted_iota(jnp.int32, (keys, queries), 0) + k0
    qpos = lax.broadcasted_iota(jnp.int32, (keys, queries), 1) + q0
    return jnp.where(same & (kpos <= qpos), 0.0, MASKED).astype(F32)


def soft(q, k, bias):
    s = dot_nt(k, q) * (HD ** (-0.5) * LOG2E) + bias
    p = jnp.exp2(s - jnp.max(s, axis=0, keepdims=True))
    return p * (1.0 / jnp.sum(p, axis=0, keepdims=True))


def head_cols(part, h):
    return slice((part * HALF + h) * HD, (part * HALF + h + 1) * HD)


def tiles(rows, queries, back):
    for q0 in range(0, rows, queries):
        lo = min(q0, back)
        yield q0, q0 - lo, queries + lo


def attend_kernel(proj_a, proj_b, col_ids, row_ids, o_ref):
    nq = 256
    for q0, k0, nk in tiles(o_ref.shape[0], nq, 128):
        at_q, at_k = slice(q0, q0 + nq), slice(k0, k0 + nk)
        bias = mask(col_ids, row_ids, q0, k0, nq, nk)
        for k, proj in enumerate((proj_a, proj_b)):
            for h in range(HALF):
                w = soft(proj[at_q, head_cols(0, h)], proj[at_k, head_cols(1, h)], bias).astype(BF)
                col = (k * HALF + h) * HD
                o_ref[at_q, col : col + HD] = dot_tn(w, proj[at_k, head_cols(2, h)]).astype(BF)


def out_kernel(att, wo, x_ref, small, middle, second):
    tn = 512

    def step(i):
        at = span(i, tn)
        middle[:, at] = x_ref[:, at].astype(F32) + dot(att[...], wo[:, at]) + small[pl.ds(OUT_B, 1), at]

    loop(wo.shape[1] // tn, step)
    ln_rows(middle, small[pl.ds(GAIN2, 1), :], small[pl.ds(BIAS2, 1), :], second)


def gelu_both(h):
    h2 = h * h
    half = 0.5 + 0.5 * jnp.tanh(h * (C0 + (C0 * 0.044715) * h2))
    act = h * half
    return act, half + act * (1.0 - half) * (2.0 * C0 + (6.0 * C0 * 0.044715) * h2)


def up_kernel(ring, a, t, second, small, *refs):
    refs, outs, middle = refs[:-5], refs[-5:-1], refs[-1]
    active, slope, wu, wd = outs
    width = second.shape[1]
    rps = width // ring.n
    xb = ring.here()[1]

    def put(part, s, ref, r0):
        row = pl.multiple_of(s * rps, rps)
        drow = pl.multiple_of(s * 2 * rps, 2 * rps)
        if part == "mid":
            wd[pl.ds(pl.multiple_of(drow + t, 16), 2 * rps - 2 * t), :] = ref[r0 : r0 + 2 * rps - 2 * t, :]
        else:
            side = xb if part == "ext" else 1 - xb
            wu[pl.ds(row, rps), pl.ds(pl.multiple_of(side * width, width), width)] = ref[0:rps, :]
            if t:
                wd[pl.ds(pl.multiple_of(drow + side * (2 * rps - t), 16), t), :] = ref[rps : rps + t, :]

    place_parts(ring, a, refs, middle, put)
    tn = 512
    per = width // tn

    def step(i):
        at = span(i, tn)
        shift = small[pl.ds(UP_B + i // per, 1), span(i % per, tn)]
        act, s = gelu_both(dot(second[...], wu[:, at]) + shift)
        active[:, at] = act.astype(BF)
        slope[:, at] = s.astype(BF)

    loop(2 * per, step)


def dact_kernel(og, wd, slope, o_ref):
    tn = 256

    def step(i):
        at = span(i, tn)
        o_ref[:, at] = (dot_nt(og[...], wd[at, :]) * slope[:, at].astype(F32)).astype(BF)

    loop(o_ref.shape[1] // tn, step)


def down_kernel(active, wd, middle, small, far, mark, o_ref, sems):
    tn = 256
    count = o_ref.shape[1] // tn

    def leave(i):
        at = span(i, tn)
        return pltpu.make_async_copy(o_ref.at[:, at], far.at[:, at], sems.at[i])

    def step(i):
        at = span(i, tn)
        o_ref[:, at] = (middle[:, at] + dot(active[...], wd[:, at]) + small[pl.ds(DOWN_B, 1), at]).astype(BF)
        leave(i).start()

    mark[...] = jnp.zeros_like(mark)
    loop(count, step)
    loop(count, lambda i: leave(i).wait())


def weight_grad_kernel(ring, tn, tl, left, right, buf, sent, sums):
    n, m = ring.n, ring.half
    half = left.shape[1] // n // 2
    slots = [ring.slot(j) for j in range(n)]
    swap = [jnp.where(k == m, ring.here()[0], 0) for k in slots]
    ones = jnp.ones((8, right.shape[0]), BF)
    per = tl // half

    def step(i):
        at = span(i, tn)
        r = right[:, at]
        sums[:, at] = dot(ones, r)
        for l in range(left.shape[1] // tl):
            v = dot_tn(left[:, l * tl : (l + 1) * tl], r).astype(BF)
            for s in range(per):
                j, q = divmod(l * per + s, 2)
                row = pl.multiple_of((2 * slots[j] + (swap[j] + q) % 2) * half, half)
                buf[pl.ds(row, half), at] = v[s * half : (s + 1) * half, :]
        sent[:, at] = buf[buf.shape[0] - sent.shape[0] :, at]

    loop(right.shape[1] // tn, step)


def norm_back(values, d, gain):
    n, r = normalized(values)
    g = d * gain
    t = r * (g - jnp.mean(g, axis=-1, keepdims=True) - n * jnp.mean(g * n, axis=-1, keepdims=True))
    return t, d * n


def group_sum(v):
    return jnp.sum(v.reshape(v.shape[0] // 8, 8, v.shape[1]), axis=0)


def dsecond_kernel(dh, wu, acc):
    tn = 256

    def step(i):
        at = span(i, tn)
        acc[:, at] = dot_nt(dh[...], wu[at, :])

    loop(acc.shape[1] // tn, step)


def second_norm_back_kernel(acc, wo, middle, og, small, dmid, dbranch, datt, sg, sb):
    g = small[pl.ds(GAIN2, 1), :]
    sg[...] = jnp.zeros_like(sg)
    sb[...] = jnp.zeros_like(sb)
    rows = 256

    def norm(i):
        at = span(i, rows)
        d = acc[at, :]
        t, dn = norm_back(middle[at, :], d, g)
        sg[...] += group_sum(dn)
        sb[...] += group_sum(d)
        v = og[at, :].astype(F32) + t
        dmid[at, :] = v
        dbranch[at, :] = v.astype(BF)

    loop(acc.shape[0] // rows, norm)
    tn = 256

    def back(i):
        at = span(i, tn)
        datt[:, at] = dot_nt(dbranch[...], wo[at, :]).astype(BF)

    loop(datt.shape[1] // tn, back)


def attend_back_kernel(part, proj, datt, col_ids, row_ids, o_ref, acc_k, acc_v):
    rows, hw = acc_k.shape
    scale = HD ** (-0.5)
    nq, back = 128, 64
    heads = range(HALF)
    acc_k[...] = jnp.zeros_like(acc_k)
    acc_v[...] = jnp.zeros_like(acc_v)

    def tile(q0, k0, nk):
        at_q, at_k = pl.ds(q0, nq), pl.ds(k0, nk)
        bias = mask(col_ids, row_ids, q0, k0, nq, nk)
        q = [proj[at_q, head_cols(0, h)] for h in heads]
        k = [proj[at_k, head_cols(1, h)] for h in heads]
        do = [datt[at_q, head_cols(part, h)] for h in heads]
        dw = [dot_nt(proj[at_k, head_cols(2, h)], do[h]) for h in heads]
        p = [soft(q[h], k[h], bias) for h in heads]
        for h in heads:
            acc_v[at_k, head_cols(0, h)] += dot(p[h].astype(BF), do[h])
        ds = [(p[h] * (dw[h] - jnp.sum(p[h] * dw[h], axis=0, keepdims=True))).astype(BF) for h in heads]
        for h in heads:
            acc_k[at_k, head_cols(0, h)] += dot(ds[h], q[h])
            o_ref[at_q, head_cols(0, h)] = (dot_tn(ds[h], k[h]) * scale).astype(BF)

    def step(i):
        for q0 in (pl.multiple_of(2 * i * nq, nq), pl.multiple_of((2 * i + 1) * nq, nq)):
            tile(q0, pl.multiple_of(jnp.maximum(q0 - back, 0), back), nq + back)

    loop(rows // nq // 2, step)
    o_ref[:, hw : 2 * hw] = (acc_k[...] * scale).astype(BF)
    o_ref[:, 2 * hw :] = acc_v[...].astype(BF)


def dfirst_kernel(da, db, wa, wb, acc):
    tn = 256

    def step(i):
        at = span(i, tn)
        acc[:, at] = dot_nt(da[...], wa[at, :]) + dot_nt(db[...], wb[at, :])

    loop(acc.shape[1] // tn, step)


def first_norm_back_kernel(acc, x_ref, dmid, small, far, sg, sb, o_ref, sems):
    g = small[pl.ds(GAIN1, 1), :]
    sg[...] = jnp.zeros_like(sg)
    sb[...] = jnp.zeros_like(sb)
    rows = 256
    count = x_ref.shape[0] // rows

    def leave(i):
        at = span(i, rows)
        return pltpu.make_async_copy(o_ref.at[at, :], far.at[at, :], sems.at[i])

    def norm(i):
        at = span(i, rows)
        d = acc[at, :]
        t, dn = norm_back(x_ref[at, :].astype(F32), d, g)
        sg[...] += group_sum(dn)
        sb[...] += group_sum(d)
        o_ref[at, :] = (dmid[at, :] + t).astype(BF)
        leave(i).start()

    loop(count, norm)
    loop(count, lambda i: leave(i).wait())


def small_grads_kernel(ring, sizes, sg1, sb1, ja, jb, so, sg2, sb2, su, sd, buf, sent):
    n, m = ring.n, ring.half
    hw = ja.shape[1] // 3
    rows = buf.shape[0] // n

    def whole(ref):
        return jnp.sum(ref[...], axis=0, keepdims=True)

    queries = jnp.concatenate([ja[0:1, 0:hw], jb[0:1, 0:hw]], axis=1)
    values = jnp.concatenate([ja[0:1, 2 * hw :], jb[0:1, 2 * hw :]], axis=1)
    vectors = [
        whole(sg1), whole(sb1), jnp.concatenate([queries, values], axis=1), so[0:1, :],
        whole(sg2), whole(sb2), su[0:1, :], sd[0:1, :],
    ]
    buf[...] = jnp.zeros_like(buf)
    c = ring.here()[0]
    for j in range(n):
        slot = ring.slot(j)
        top = pl.multiple_of((2 * slot + jnp.where(slot == m, c, 0)) * (rows // 2), rows // 2)
        for size in sorted(set(sizes)):
            parts = [v[:, j * size : (j + 1) * size] for v, k in zip(vectors, sizes) if k == size]
            parts.append(jnp.zeros((rows // 2 - len(parts), size), F32))
            block = jnp.concatenate(parts, axis=0).astype(BF)
            at = 0 if size == min(sizes) else SMALL_COL
            buf[pl.ds(top, rows // 2), at : at + size] = block
    sent[...] = buf[buf.shape[0] - sent.shape[0] :, :]


class Grads:
    def __init__(self, n, bufs, recvs, width):
        self.bufs, self.recvs, self.width = bufs, recvs, width
        self.sizes = [(b.shape[0] // n, b.shape[1] // width) for b in bufs]
        self.rows = sum(r * c for r, c in self.sizes)


def reduce_step(ring, gr, k, got):
    m, n = ring.half, ring.n
    width = gr.width
    half = k == m
    total = gr.rows // 2 if half else gr.rows
    args = [*gr.bufs, *gr.recvs] + ([got] if got is not None else [])
    nb = len(gr.bufs)

    def body(*refs):
        bs, rs = refs[:nb], refs[nb : 2 * nb]
        g = refs[2 * nb] if got is not None else None
        o = refs[-1]
        c = ring.here()[0]
        at, gat = 0, 0
        for b, rv, (r, cs) in zip(bs, rs, gr.sizes):
            h = r // 2
            for j in range(cs):
                col = slice(j * width, (j + 1) * width)
                if half:
                    v = b[m * r : m * r + h, col].astype(F32) + rv[0:h, col].astype(F32)
                    o[at : at + h, :] = v.astype(BF)
                    at += h
                else:
                    base = h + (n - k - m - 1) * r
                    v = b[k * r : (k + 1) * r, col].astype(F32) + rv[base : base + r, col].astype(F32)
                    if g.shape[0] == total:
                        o[at : at + r, :] = (v + g[at : at + r, :].astype(F32)).astype(BF)
                    else:
                        top = jnp.where(c == 0, 1.0, 0.0)
                        gv = g[gat : gat + h, :].astype(F32)
                        o[at : at + h, :] = (v[:h] + gv * top).astype(BF)
                        o[at + h : at + r, :] = (v[h:] + gv * (1.0 - top)).astype(BF)
                        gat += h
                    at += r

    return body, [out((total, width), BF)], args


def owner_sum(ring, gr, got):
    nb = len(gr.bufs)

    def body(*refs):
        bs, g, keep, send = refs[:nb], refs[nb], refs[nb + 1], refs[nb + 2]
        c = ring.here()[0]
        at, to = 0, 0
        for b, (r, cs) in zip(bs, gr.sizes):
            h = r // 2
            for j in range(cs):
                v = b[0:r, j * gr.width : (j + 1) * gr.width].astype(F32) + g[at : at + r, :].astype(F32)
                v = v.astype(BF)
                keep[to : to + h, :] = jnp.where(c == 0, v[:h], v[h:])
                send[to : to + h, :] = jnp.where(c == 0, v[h:], v[:h])
                at += r
                to += h

    o = out((gr.rows // 2, gr.width), BF)
    return body, [o, o], [*gr.bufs, got]


def add_kernel(a_ref, b_ref, o_ref):
    o_ref[...] = (a_ref[...].astype(F32) + b_ref[...].astype(F32)).astype(o_ref.dtype)


def add2(a, b):
    return add_kernel, [out(a.shape, a.dtype)], [a, b]


def reduce_group(ring, gr):
    got = None
    for k in range(ring.half, 0, -1):
        (part,) = yield reduce_step(ring, gr, k, got)
        got = ring.along(part)
    keep, send = yield owner_sum(ring, gr, got)
    (u,) = yield add2(keep, ring.core(send))
    bit = 2
    while bit < ring.reps:
        (u,) = yield add2(u, ring.send(u, lambda r, f, bit=bit: (r ^ bit, f)))
        bit *= 2
    return u, ring.core(u)


class Rounds:
    def __init__(self, line):
        self.line = line
        self.long = False
        self.live = {}
        self.jobs = {}
        self.done = {}

    def _advance(self, name, results):
        try:
            self.jobs[name] = next(self.live[name]) if results is None else self.live[name].send(results)
        except StopIteration as stop:
            self.done[name] = stop.value
            del self.live[name]
            self.jobs.pop(name, None)

    def add(self, name, chain):
        self.live[name] = chain
        self._advance(name, None)

    def turn(self, *names):
        names = [k for k in names or self.jobs if k in self.jobs]
        if not names:
            return
        jobs = [self.jobs[k] for k in names]
        args = [a for _, _, given in jobs for a in given]
        outs = [o for _, made, _ in jobs for o in made]

        def body(*refs):
            i, j = 0, len(args)
            for run, made, given in jobs:
                run(*refs[i : i + len(given)], *refs[j : j + len(made)])
                i, j = i + len(given), j + len(made)

        got = list(self.line.call(body, outs, args, long=self.long, name="sums"))
        for name, (_, made, _) in zip(names, jobs):
            self._advance(name, got[: len(made)])
            got = got[len(made) :]


def join_halves(c, parts, sizes, width, place):
    a_ref, b_ref = parts
    to = 0
    for i, (r, cs) in enumerate(sizes):
        h = r // 2
        for j in range(cs):
            a = a_ref[to : to + h, :].astype(F32)
            b = b_ref[to : to + h, :].astype(F32)
            place(i, slice(0, h), j, jnp.where(c == 0, a, b))
            place(i, slice(h, r), j, jnp.where(c == 0, b, a))
            to += h


def last_sum(job):
    return (yield job)


def finish(ring, gr, parts):
    def body(a_ref, b_ref, *outs):
        def place(i, rows, j, v):
            outs[i][rows, j * gr.width : (j + 1) * gr.width] = v

        join_halves(ring.here()[0], (a_ref, b_ref), gr.sizes, gr.width, place)

    return body, [out((r, cs * gr.width), F32) for r, cs in gr.sizes], list(parts)


def finish_joint(ring, gr_a, gr_b, parts_a, parts_b, sizes):
    (r, cs), (_, ocs), width = *gr_a.sizes, gr_a.width

    def body(a1, a2, b1, b2, o, o2, small, *outs):
        for k, pair in enumerate(((a1, a2), (b1, b2))):
            def place(i, rows, j, v, k=k):
                if i == 0:
                    at = (2 * j + k) * width
                    o[rows, at : at + width] = v
                elif k == 0:
                    o2[rows, j * width : (j + 1) * width] = v
                else:
                    small[rows, :] = v

            join_halves(ring.here()[0], pair, (gr_a, gr_b)[k].sizes, width, place)
        row = {}
        for size, got in zip(sizes, outs):
            k = row.setdefault(size, 0)
            row[size] += 1
            at = 0 if size == min(sizes) else SMALL_COL
            got[...] = small[k : k + 1, at : at + size]

    outs = [out((r, 2 * cs * width), F32), out((r, ocs * width), F32), out((SMALL_SHARD, width), F32)] + [out((1, k), F32) for k in sizes]
    return body, outs, [*parts_a, *parts_b]


def step_fn(mesh):
    ring = Ring(mesh)
    n, m = ring.n, ring.half

    def on_device(
        layer_input, item_ids, norm_gain, norm_bias, joint_weight, joint_bias, out_weight, out_bias,
        second_gain, second_bias, up_weight, up_bias, down_weight, down_bias, output_grad,
    ):
        rows, width = layer_input.shape
        ff = up_weight.shape[1]
        hw = width // 2
        rps = width // n
        t = (rps // 4) // 16 * 16
        a, b = rps + t, 2 * rps - 2 * t
        dma = pltpu.SemaphoreType.DMA
        shapes = [out((a + b, width), BF), out((a, width), BF)]
        line = Line()
        first1, opp1 = line.call(
            functools.partial(split_kernel, ring, t), shapes, [joint_weight, out_weight],
            far=(0, 1), scratch=[dma((6,))], name="split",
        )
        ids = [item_ids[:, None], item_ids[None, :]]
        first2, opp2 = line.call(
            functools.partial(split_ff_kernel, ring, t), shapes, [up_weight, down_weight], deps=ids,
            far=(0, 1), scratch=[dma((5,))], name="split_ff",
        )
        vectors = (norm_gain, norm_bias, joint_bias, out_bias, second_gain, second_bias, up_bias, down_bias)
        shared = {}

        def small_parts():
            (small,) = line.call(
                functools.partial(small_kernel, ring), [out((SMALL_ROWS, width), F32)], vectors, name="small",
            )
            mark = yield
            bit = 1
            while bit < n:
                other = ring.send(small, lambda r, f, bit=bit: (r, f ^ bit))
                yield (small if bit > 1 else None)
                mark = yield
                (small,) = kernel_call(add_f32_kernel, [out(small.shape, F32)], [small, other], deps=[mark], name="small_sum")
                bit *= 2
            shared["small"] = small
            (shared["first"],) = kernel_call(
                ln_kernel, [out((rows, width), BF)], [layer_input, small], deps=[mark], name="first_norm",
            )
            mark = yield shared["first"]
            while True:
                yield

        extras = small_parts()
        next(extras)
        g1, g2 = gather(ring, [first1, first2], a, extras)
        small, first = shared["small"], shared["first"]

        args = [first, small, *flat(first1, opp1, g1)]
        halves = [out((rows, 3 * hw), BF)] * 2
        proj_a, proj_b, wa, wb, wo = line.call(
            functools.partial(qkv_kernel, ring, a, t),
            halves + [out((width, 3 * hw), BF)] * 2 + [out((width, width), BF)],
            args, scratch=[VM((b, width), BF)], name="projection",
        )
        g2["ring"][-1], wo = there_first(g2["ring"][-1], wo)
        g2["pring"].append(ring.core(g2["ring"][-1]))
        (attended,) = line.call(attend_kernel, [out((rows, width), BF)], [proj_a, proj_b, *ids], name="attend")
        middle, second = line.call(
            out_kernel, [out((rows, width), F32), out((rows, width), BF)],
            [attended, wo, layer_input, small], name="out_projection",
        )
        args = [second, small, *flat(first2, opp2, g2)]
        active, slope, wu, wd = line.call(
            functools.partial(up_kernel, ring, a, t),
            [out((rows, ff), BF), out((rows, ff), BF), out((width, ff), BF), out((ff, width), BF)],
            args, scratch=[VM((b, width), BF)], name="up_projection",
        )

        def weight_grad(l, r, tl=512, tn=512, name=None):
            kl, kr = l.shape[1], r.shape[1]
            kept = m * (kl // n) + kl // n // 2
            buf, sent, sums = line.call(
                functools.partial(weight_grad_kernel, ring, tn, tl),
                [out((kl, kr), BF), out((kl - kept, kr), BF), out((8, kr), F32)], [l, r], name=name,
            )
            return buf, ring.core(sent), sums

        rounds = Rounds(line)

        def begin(name, bufs, recvs, w):
            gr = Grads(n, bufs, recvs, w)
            rounds.add(name, reduce_group(ring, gr))
            return gr

        down_buf, down_recv, s_down = weight_grad(active, output_grad, name="down_grad")
        (dhidden,) = line.call(
            dact_kernel, [out((rows, ff), BF)], [output_grad, wd, slope], name="hidden_grad",
        )
        gr_down = begin("down", [down_buf], [down_recv], width)
        rounds.turn("down")
        up_buf, up_recv, s_up = weight_grad(second, dhidden, name="up_grad")
        rounds.turn("down")
        (dsecond,) = line.call(dsecond_kernel, [out((rows, width), F32)], [dhidden, wu], name="dsecond")
        gr_up = begin("up", [up_buf], [up_recv], width)
        rounds.turn("up")
        dmid, dbranch, datt, sg2, sb2 = line.call(
            second_norm_back_kernel,
            [out((rows, width), F32), out((rows, width), BF), out((rows, width), BF), out((8, width), F32), out((8, width), F32)],
            [dsecond, wo, middle, output_grad, small], name="second_norm_grad",
        )
        rounds.turn("down")
        out_buf, out_recv, s_out = weight_grad(attended, dbranch, name="out_grad")
        rounds.turn("up")

        def attend_back(part, proj):
            return line.call(
                functools.partial(attend_back_kernel, part), [out((rows, 3 * hw), BF)], [proj, datt, *ids],
                scratch=[VM((rows, hw), F32), VM((rows, hw), F32)], name="attend_grad",
            )[0]

        da = attend_back(0, proj_a)
        rounds.turn("down")
        ja_buf, ja_recv, s_ja = weight_grad(first, da, name="joint_grad")
        rounds.turn("up")
        db = attend_back(1, proj_b)
        gr_ja = begin("ja", [ja_buf, out_buf], [ja_recv, out_recv], hw)
        rounds.turn("ja", "down")
        jb_buf, jb_recv, s_jb = weight_grad(first, db, name="joint_grad")
        rounds.turn("up")
        (dfirst,) = line.call(dfirst_kernel, [out((rows, width), F32)], [da, db, wa, wb], name="dfirst")
        rounds.turn("ja")
        input_grad, sg1, sb1 = line.call(
            first_norm_back_kernel, [out((rows, width), BF), out((8, width), F32), out((8, width), F32)],
            [dfirst, layer_input, dmid, small], straight=(0,),
            scratch=[VM((rows, width), BF), dma((rows // 256,))], name="first_norm_grad",
        )
        small_sizes = [v.shape[0] for v in vectors]
        small_kept = m * SMALL_SHARD + SMALL_SHARD // 2
        small_buf, small_sent = line.call(
            functools.partial(small_grads_kernel, ring, small_sizes),
            [out((n * SMALL_SHARD, hw), BF), out((n * SMALL_SHARD - small_kept, hw), BF)],
            [sg1, sb1, s_ja, s_jb, s_out, sg2, sb2, s_up, s_down], long=False, name="small_grads",
        )
        gr_jb = begin("jb", [jb_buf, small_buf], [jb_recv, ring.core(small_sent)], hw)
        rounds.turn("jb", "down")
        rounds.long = True
        rounds.turn("ja", "up")
        done, ready = rounds.done, set()
        pairs = ("jb", "up", "got up"), ("ja", "down", "got down")
        k = 0
        while rounds.jobs:
            if k == m + 1:
                rounds.long = False
                layer_output, _ = line.call(
                    down_kernel, [out((rows, width), BF), out((8, 128), F32)], [active, wd, middle, small],
                    straight=(0,), scratch=[VM((rows, width), BF), dma((width // 256,))], name="down_projection",
                )
            rounds.turn(*(pairs[k % 2] if k < m else ()))
            k += 1
            for name, gr in (("down", gr_down), ("up", gr_up)):
                if name in done and name not in ready:
                    ready.add(name)
                    rounds.add("got " + name, last_sum(finish(ring, gr, done[name])))
            if "ja" in done and "jb" in done and "joint" not in ready:
                ready.add("joint")
                rounds.add("got joint", last_sum(finish_joint(ring, gr_ja, gr_jb, done["ja"], done["jb"], small_sizes)))
        (g_down,), (g_up,), (g_joint, g_out, _, *v) = (done["got " + k] for k in ("down", "up", "joint"))
        v = [k.reshape(-1) for k in v]
        return (
            layer_output, input_grad, v[0], v[1], g_joint, v[2], g_out, v[3], v[4], v[5], g_up, v[6], g_down, v[7],
        )

    return on_device


def solution(mesh):
    row, vecs, mat = P(("rep", "fsdp"), None), P("fsdp"), P("fsdp", None)
    placed = (
        row, P(("rep", "fsdp")), vecs, vecs, mat, vecs, mat, vecs, vecs, vecs, mat, vecs, mat, vecs, row,
    )
    return jax.shard_map(
        step_fn(mesh),
        mesh=mesh,
        in_specs=placed,
        out_specs=(row, row, vecs, vecs, mat, vecs, mat, vecs, vecs, vecs, mat, vecs, mat, vecs),
        check_vma=False,
    )
```

```python
import functools
import math

import jax
import jax.numpy as jnp
from jax import lax
from jax.experimental import pallas as pl
from jax.experimental.pallas import tpu as pltpu
from jax.sharding import PartitionSpec as P

H = 8
HD = 128
HALF = H // 2
EPS = 1e-05
MASKED = -1e30
LOG2E = 1.4426950408889634
C0 = math.sqrt(2.0 / math.pi)
BF = jnp.bfloat16
F32 = jnp.float32
VM = pltpu.VMEM
MAIN = 60 * 10**9
MIB = 2**20

GAIN1, BIAS1, JB_Q, JB_V, OUT_B, GAIN2, BIAS2, UP_B, DOWN_B = 0, 1, 2, 3, 4, 5, 6, 7, 9
SMALL_ROWS = 16
SMALL_SHARD, SMALL_COL = 32, 256


def nbytes(a):
    return math.prod(a.shape) * jnp.dtype(a.dtype).itemsize


def kernel_call(body, outs, args, deps=(), smem=(), anys=(), far=(), scratch=(), straight=(), extra=3, long=True, name=None):
    own = sum(nbytes(s) for s in scratch if getattr(s, "dtype", None) in (BF, F32))
    count, made = len(args), len(outs)
    deps = [d for d in deps if d is not None]

    def space(i):
        return pl.ANY if i in anys else pltpu.HBM if i in far else pltpu.SMEM if i in smem else VM

    args = [pltpu.with_memory_space_constraint(v, pltpu.HBM) if i in far else v for i, v in enumerate(args)]

    def run(*refs):
        body(*refs[:count], *refs[count + len(deps) :])

    return pl.pallas_call(
        run,
        out_shape=[pltpu.HBM(o.shape, o.dtype) if i in straight else o for i, o in enumerate(outs)],
        in_specs=[pl.BlockSpec(memory_space=space(i)) for i in range(count)]
        + [pl.BlockSpec(memory_space=pl.ANY) for _ in deps],
        out_specs=[pl.BlockSpec(memory_space=pltpu.HBM if i in straight else VM) for i in range(len(outs))],
        scratch_shapes=list(scratch),
        compiler_params=pltpu.CompilerParams(vmem_limit_bytes=own + int(extra * MIB)),
        cost_estimate=pl.CostEstimate(flops=MAIN if long else 0, bytes_accessed=0, transcendentals=0),
        name=name,
    )(*args, *deps)


def out(shape, dtype):
    return jax.ShapeDtypeStruct(shape, dtype)


class Line:
    def __init__(self):
        self.mark = None

    def call(self, body, outs, args, deps=(), **kw):
        made = kernel_call(body, outs, args, deps=(self.mark, *deps), **kw)
        self.mark = min(made, key=nbytes)
        return made


def dot(a, b):
    return jnp.dot(a, b, preferred_element_type=F32)


def dot_tn(a, b):
    return lax.dot_general(a, b, (((0,), (0,)), ((), ())), preferred_element_type=F32)


def dot_nt(a, b):
    return lax.dot_general(a, b, (((1,), (1,)), ((), ())), preferred_element_type=F32)


def loop(count, step):
    lax.fori_loop(0, count, lambda i, z: (step(i), z)[1], 0)


def span(i, size):
    return pl.ds(pl.multiple_of(i * size, size), size)


def normalized(values):
    center = values - jnp.mean(values, axis=-1, keepdims=True)
    spread = jnp.mean(center * center, axis=-1, keepdims=True)
    factor = lax.rsqrt(spread + EPS)
    return center * factor, factor


class Ring:
    def __init__(self, mesh):
        self.axes = ("rep", "fsdp")
        self.n = mesh.shape["fsdp"]
        self.reps = mesh.shape["rep"]
        n = self.n
        self.order = list(range(0, n, 2)) + list(range(n - 1, 0, -2))
        self.place = [self.order.index(f) for f in range(n)]
        self.half = n // 2

    def send(self, v, target, keep=lambda r, f: True):
        n = self.n
        pairs = []
        for r in range(self.reps):
            for f in range(n):
                if keep(r, f):
                    r2, f2 = target(r, f)
                    pairs.append((r * n + f, r2 * n + f2))
        return lax.ppermute(v, self.axes, pairs)

    def along(self, v):
        def target(r, f):
            step = 1 if r % 2 == 0 else -1
            return r, self.order[(self.place[f] + step) % self.n]

        return self.send(v, target)

    def core(self, v):
        return self.send(v, lambda r, f: (r ^ 1, f))

    def across(self, v, keep=lambda r, f: True):
        return self.send(v, lambda r, f: (r ^ 2, f), keep)

    def here(self):
        r = lax.axis_index("rep")
        return r % 2, (r // 2) % 2, lax.axis_index("fsdp")

    def own_place(self):
        n, (c, _, f) = self.n, self.here()
        return jnp.where(f % 2 == 0, f // 2, n - 1 - f // 2), 1 - 2 * c

    def shard_back(self, h):
        n, (p, d) = self.n, self.own_place()
        q = lax.rem(p - d * h + 2 * n, n)
        return jnp.where(q < n // 2, 2 * q, 2 * (n - 1 - q) + 1)

    def slot(self, j):
        n, (p, d) = self.n, self.own_place()
        return lax.rem((self.place[j] - p) * d + n, n)


def cut_kernel(a, v, ext, *more):
    ext[...] = v[0:a, :]
    if more:
        more[0][...] = v[...]


def last_kernel(ring, a, v, other, o_ref):
    half = (v.shape[0] - a) // 2

    @pl.when(ring.here()[0] == 0)
    def _():
        o_ref[...] = v[0 : a + half, :]

    @pl.when(ring.here()[0] == 1)
    def _():
        o_ref[0:a, :] = other[...]
        o_ref[a:, :] = v[a + half :, :]


def there_first(x, other):
    return lax.optimization_barrier((x, other))


def gather(ring, firsts, a, extras):
    m = ring.half
    b, width = firsts[0].shape[0] - a, firsts[0].shape[1]
    groups = [dict(ring=[], out=[], pring=[], pout=[], due=[]) for _ in firsts]
    for h in range(1, m + 1):
        for i, g in enumerate(groups):
            if h == 1:
                g["ring"].append(ring.along(firsts[i]))
                continue
            v = g["ring"][-1]
            shapes = [out((a, width), BF)] + ([out(v.shape, BF)] if h < m else [])
            x = list(kernel_call(functools.partial(cut_kernel, a), shapes, [v], deps=g["due"], name="cut"))
            if h > 2:
                x[-1], g["out"][-1] = there_first(x[-1], g["out"][-1])
                g["pout"].append(ring.core(g["out"][-1]))
            if h < m:
                g["ring"].append(ring.along(x[1]))
            g["due"] = [ring.across(x[0]), ring.core(v)] + g["pout"][-1:]
            g["out"].append(g["due"][0])
            g["pring"].append(g["due"][1])
            more = extras.send(x[0])
            if more is not None:
                g["due"].append(more)
    more = None
    for i, g in enumerate(groups):
        (part,) = kernel_call(
            functools.partial(last_kernel, ring, a), [out((a + b // 2, width), BF)], [g["ring"][-1], g["out"][-1]],
            deps=[more], name="last",
        )
        g["ring"].append(ring.along(part))
        g["pout"].append(ring.core(g["out"][-1]))
        more = extras.send(part)
    groups[0]["pring"].append(ring.core(groups[0]["ring"][-1]))
    return groups


def flat(own, opp, g):
    return [own, opp, *g["ring"], *g["pring"], *g["out"], *g["pout"]]


def place_parts(ring, a, refs, middle, put):
    n, m = ring.n, ring.half
    own, opp, refs = refs[0], refs[1], refs[2:]
    rings, prings = refs[:m], refs[m : 2 * m]
    outs, pouts = refs[2 * m : 3 * m - 1], refs[3 * m - 1 :]

    def all_parts(step, ext, mid, mid0, other):
        s = ring.shard_back(step)
        put("mid", s, mid, mid0)
        put("ext", s, ext, 0)
        put("opp", s, other, 0)

    all_parts(0, own, own, a, opp)
    for h in range(1, m):
        all_parts(h, rings[h - 1], rings[h - 1], a, outs[h - 1])
        all_parts(n - h, prings[h - 1], prings[h - 1], a, pouts[h - 1])
    half = middle.shape[0] // 2

    def last(low, high):
        middle[0:half, :] = low[a:, :]
        middle[half:, :] = high[a:, :]
        all_parts(m, low, middle, 0, high)

    c = ring.here()[0]

    @pl.when(c == 0)
    def _():
        last(rings[-1], prings[-1])

    @pl.when(c == 1)
    def _():
        last(prings[-1], rings[-1])


def ln_rows(x_ref, gain, bias, o_ref, rows=384):
    def step(i):
        at = span(i, rows)
        n, _ = normalized(x_ref[at, :].astype(F32))
        o_ref[at, :] = (n * gain + bias).astype(BF)

    loop(x_ref.shape[0] // rows, step)


def split_kernel(ring, t, jw, ow, first, opp, sems):
    width = ow.shape[1]
    rps = ow.shape[0]
    a = rps + t
    x = ring.here()[1]
    made = []

    def copy(src, dst):
        c = pltpu.make_async_copy(src, dst, sems.at[len(made)])
        c.start()
        made.append(c)

    def cols(side):
        return jw.at[:, pl.ds(pl.multiple_of(side * 2 * width, width), width)]

    copy(cols(x), first.at[pl.ds(0, rps), :])
    copy(jw.at[:, pl.ds(width, width)], first.at[pl.ds(a, rps), :])
    copy(ow.at[pl.ds(t, rps - 2 * t), :], first.at[pl.ds(a + rps, rps - 2 * t), :])
    copy(cols(1 - x), opp.at[pl.ds(0, rps), :])
    if t:
        copy(ow.at[pl.ds(pl.multiple_of(x * (rps - t), 16), t), :], first.at[pl.ds(rps, t), :])
        copy(ow.at[pl.ds(pl.multiple_of((1 - x) * (rps - t), 16), t), :], opp.at[pl.ds(rps, t), :])
    for c in made:
        c.wait()


def split_ff_kernel(ring, t, uw, dw, first, opp, sems):
    width = dw.shape[1]
    rps = uw.shape[0]
    a = rps + t
    x = ring.here()[1]
    made = []

    def copy(src, dst):
        c = pltpu.make_async_copy(src, dst, sems.at[len(made)])
        c.start()
        made.append(c)

    def cols(side):
        return uw.at[:, pl.ds(pl.multiple_of(side * width, width), width)]

    copy(cols(x), first.at[pl.ds(0, rps), :])
    copy(dw.at[pl.ds(t, 2 * rps - 2 * t), :], first.at[pl.ds(a, 2 * rps - 2 * t), :])
    copy(cols(1 - x), opp.at[pl.ds(0, rps), :])
    if t:
        copy(dw.at[pl.ds(pl.multiple_of(x * (2 * rps - t), 16), t), :], first.at[pl.ds(rps, t), :])
        copy(dw.at[pl.ds(pl.multiple_of((1 - x) * (2 * rps - t), 16), t), :], opp.at[pl.ds(rps, t), :])
    for c in made:
        c.wait()


def small_kernel(ring, *refs):
    parts, o_ref = refs[:-1], refs[-1]
    width = o_ref.shape[1]
    n, f = ring.n, ring.here()[2]
    row = 0
    o_ref[...] = jnp.zeros_like(o_ref)
    for part in parts:
        size = part.shape[0]
        full = size * n
        i = lax.broadcasted_iota(jnp.int32, (size, full), 0)
        j = lax.broadcasted_iota(jnp.int32, (size, full), 1)
        hot = jnp.where(j == i + f * size, 1.0, 0.0).astype(BF)
        placed = dot(jnp.broadcast_to(part[...].astype(F32)[None, :], (8, size)).astype(BF), hot)
        for k in range(full // width):
            o_ref[row : row + 1, :] = placed[0:1, k * width : (k + 1) * width]
            row += 1


def add_f32_kernel(a_ref, b_ref, o_ref):
    o_ref[...] = a_ref[...] + b_ref[...]


def ln_kernel(x_ref, small, o_ref):
    ln_rows(x_ref, small[pl.ds(GAIN1, 1), :], small[pl.ds(BIAS1, 1), :], o_ref)


def qkv_kernel(ring, a, t, first, small, *refs):
    refs, outs, middle = refs[:-6], refs[-6:-1], refs[-1]
    proj, ws, wo = outs[:2], outs[2:4], outs[4]
    width = first.shape[1]
    rps = width // ring.n
    hw = width // 2
    xb = ring.here()[1]

    def put(part, s, ref, r0):
        row = pl.multiple_of(s * rps, rps)
        if part == "mid":
            for k in range(2):
                ws[k][pl.ds(row, rps), hw : 2 * hw] = ref[r0 : r0 + rps, k * hw : (k + 1) * hw]
            wo[pl.ds(pl.multiple_of(row + t, 16), rps - 2 * t), :] = ref[r0 + rps : r0 + 2 * rps - 2 * t, :]
        else:
            side = xb if part == "ext" else 1 - xb
            col = pl.multiple_of(side * 2 * hw, hw)
            for k in range(2):
                ws[k][pl.ds(row, rps), pl.ds(col, hw)] = ref[0:rps, k * hw : (k + 1) * hw]
            if t:
                wo[pl.ds(pl.multiple_of(row + side * (rps - t), 16), t), :] = ref[rps : rps + t, :]

    place_parts(ring, a, refs, middle, put)
    for k in range(2):

        def tile(i, k=k):
            at = span(i, hw)
            v = dot(first[...], ws[k][:, at])
            use = jnp.where(i == 0, 1.0, 0.0), jnp.where(i == 2, 1.0, 0.0)
            shift = small[pl.ds(JB_Q, 1), k * hw : (k + 1) * hw] * use[0]
            shift = shift + small[pl.ds(JB_V, 1), k * hw : (k + 1) * hw] * use[1]
            proj[k][:, at] = (v + shift).astype(BF)

        loop(3, tile)


def mask(col_ids, row_ids, q0, k0, queries, keys):
    same = col_ids[pl.ds(k0, keys), :] == row_ids[:, pl.ds(q0, queries)]
    kpos = lax.broadcasted_iota(jnp.int32, (keys, queries), 0) + k0
    qpos = lax.broadcasted_iota(jnp.int32, (keys, queries), 1) + q0
    return jnp.where(same & (kpos <= qpos), 0.0, MASKED).astype(F32)


def soft(q, k, bias):
    s = dot_nt(k, q) * (HD ** (-0.5) * LOG2E) + bias
    p = jnp.exp2(s - jnp.max(s, axis=0, keepdims=True))
    return p * (1.0 / jnp.sum(p, axis=0, keepdims=True))


def head_cols(part, h):
    return slice((part * HALF + h) * HD, (part * HALF + h + 1) * HD)


def tiles(rows, queries, back):
    for q0 in range(0, rows, queries):
        lo = min(q0, back)
        yield q0, q0 - lo, queries + lo


def attend_kernel(proj_a, proj_b, col_ids, row_ids, o_ref):
    nq = 256
    for q0, k0, nk in tiles(o_ref.shape[0], nq, 128):
        at_q, at_k = slice(q0, q0 + nq), slice(k0, k0 + nk)
        bias = mask(col_ids, row_ids, q0, k0, nq, nk)
        for k, proj in enumerate((proj_a, proj_b)):
            for h in range(HALF):
                w = soft(proj[at_q, head_cols(0, h)], proj[at_k, head_cols(1, h)], bias).astype(BF)
                col = (k * HALF + h) * HD
                o_ref[at_q, col : col + HD] = dot_tn(w, proj[at_k, head_cols(2, h)]).astype(BF)


def out_kernel(att, wo, x_ref, small, middle, second):
    tn = 512

    def step(i):
        at = span(i, tn)
        middle[:, at] = x_ref[:, at].astype(F32) + dot(att[...], wo[:, at]) + small[pl.ds(OUT_B, 1), at]

    loop(wo.shape[1] // tn, step)
    ln_rows(middle, small[pl.ds(GAIN2, 1), :], small[pl.ds(BIAS2, 1), :], second)


def gelu_both(h):
    h2 = h * h
    half = 0.5 + 0.5 * jnp.tanh(h * (C0 + (C0 * 0.044715) * h2))
    act = h * half
    return act, half + act * (1.0 - half) * (2.0 * C0 + (6.0 * C0 * 0.044715) * h2)


def up_kernel(ring, a, t, second, small, *refs):
    refs, outs, middle = refs[:-5], refs[-5:-1], refs[-1]
    active, slope, wu, wd = outs
    width = second.shape[1]
    rps = width // ring.n
    xb = ring.here()[1]

    def put(part, s, ref, r0):
        row = pl.multiple_of(s * rps, rps)
        drow = pl.multiple_of(s * 2 * rps, 2 * rps)
        if part == "mid":
            wd[pl.ds(pl.multiple_of(drow + t, 16), 2 * rps - 2 * t), :] = ref[r0 : r0 + 2 * rps - 2 * t, :]
        else:
            side = xb if part == "ext" else 1 - xb
            wu[pl.ds(row, rps), pl.ds(pl.multiple_of(side * width, width), width)] = ref[0:rps, :]
            if t:
                wd[pl.ds(pl.multiple_of(drow + side * (2 * rps - t), 16), t), :] = ref[rps : rps + t, :]

    place_parts(ring, a, refs, middle, put)
    tn = 512
    per = width // tn

    def step(i):
        at = span(i, tn)
        shift = small[pl.ds(UP_B + i // per, 1), span(i % per, tn)]
        act, s = gelu_both(dot(second[...], wu[:, at]) + shift)
        active[:, at] = act.astype(BF)
        slope[:, at] = s.astype(BF)

    loop(2 * per, step)


def dact_kernel(og, wd, slope, o_ref):
    tn = 512

    def step(i):
        at = span(i, tn)
        o_ref[:, at] = (dot_nt(og[...], wd[at, :]) * slope[:, at].astype(F32)).astype(BF)

    loop(o_ref.shape[1] // tn, step)


def down_kernel(active, wd, middle, small, far, mark, o_ref, sems):
    tn = 256
    count = o_ref.shape[1] // tn

    def leave(i):
        at = span(i, tn)
        return pltpu.make_async_copy(o_ref.at[:, at], far.at[:, at], sems.at[i])

    def step(i):
        at = span(i, tn)
        o_ref[:, at] = (middle[:, at] + dot(active[...], wd[:, at]) + small[pl.ds(DOWN_B, 1), at]).astype(BF)
        leave(i).start()

    mark[...] = jnp.zeros_like(mark)
    loop(count, step)
    loop(count, lambda i: leave(i).wait())


def weight_grad_kernel(ring, tn, tl, left, right, buf, sent, sums):
    n, m = ring.n, ring.half
    half = left.shape[1] // n // 2
    slots = [ring.slot(j) for j in range(n)]
    swap = [jnp.where(k == m, ring.here()[0], 0) for k in slots]
    ones = jnp.ones((8, right.shape[0]), BF)
    per = tl // half

    def step(i):
        at = span(i, tn)
        r = right[:, at]
        sums[:, at] = dot(ones, r)
        for l in range(left.shape[1] // tl):
            v = dot_tn(left[:, l * tl : (l + 1) * tl], r).astype(BF)
            for s in range(per):
                j, q = divmod(l * per + s, 2)
                row = pl.multiple_of((2 * slots[j] + (swap[j] + q) % 2) * half, half)
                buf[pl.ds(row, half), at] = v[s * half : (s + 1) * half, :]
        sent[:, at] = buf[buf.shape[0] - sent.shape[0] :, at]

    loop(right.shape[1] // tn, step)


def norm_back(values, d, gain):
    n, r = normalized(values)
    g = d * gain
    t = r * (g - jnp.mean(g, axis=-1, keepdims=True) - n * jnp.mean(g * n, axis=-1, keepdims=True))
    return t, d * n


def group_sum(v):
    return jnp.sum(v.reshape(v.shape[0] // 8, 8, v.shape[1]), axis=0)


def dsecond_kernel(dh, wu, acc):
    tn = 256

    def step(i):
        at = span(i, tn)
        acc[:, at] = dot_nt(dh[...], wu[at, :])

    loop(acc.shape[1] // tn, step)


def second_norm_back_kernel(acc, wo, middle, og, small, dmid, dbranch, datt, sg, sb):
    g = small[pl.ds(GAIN2, 1), :]
    sg[...] = jnp.zeros_like(sg)
    sb[...] = jnp.zeros_like(sb)
    rows = 256

    def norm(i):
        at = span(i, rows)
        d = acc[at, :]
        t, dn = norm_back(middle[at, :], d, g)
        sg[...] += group_sum(dn)
        sb[...] += group_sum(d)
        v = og[at, :].astype(F32) + t
        dmid[at, :] = v
        dbranch[at, :] = v.astype(BF)

    loop(acc.shape[0] // rows, norm)
    tn = 256

    def back(i):
        at = span(i, tn)
        datt[:, at] = dot_nt(dbranch[...], wo[at, :]).astype(BF)

    loop(datt.shape[1] // tn, back)


def attend_back_kernel(part, proj, datt, col_ids, row_ids, o_ref, acc_k, acc_v):
    rows, hw = acc_k.shape
    scale = HD ** (-0.5)
    nq, back = 128, 64
    heads = range(HALF)
    acc_k[...] = jnp.zeros_like(acc_k)
    acc_v[...] = jnp.zeros_like(acc_v)

    def tile(q0, k0, nk):
        at_q, at_k = pl.ds(q0, nq), pl.ds(k0, nk)
        bias = mask(col_ids, row_ids, q0, k0, nq, nk)
        q = [proj[at_q, head_cols(0, h)] for h in heads]
        k = [proj[at_k, head_cols(1, h)] for h in heads]
        do = [datt[at_q, head_cols(part, h)] for h in heads]
        dw = [dot_nt(proj[at_k, head_cols(2, h)], do[h]) for h in heads]
        p = [soft(q[h], k[h], bias) for h in heads]
        for h in heads:
            acc_v[at_k, head_cols(0, h)] += dot(p[h].astype(BF), do[h])
        ds = [(p[h] * (dw[h] - jnp.sum(p[h] * dw[h], axis=0, keepdims=True))).astype(BF) for h in heads]
        for h in heads:
            acc_k[at_k, head_cols(0, h)] += dot(ds[h], q[h])
            o_ref[at_q, head_cols(0, h)] = (dot_tn(ds[h], k[h]) * scale).astype(BF)

    def step(i):
        for q0 in (pl.multiple_of(2 * i * nq, nq), pl.multiple_of((2 * i + 1) * nq, nq)):
            tile(q0, pl.multiple_of(jnp.maximum(q0 - back, 0), back), nq + back)

    loop(rows // nq // 2, step)
    o_ref[:, hw : 2 * hw] = (acc_k[...] * scale).astype(BF)
    o_ref[:, 2 * hw :] = acc_v[...].astype(BF)


def dfirst_kernel(da, db, wa, wb, acc):
    tn = 256

    def step(i):
        at = span(i, tn)
        acc[:, at] = dot_nt(da[...], wa[at, :]) + dot_nt(db[...], wb[at, :])

    loop(acc.shape[1] // tn, step)


def first_norm_back_kernel(acc, x_ref, dmid, small, far, sg, sb, o_ref, sems):
    g = small[pl.ds(GAIN1, 1), :]
    sg[...] = jnp.zeros_like(sg)
    sb[...] = jnp.zeros_like(sb)
    rows = 256
    count = x_ref.shape[0] // rows

    def leave(i):
        at = span(i, rows)
        return pltpu.make_async_copy(o_ref.at[at, :], far.at[at, :], sems.at[i])

    def norm(i):
        at = span(i, rows)
        d = acc[at, :]
        t, dn = norm_back(x_ref[at, :].astype(F32), d, g)
        sg[...] += group_sum(dn)
        sb[...] += group_sum(d)
        o_ref[at, :] = (dmid[at, :] + t).astype(BF)
        leave(i).start()

    loop(count, norm)
    loop(count, lambda i: leave(i).wait())


def small_grads_kernel(ring, sizes, sg1, sb1, ja, jb, so, sg2, sb2, su, sd, buf, sent):
    n, m = ring.n, ring.half
    hw = ja.shape[1] // 3
    rows = buf.shape[0] // n

    def whole(ref):
        return jnp.sum(ref[...], axis=0, keepdims=True)

    queries = jnp.concatenate([ja[0:1, 0:hw], jb[0:1, 0:hw]], axis=1)
    values = jnp.concatenate([ja[0:1, 2 * hw :], jb[0:1, 2 * hw :]], axis=1)
    vectors = [
        whole(sg1), whole(sb1), jnp.concatenate([queries, values], axis=1), so[0:1, :],
        whole(sg2), whole(sb2), su[0:1, :], sd[0:1, :],
    ]
    buf[...] = jnp.zeros_like(buf)
    c = ring.here()[0]
    for j in range(n):
        slot = ring.slot(j)
        top = pl.multiple_of((2 * slot + jnp.where(slot == m, c, 0)) * (rows // 2), rows // 2)
        for size in sorted(set(sizes)):
            parts = [v[:, j * size : (j + 1) * size] for v, k in zip(vectors, sizes) if k == size]
            parts.append(jnp.zeros((rows // 2 - len(parts), size), F32))
            block = jnp.concatenate(parts, axis=0).astype(BF)
            at = 0 if size == min(sizes) else SMALL_COL
            buf[pl.ds(top, rows // 2), at : at + size] = block
    sent[...] = buf[buf.shape[0] - sent.shape[0] :, :]


class Grads:
    def __init__(self, n, bufs, recvs, width):
        self.bufs, self.recvs, self.width = bufs, recvs, width
        self.sizes = [(b.shape[0] // n, b.shape[1] // width) for b in bufs]
        self.rows = sum(r * c for r, c in self.sizes)


def reduce_step(ring, gr, k, got):
    m, n = ring.half, ring.n
    width = gr.width
    half = k == m
    total = gr.rows // 2 if half else gr.rows
    args = [*gr.bufs, *gr.recvs] + ([got] if got is not None else [])
    nb = len(gr.bufs)

    def body(*refs):
        bs, rs = refs[:nb], refs[nb : 2 * nb]
        g = refs[2 * nb] if got is not None else None
        o = refs[-1]
        c = ring.here()[0]
        at, gat = 0, 0
        for b, rv, (r, cs) in zip(bs, rs, gr.sizes):
            h = r // 2
            for j in range(cs):
                col = slice(j * width, (j + 1) * width)
                if half:
                    v = b[m * r : m * r + h, col].astype(F32) + rv[0:h, col].astype(F32)
                    o[at : at + h, :] = v.astype(BF)
                    at += h
                else:
                    base = h + (n - k - m - 1) * r
                    v = b[k * r : (k + 1) * r, col].astype(F32) + rv[base : base + r, col].astype(F32)
                    if g.shape[0] == total:
                        o[at : at + r, :] = (v + g[at : at + r, :].astype(F32)).astype(BF)
                    else:
                        top = jnp.where(c == 0, 1.0, 0.0)
                        gv = g[gat : gat + h, :].astype(F32)
                        o[at : at + h, :] = (v[:h] + gv * top).astype(BF)
                        o[at + h : at + r, :] = (v[h:] + gv * (1.0 - top)).astype(BF)
                        gat += h
                    at += r

    return body, [out((total, width), BF)], args


def owner_sum(ring, gr, got):
    nb = len(gr.bufs)

    def body(*refs):
        bs, g, keep, send = refs[:nb], refs[nb], refs[nb + 1], refs[nb + 2]
        c = ring.here()[0]
        at, to = 0, 0
        for b, (r, cs) in zip(bs, gr.sizes):
            h = r // 2
            for j in range(cs):
                v = b[0:r, j * gr.width : (j + 1) * gr.width].astype(F32) + g[at : at + r, :].astype(F32)
                v = v.astype(BF)
                keep[to : to + h, :] = jnp.where(c == 0, v[:h], v[h:])
                send[to : to + h, :] = jnp.where(c == 0, v[h:], v[:h])
                at += r
                to += h

    o = out((gr.rows // 2, gr.width), BF)
    return body, [o, o], [*gr.bufs, got]


def add_kernel(a_ref, b_ref, o_ref):
    o_ref[...] = (a_ref[...].astype(F32) + b_ref[...].astype(F32)).astype(o_ref.dtype)


def add2(a, b):
    return add_kernel, [out(a.shape, a.dtype)], [a, b]


def reduce_group(ring, gr):
    got = None
    for k in range(ring.half, 0, -1):
        (part,) = yield reduce_step(ring, gr, k, got)
        got = ring.along(part)
    keep, send = yield owner_sum(ring, gr, got)
    (u,) = yield add2(keep, ring.core(send))
    bit = 2
    while bit < ring.reps:
        (u,) = yield add2(u, ring.send(u, lambda r, f, bit=bit: (r ^ bit, f)))
        bit *= 2
    return u, ring.core(u)


class Rounds:
    def __init__(self, line):
        self.line = line
        self.long = False
        self.live = {}
        self.jobs = {}
        self.done = {}

    def _advance(self, name, results):
        try:
            self.jobs[name] = next(self.live[name]) if results is None else self.live[name].send(results)
        except StopIteration as stop:
            self.done[name] = stop.value
            del self.live[name]
            self.jobs.pop(name, None)

    def add(self, name, chain):
        self.live[name] = chain
        self._advance(name, None)

    def turn(self, *names):
        names = [k for k in names or self.jobs if k in self.jobs]
        if not names:
            return
        jobs = [self.jobs[k] for k in names]
        args = [a for _, _, given in jobs for a in given]
        outs = [o for _, made, _ in jobs for o in made]

        def body(*refs):
            i, j = 0, len(args)
            for run, made, given in jobs:
                run(*refs[i : i + len(given)], *refs[j : j + len(made)])
                i, j = i + len(given), j + len(made)

        got = list(self.line.call(body, outs, args, long=self.long, name="sums"))
        for name, (_, made, _) in zip(names, jobs):
            self._advance(name, got[: len(made)])
            got = got[len(made) :]


def join_halves(c, parts, sizes, width, place):
    a_ref, b_ref = parts
    to = 0
    for i, (r, cs) in enumerate(sizes):
        h = r // 2
        for j in range(cs):
            a = a_ref[to : to + h, :].astype(F32)
            b = b_ref[to : to + h, :].astype(F32)
            place(i, slice(0, h), j, jnp.where(c == 0, a, b))
            place(i, slice(h, r), j, jnp.where(c == 0, b, a))
            to += h


def last_sum(job):
    return (yield job)


def finish(ring, gr, parts):
    def body(a_ref, b_ref, *outs):
        def place(i, rows, j, v):
            outs[i][rows, j * gr.width : (j + 1) * gr.width] = v

        join_halves(ring.here()[0], (a_ref, b_ref), gr.sizes, gr.width, place)

    return body, [out((r, cs * gr.width), F32) for r, cs in gr.sizes], list(parts)


def finish_joint(ring, gr_a, gr_b, parts_a, parts_b, sizes):
    (r, cs), (_, ocs), width = *gr_a.sizes, gr_a.width

    def body(a1, a2, b1, b2, o, o2, small, *outs):
        for k, pair in enumerate(((a1, a2), (b1, b2))):
            def place(i, rows, j, v, k=k):
                if i == 0:
                    at = (2 * j + k) * width
                    o[rows, at : at + width] = v
                elif k == 0:
                    o2[rows, j * width : (j + 1) * width] = v
                else:
                    small[rows, :] = v

            join_halves(ring.here()[0], pair, (gr_a, gr_b)[k].sizes, width, place)
        row = {}
        for size, got in zip(sizes, outs):
            k = row.setdefault(size, 0)
            row[size] += 1
            at = 0 if size == min(sizes) else SMALL_COL
            got[...] = small[k : k + 1, at : at + size]

    outs = [out((r, 2 * cs * width), F32), out((r, ocs * width), F32), out((SMALL_SHARD, width), F32)] + [out((1, k), F32) for k in sizes]
    return body, outs, [*parts_a, *parts_b]


def step_fn(mesh):
    ring = Ring(mesh)
    n, m = ring.n, ring.half

    def on_device(
        layer_input, item_ids, norm_gain, norm_bias, joint_weight, joint_bias, out_weight, out_bias,
        second_gain, second_bias, up_weight, up_bias, down_weight, down_bias, output_grad,
    ):
        rows, width = layer_input.shape
        ff = up_weight.shape[1]
        hw = width // 2
        rps = width // n
        t = (rps // 4) // 16 * 16
        a, b = rps + t, 2 * rps - 2 * t
        dma = pltpu.SemaphoreType.DMA
        shapes = [out((a + b, width), BF), out((a, width), BF)]
        line = Line()
        first1, opp1 = line.call(
            functools.partial(split_kernel, ring, t), shapes, [joint_weight, out_weight],
            far=(0, 1), scratch=[dma((6,))], name="split",
        )
        ids = [item_ids[:, None], item_ids[None, :]]
        first2, opp2 = line.call(
            functools.partial(split_ff_kernel, ring, t), shapes, [up_weight, down_weight], deps=ids,
            far=(0, 1), scratch=[dma((5,))], name="split_ff",
        )
        vectors = (norm_gain, norm_bias, joint_bias, out_bias, second_gain, second_bias, up_bias, down_bias)
        shared = {}

        def small_parts():
            (small,) = line.call(
                functools.partial(small_kernel, ring), [out((SMALL_ROWS, width), F32)], vectors, name="small",
            )
            mark = yield
            bit = 1
            while bit < n:
                other = ring.send(small, lambda r, f, bit=bit: (r, f ^ bit))
                yield (small if bit > 1 else None)
                mark = yield
                (small,) = kernel_call(add_f32_kernel, [out(small.shape, F32)], [small, other], deps=[mark], name="small_sum")
                bit *= 2
            shared["small"] = small
            (shared["first"],) = kernel_call(
                ln_kernel, [out((rows, width), BF)], [layer_input, small], deps=[mark], name="first_norm",
            )
            mark = yield shared["first"]
            while True:
                yield

        extras = small_parts()
        next(extras)
        g1, g2 = gather(ring, [first1, first2], a, extras)
        small, first = shared["small"], shared["first"]

        args = [first, small, *flat(first1, opp1, g1)]
        halves = [out((rows, 3 * hw), BF)] * 2
        proj_a, proj_b, wa, wb, wo = line.call(
            functools.partial(qkv_kernel, ring, a, t),
            halves + [out((width, 3 * hw), BF)] * 2 + [out((width, width), BF)],
            args, scratch=[VM((b, width), BF)], name="projection",
        )
        g2["ring"][-1], wo = there_first(g2["ring"][-1], wo)
        g2["pring"].append(ring.core(g2["ring"][-1]))
        (attended,) = line.call(attend_kernel, [out((rows, width), BF)], [proj_a, proj_b, *ids], name="attend")
        middle, second = line.call(
            out_kernel, [out((rows, width), F32), out((rows, width), BF)],
            [attended, wo, layer_input, small], name="out_projection",
        )
        args = [second, small, *flat(first2, opp2, g2)]
        active, slope, wu, wd = line.call(
            functools.partial(up_kernel, ring, a, t),
            [out((rows, ff), BF), out((rows, ff), BF), out((width, ff), BF), out((ff, width), BF)],
            args, scratch=[VM((b, width), BF)], name="up_projection",
        )

        def weight_grad(l, r, tl=512, tn=512, name=None):
            kl, kr = l.shape[1], r.shape[1]
            kept = m * (kl // n) + kl // n // 2
            buf, sent, sums = line.call(
                functools.partial(weight_grad_kernel, ring, tn, tl),
                [out((kl, kr), BF), out((kl - kept, kr), BF), out((8, kr), F32)], [l, r], name=name,
            )
            return buf, ring.core(sent), sums

        rounds = Rounds(line)

        def begin(name, bufs, recvs, w):
            gr = Grads(n, bufs, recvs, w)
            rounds.add(name, reduce_group(ring, gr))
            return gr

        down_buf, down_recv, s_down = weight_grad(active, output_grad, name="down_grad")
        (dhidden,) = line.call(
            dact_kernel, [out((rows, ff), BF)], [output_grad, wd, slope], name="hidden_grad",
        )
        gr_down = begin("down", [down_buf], [down_recv], width)
        rounds.turn("down")
        up_buf, up_recv, s_up = weight_grad(second, dhidden, name="up_grad")
        rounds.turn("down")
        (dsecond,) = line.call(dsecond_kernel, [out((rows, width), F32)], [dhidden, wu], name="dsecond")
        gr_up = begin("up", [up_buf], [up_recv], width)
        rounds.turn("up")
        dmid, dbranch, datt, sg2, sb2 = line.call(
            second_norm_back_kernel,
            [out((rows, width), F32), out((rows, width), BF), out((rows, width), BF), out((8, width), F32), out((8, width), F32)],
            [dsecond, wo, middle, output_grad, small], name="second_norm_grad",
        )
        rounds.turn("down")
        out_buf, out_recv, s_out = weight_grad(attended, dbranch, name="out_grad")
        rounds.turn("up")

        def attend_back(part, proj):
            return line.call(
                functools.partial(attend_back_kernel, part), [out((rows, 3 * hw), BF)], [proj, datt, *ids],
                scratch=[VM((rows, hw), F32), VM((rows, hw), F32)], name="attend_grad",
            )[0]

        da = attend_back(0, proj_a)
        rounds.turn("down")
        ja_buf, ja_recv, s_ja = weight_grad(first, da, name="joint_grad")
        rounds.turn("up")
        db = attend_back(1, proj_b)
        gr_ja = begin("ja", [ja_buf, out_buf], [ja_recv, out_recv], hw)
        rounds.turn("ja", "down")
        jb_buf, jb_recv, s_jb = weight_grad(first, db, name="joint_grad")
        rounds.turn("up")
        (dfirst,) = line.call(dfirst_kernel, [out((rows, width), F32)], [da, db, wa, wb], name="dfirst")
        rounds.turn("ja")
        input_grad, sg1, sb1 = line.call(
            first_norm_back_kernel, [out((rows, width), BF), out((8, width), F32), out((8, width), F32)],
            [dfirst, layer_input, dmid, small], straight=(0,),
            scratch=[VM((rows, width), BF), dma((rows // 256,))], name="first_norm_grad",
        )
        small_sizes = [v.shape[0] for v in vectors]
        small_kept = m * SMALL_SHARD + SMALL_SHARD // 2
        small_buf, small_sent = line.call(
            functools.partial(small_grads_kernel, ring, small_sizes),
            [out((n * SMALL_SHARD, hw), BF), out((n * SMALL_SHARD - small_kept, hw), BF)],
            [sg1, sb1, s_ja, s_jb, s_out, sg2, sb2, s_up, s_down], long=False, name="small_grads",
        )
        gr_jb = begin("jb", [jb_buf, small_buf], [jb_recv, ring.core(small_sent)], hw)
        rounds.turn("jb", "down")
        rounds.long = True
        rounds.turn("ja", "up")
        done, ready = rounds.done, set()
        pairs = ("jb", "up", "got up"), ("ja", "down", "got down")
        k = 0
        while rounds.jobs:
            if k == m + 1:
                rounds.long = False
                layer_output, _ = line.call(
                    down_kernel, [out((rows, width), BF), out((8, 128), F32)], [active, wd, middle, small],
                    straight=(0,), scratch=[VM((rows, width), BF), dma((width // 256,))], name="down_projection",
                )
            rounds.turn(*(pairs[k % 2] if k < m else ()))
            k += 1
            for name, gr in (("down", gr_down), ("up", gr_up)):
                if name in done and name not in ready:
                    ready.add(name)
                    rounds.add("got " + name, last_sum(finish(ring, gr, done[name])))
            if "ja" in done and "jb" in done and "joint" not in ready:
                ready.add("joint")
                rounds.add("got joint", last_sum(finish_joint(ring, gr_ja, gr_jb, done["ja"], done["jb"], small_sizes)))
        (g_down,), (g_up,), (g_joint, g_out, _, *v) = (done["got " + k] for k in ("down", "up", "joint"))
        v = [k.reshape(-1) for k in v]
        return (
            layer_output, input_grad, v[0], v[1], g_joint, v[2], g_out, v[3], v[4], v[5], g_up, v[6], g_down, v[7],
        )

    return on_device


def solution(mesh):
    row, vecs, mat = P(("rep", "fsdp"), None), P("fsdp"), P("fsdp", None)
    placed = (
        row, P(("rep", "fsdp")), vecs, vecs, mat, vecs, mat, vecs, vecs, vecs, mat, vecs, mat, vecs, row,
    )
    return jax.shard_map(
        step_fn(mesh),
        mesh=mesh,
        in_specs=placed,
        out_specs=(row, row, vecs, vecs, mat, vecs, mat, vecs, vecs, vecs, mat, vecs, mat, vecs),
        check_vma=False,
    )
```
